32 devices in a mesh: dp: 16 (over z, y, x), tensor: 2 (over core).
Axes of the slice: x: 2, y: 2, z: 4, core: 2. Of those that a mesh axis runs over, the one named last changes fastest.
Arguments:
- inputs: bfloat16 [17664, 1024], P(('dp', 'tensor')), may hold values from -6 to 6
- cotangent: bfloat16 [17664, 1024], P(('dp', 'tensor')), may hold values from -6 to 6
- slot_live: int32 [16], P('dp'), may hold values from 0 to 1, as said below
- token_type: int32 [17664], P(('dp', 'tensor')), may hold values from 0 to 3, as said below
- attn_norm_gain: bfloat16 [1024], P('dp'), may hold values from 0.25 to 1.75
- attn_norm_bias: bfloat16 [1024], P('dp'), may hold values from -4 to 4
- qkv_weight: bfloat16 [3, 1024, 1024], P(None, 'dp', 'tensor'), may hold values from -0.1875 to 0.1875
- proj_weight: bfloat16 [1024, 1024], P('tensor', 'dp'), may hold values from -1 to 1
- proj_bias: bfloat16 [1024], P('dp'), may hold values from -4 to 4
- mlp_norm_gain: bfloat16 [1024], P('dp'), may hold values from 0.25 to 1.75
- mlp_norm_bias: bfloat16 [1024], P('dp'), may hold values from -4 to 4
- fc1_weight: bfloat16 [1024, 4096], P('dp', 'tensor'), may hold values from -0.1875 to 0.1875
- fc1_bias: bfloat16 [4096], P(('tensor', 'dp')), may hold values from -6 to 6
- fc2_weight: bfloat16 [4096, 1024], P('tensor', 'dp'), may hold values from -0.09375 to 0.09375
- fc2_bias: bfloat16 [1024], P('dp'), may hold values from -4 to 4
Outputs:
- outputs: bfloat16 [17664, 1024], P(('dp', 'tensor'))
- grad_inputs: bfloat16 [17664, 1024], P(('dp', 'tensor'))
- grad_attn_norm_gain: float32 [1024], P('dp')
- grad_attn_norm_bias: float32 [1024], P('dp')
- grad_qkv_weight: float32 [3, 1024, 1024], P(None, 'dp', 'tensor')
- grad_proj_weight: float32 [1024, 1024], P('tensor', 'dp')
- grad_proj_bias: float32 [1024], P('dp')
- grad_mlp_norm_gain: float32 [1024], P('dp')
- grad_mlp_norm_bias: float32 [1024], P('dp')
- grad_fc1_weight: float32 [1024, 4096], P('dp', 'tensor')
- grad_fc1_bias: float32 [4096], P(('tensor', 'dp'))
- grad_fc2_weight: float32 [4096, 1024], P('tensor', 'dp')
- grad_fc2_bias: float32 [1024], P('dp')
The draws below stay inside these ranges and needn't reach their ends.
Inputs may be any that keep to these rules, and one draw needn't show every extreme that they name: `slot_live`: the ones of each data group's 1 entries come first; some data group holds 1 sequence. `token_type`: in each sequence position 0 is 0; positions 1 to 77 are 1 up to a caption length of at least one and 3 after it; later positions are 2, except the last two, which are 3.
All inputs are finite; a program needn't handle non-finite values.
Results may differ from the reference program's by a relative error of at most 0.02.
Values may be sent and summed in bfloat16 or wider, within the bound.
No kernel may reach another device: no remote copies, remote signals or barrier semaphores. Data moves between devices by JAX's collectives and lax.ppermute only.
A program may use at most 256 MiB of HBM per device.

```python
import jax
import jax.numpy as jnp
from jax import lax

D = 1024
HEADS = 16
HEAD_DIM = 64
FF = 4096
SEQ_LEN = 1104
TEXT = 77
SLOTS = 1
SEQS = 16
ROWS = 17664


def draw_slot_live(key, part):
    group_count = SEQS // SLOTS
    group_load = jax.random.randint(jax.random.fold_in(key, 11), (group_count,), 0, SLOTS + 1)
    full_group = jax.random.randint(jax.random.fold_in(key, 12), (), 0, group_count)
    group_load = jnp.where(jnp.arange(group_count) == full_group, SLOTS, group_load)
    slot_place = jnp.arange(SEQS) % SLOTS
    slot_owner = jnp.arange(SEQS) // SLOTS
    return (slot_place < group_load[slot_owner]).astype(jnp.int32)


def draw_token_type(key, part):
    caption = jax.random.randint(jax.random.fold_in(key, 21), (SEQS, 1), 1, TEXT + 1)
    position = jnp.arange(SEQ_LEN)[None, :]
    token_kind = jnp.where(position <= caption, 1, 3)
    token_kind = jnp.where(position > TEXT, 2, token_kind)
    token_kind = jnp.where(position >= SEQ_LEN - 2, 3, token_kind)
    token_kind = jnp.where(position == 0, 0, token_kind)
    return token_kind.reshape(SEQS * SEQ_LEN).astype(jnp.int32)


def steps_of(rng, shape, pieces, low, largest):
    def one(dim, parts):
        draws = jax.random.uniform(jax.random.fold_in(jax.random.fold_in(rng, 6), dim), (parts,), jnp.float32, low / len(pieces), largest / len(pieces))
        return jnp.repeat(jnp.exp(draws), shape[dim] // parts).reshape((-1,) + (1,) * (len(shape) - dim - 1))

    gain = one(*pieces[0])
    for cut in pieces[1:]:
        gain = gain * one(*cut)
    return gain


def noise(key, shape, spread, limit, cuts=(), kind=jnp.bfloat16):
    values = spread * jax.random.normal(key, shape, jnp.float32)
    if cuts:
        values = values * steps_of(key, shape, cuts, -0.22, 0.18)
    return jnp.clip(values, -limit, limit).astype(kind)


def setup_inputs(seed: int = 0) -> dict:
    key_list = jax.random.split(jax.random.key(seed), 16)
    return {
        "inputs": noise(key_list[0], (ROWS, D), 1.0, 6.0, ((0, 32),)),
        "cotangent": noise(key_list[1], (ROWS, D), 1.0, 6.0, ((0, 32),)),
        "slot_live": draw_slot_live(jax.random.fold_in(key_list[15], 71), 0),
        "token_type": draw_token_type(jax.random.fold_in(key_list[15], 71), 0),
        "attn_norm_gain": jnp.clip(1.0 + 0.15 * jax.random.normal(key_list[4], (D,), jnp.float32), 0.25, 1.75).astype(jnp.bfloat16),
        "attn_norm_bias": noise(key_list[5], (D,), 0.3, 4.0, ((0, 16),)),
        "qkv_weight": noise(key_list[6], (3, D, D), D ** -0.5, 0.1875, ((1, 16), (2, 2))),
        "proj_weight": noise(key_list[7], (D, D), (max(D * 32 // SEQ_LEN, 1)) ** -0.5, 1.0, ((0, 2), (1, 16))),
        "proj_bias": noise(key_list[8], (D,), 0.3, 4.0, ((0, 16),)),
        "mlp_norm_gain": jnp.clip(1.0 + 0.15 * jax.random.normal(key_list[9], (D,), jnp.float32), 0.25, 1.75).astype(jnp.bfloat16),
        "mlp_norm_bias": noise(key_list[10], (D,), 0.3, 4.0, ((0, 16),)),
        "fc1_weight": noise(key_list[11], (D, FF), D ** -0.5, 0.1875, ((0, 16), (1, 2))),
        "fc1_bias": noise(key_list[12], (FF,), 0.5, 6.0, ((0, 32),)),
        "fc2_weight": noise(key_list[13], (FF, D), FF ** -0.5, 0.09375, ((0, 2), (1, 16))),
        "fc2_bias": noise(key_list[14], (D,), 0.3, 4.0, ((0, 16),)),
    }


@jax.custom_vjp
def low(v):
    return lax.optimization_barrier(v.astype(jnp.bfloat16)).astype(jnp.float32)

@jax.custom_vjp
def low_back(v):
    return v

def low_keep(v):
    return (low(v), None)

def low_pass(kept, grad):
    return (grad,)

def back_keep(v):
    return (v, None)

def back_low(kept, grad):
    return (low(grad),)
low.defvjp(low_keep, low_pass)
low_back.defvjp(back_keep, back_low)

def layer_norm(values, norm_gain, norm_shift):
    row_mean = lax.optimization_barrier(jnp.mean(values, axis=-1, keepdims=True))
    centered = values - row_mean
    variance = lax.optimization_barrier(jnp.mean(centered * centered, axis=-1, keepdims=True))
    return centered * lax.rsqrt(variance + 1e-05) * norm_gain + norm_shift

def attend(packed, key_valid):
    highest = lax.Precision.HIGHEST
    query = packed[0].reshape(SEQ_LEN, HEADS, HEAD_DIM)
    keys = packed[1].reshape(SEQ_LEN, HEADS, HEAD_DIM)
    values = packed[2].reshape(SEQ_LEN, HEADS, HEAD_DIM)
    scores = jnp.einsum('qhd,khd->hqk', query, keys, precision=highest) * HEAD_DIM ** (-0.5)
    scores = low_back(scores)
    scores = jnp.where(key_valid[None, None, :] > 0, scores, -1e+30)
    attn_prob = low(jax.nn.softmax(scores, axis=-1))
    mixed = jnp.einsum('hqk,khd->qhd', attn_prob, values, precision=highest)
    return mixed.reshape(SEQ_LEN, D)

def forward(params, rows_in, live_rows, key_valid):
    attn_norm_gain, attn_norm_bias, qkv_weight, proj_weight, proj_bias, mlp_norm_gain, mlp_norm_bias, fc1_weight, fc1_bias, fc2_weight, fc2_bias = params
    highest = lax.Precision.HIGHEST
    normed_one = low(layer_norm(rows_in, attn_norm_gain, attn_norm_bias))
    packed = low(low_back(jnp.einsum('nd,jdc->jnc', normed_one, qkv_weight, precision=highest)))
    packed = packed.reshape(3, SEQS, SEQ_LEN, D).transpose(1, 0, 2, 3)
    valid_seq = key_valid.reshape(SEQS, SEQ_LEN)
    mixed = lax.map(jax.checkpoint(lambda slot_item: attend(slot_item[0], slot_item[1])), (packed, valid_seq))
    mixed = low(low_back(mixed.reshape(ROWS, D)))
    branch = low_back(jnp.dot(mixed, proj_weight, precision=highest) + proj_bias)
    middle = rows_in + live_rows[:, None] * branch
    normed_two = low(layer_norm(middle, mlp_norm_gain, mlp_norm_bias))
    hidden_pre = low_back(jnp.dot(normed_two, fc1_weight, precision=highest) + fc1_bias)
    hidden_act = low(jax.nn.gelu(hidden_pre, approximate=False))
    mlp_branch = low_back(jnp.dot(hidden_act, fc2_weight, precision=highest) + fc2_bias)
    return middle + live_rows[:, None] * mlp_branch

def reference(inputs, cotangent, slot_live, token_type, attn_norm_gain, attn_norm_bias, qkv_weight, proj_weight, proj_bias, mlp_norm_gain, mlp_norm_bias, fc1_weight, fc1_bias, fc2_weight, fc2_bias):
    live_rows = jnp.repeat(slot_live.astype(jnp.float32), SEQ_LEN)
    key_valid = (token_type != 3).astype(jnp.float32)
    params = tuple((weight_arg.astype(jnp.float32) for weight_arg in (attn_norm_gain, attn_norm_bias, qkv_weight, proj_weight, proj_bias, mlp_norm_gain, mlp_norm_bias, fc1_weight, fc1_bias, fc2_weight, fc2_bias)))
    outputs, pull_back = jax.vjp(lambda weights, rows_in: forward(weights, rows_in, live_rows, key_valid), params, inputs.astype(jnp.float32))
    grads, grad_rows = pull_back(cotangent.astype(jnp.float32))
    return (outputs.astype(jnp.bfloat16), grad_rows.astype(jnp.bfloat16), grads[0], grads[1], grads[2], grads[3], grads[4], grads[5], grads[6], grads[7], grads[8], grads[9], grads[10])
```

```python
import jax
import jax.numpy as jnp
from jax import lax
from jax.sharding import PartitionSpec as P

HEAD_DIM = 64
SEQ_LEN = 1104
F32 = jnp.float32
BF16 = jnp.bfloat16


def dp_factors(size):
    if size % 8 == 0:
        return (4, 2, size // 8)
    return (1, 1, size)


class DpGrid:
    def __init__(self, size):
        self.size = size
        self.factors = dp_factors(size)

    def coords(self, index):
        _, second, third = self.factors
        return (index // (second * third), (index // third) % second, index % third)

    def index(self, coords):
        _, second, third = self.factors
        return (coords[0] * second + coords[1]) * third + coords[2]

    def ahead(self, index, axis, step):
        coords = list(self.coords(index))
        coords[axis] = (coords[axis] + step) % self.factors[axis]
        return self.index(coords)

    def fetch(self, value, axis, step):
        pairs = [(self.ahead(i, axis, step), i) for i in range(self.size)]
        return lax.ppermute(value, "dp", pairs)

    def push(self, value, axis, step):
        pairs = [(i, self.ahead(i, axis, step)) for i in range(self.size)]
        return lax.ppermute(value, "dp", pairs)

    def gather(self, value, order):
        done = []
        for axis in order:
            pieces = [value] + [
                self.fetch(value, axis, step) for step in range(1, self.factors[axis])
            ]
            place = sum(1 for other in done if other < axis)
            value = jnp.stack(pieces, axis=place)
            done.append(axis)
        return value

    def scatter(self, value, order):
        left = [0, 1, 2]
        for axis in order:
            place = left.index(axis)
            total = lax.index_in_dim(value, 0, place, keepdims=False).astype(F32)
            for step in range(1, self.factors[axis]):
                piece = lax.index_in_dim(value, step, place, keepdims=False)
                total = total + self.push(piece, axis, step).astype(F32)
            left.remove(axis)
            value = total.astype(BF16) if left else total
        return value

    def block_order(self):
        here = self.coords(lax.axis_index("dp"))
        rel = self.coords(jnp.arange(self.size, dtype=jnp.int32))
        return self.index([(h + r) % f for h, r, f in zip(here, rel, self.factors)])


class TensorPair:
    def __init__(self, size, slot_count, local_rows):
        self.size = size
        self.relative = size == 2 and slot_count == 1
        self.local_rows = local_rows

    def swap(self, value):
        return lax.ppermute(value, "tensor", [(0, 1), (1, 0)])

    def whole(self, value):
        if self.relative:
            return jnp.concatenate([value, self.swap(value)], axis=0)
        return lax.all_gather(value, "tensor", axis=0, tiled=True)

    def own(self, value):
        if self.relative:
            return value[: self.local_rows]
        start = lax.axis_index("tensor") * self.local_rows
        return lax.dynamic_slice_in_dim(value, start, self.local_rows, axis=0)

    def total(self, value):
        if self.relative:
            other = self.swap(value)
            other = jnp.concatenate([other[self.local_rows :], other[: self.local_rows]], axis=0)
            return value.astype(F32) + other.astype(F32)
        return lax.psum(value.astype(F32), "tensor")

    def own_total(self, value):
        if self.relative:
            kept = value[: self.local_rows].astype(F32)
            return kept + self.swap(value[self.local_rows :]).astype(F32)
        return lax.psum_scatter(value, "tensor", scatter_dimension=0, tiled=True).astype(F32)

    def small_total(self, value):
        if self.size == 2:
            return value + self.swap(value)
        return lax.psum(value, "tensor")


def normalize(values):
    row_mean = jnp.mean(values, axis=-1, keepdims=True)
    centered = values - row_mean
    variance = jnp.mean(centered * centered, axis=-1, keepdims=True)
    inverse = lax.rsqrt(variance + 1e-05)
    return centered * inverse, inverse


def norm_input_grad(grad, gain, normed, inverse):
    scaled = grad * gain
    first = jnp.mean(scaled, axis=-1, keepdims=True)
    second = jnp.mean(scaled * normed, axis=-1, keepdims=True)
    return inverse * (scaled - first - normed * second)


def masked_scores(query, keys, key_valid, score_scale):
    scores = jnp.einsum("qhd,khd->hqk", query, keys, preferred_element_type=F32) * score_scale
    return jnp.where(key_valid[None, None, :] > 0, scores, -1e30)


def attend_forward(query, keys, values, key_valid, score_scale):
    scores = masked_scores(query, keys, key_valid, score_scale)
    row_max = jnp.max(scores, axis=-1, keepdims=True)
    exp_scores = jnp.exp(scores - row_max)
    row_sum = jnp.sum(exp_scores, axis=-1, keepdims=True)
    attn_prob = (exp_scores / row_sum).astype(BF16)
    mixed = jnp.einsum("hqk,khd->qhd", attn_prob, values, preferred_element_type=F32)
    return (mixed.astype(BF16), row_max + jnp.log(row_sum))


def attend_backward(query, keys, values, key_valid, log_total, grad_mixed, score_scale):
    scores = masked_scores(query, keys, key_valid, score_scale)
    attn_prob = jnp.exp(scores - log_total)
    grad_prob = jnp.einsum("qhd,khd->hqk", grad_mixed, values, preferred_element_type=F32)
    row_dot = jnp.sum(attn_prob * grad_prob, axis=-1, keepdims=True)
    grad_scores = (attn_prob * (grad_prob - row_dot)).astype(BF16)
    grad_query = (
        jnp.einsum("hqk,khd->qhd", grad_scores, keys, preferred_element_type=F32) * score_scale
    )
    grad_keys = (
        jnp.einsum("hqk,qhd->khd", grad_scores, query, preferred_element_type=F32) * score_scale
    )
    grad_values = jnp.einsum(
        "hqk,qhd->khd", attn_prob.astype(BF16), grad_mixed, preferred_element_type=F32
    )
    return (grad_query.astype(BF16), grad_keys.astype(BF16), grad_values.astype(BF16))


def dot_nn(left, right):
    return lax.dot_general(left, right, (((1,), (0,)), ((), ())), preferred_element_type=F32)


def dot_tn(left, right):
    return lax.dot_general(left, right, (((0,), (0,)), ((), ())), preferred_element_type=F32)


def dot_nt(left, right):
    return lax.dot_general(left, right, (((1,), (1,)), ((), ())), preferred_element_type=F32)


def gelu_and_slope(values):
    cdf = 0.5 * (1.0 + lax.erf(values * (0.5**0.5)))
    density = jnp.exp(-0.5 * values * values) * 0.3989422804014327
    return values * cdf, cdf + values * density


def on_device(
    inputs,
    cotangent,
    slot_live,
    token_type,
    attn_norm_gain,
    attn_norm_bias,
    qkv_weight,
    proj_weight,
    proj_bias,
    mlp_norm_gain,
    mlp_norm_bias,
    fc1_weight,
    fc1_bias,
    fc2_weight,
    fc2_bias,
):
    dp_size = lax.axis_size("dp")
    tensor_size = lax.axis_size("tensor")
    local_rows, width = inputs.shape
    slot_count = slot_live.shape[0]
    whole_rows = local_rows * tensor_size
    block = fc1_weight.shape[0]
    width_here = qkv_weight.shape[2]
    heads_here = width_here // HEAD_DIM
    hidden_here = fc1_weight.shape[1]
    hidden_block = fc1_bias.shape[0]
    hidden_cut = hidden_here // 2
    score_scale = HEAD_DIM ** (-0.5)
    grid = DpGrid(dp_size)
    pair = TensorPair(tensor_size, slot_count, local_rows)
    first_order, second_order = (0, 2, 1), (0, 1, 2)

    smalls = jnp.stack(
        (attn_norm_gain, attn_norm_bias, proj_bias, mlp_norm_gain, mlp_norm_bias, fc2_bias)
    )
    bias_rows = -(-hidden_block // block)
    bias_pad = bias_rows * block - hidden_block
    bias_block = jnp.pad(fc1_bias, (0, bias_pad)).reshape(bias_rows, block)
    smalls = jnp.concatenate([smalls, bias_block], axis=0)
    smalls = grid.gather(smalls, second_order).reshape(dp_size, 6 + bias_rows, block)

    def rows_of(weight):
        return weight.reshape(width, weight.shape[-1])

    weight_q, weight_k, weight_v = qkv_weight[0], qkv_weight[1], qkv_weight[2]
    query_key = rows_of(grid.gather(jnp.concatenate([weight_q, weight_k], axis=1), first_order))
    value_proj = rows_of(
        grid.gather(jnp.concatenate([weight_v, proj_weight.T], axis=1), second_order)
    )
    fc2_t = fc2_weight.T
    fc1_parts, fc2_parts = [], []
    for start in (0, hidden_cut):
        cut = slice(start, start + hidden_cut)
        fc1_parts.append(rows_of(grid.gather(fc1_weight[:, cut], first_order)))
        fc2_parts.append(rows_of(grid.gather(fc2_t[:, cut], second_order)))

    order = grid.block_order()
    feature = jnp.repeat(order * block, block) + jnp.tile(
        jnp.arange(block, dtype=jnp.int32), dp_size
    )
    select = (jnp.arange(width, dtype=jnp.int32)[:, None] == feature[None, :]).astype(BF16)
    rows_in_b = pair.whole(dot_nn(inputs, select).astype(BF16))
    grad_out_b = pair.whole(dot_nn(cotangent, select).astype(BF16))
    rows_in = rows_in_b.astype(F32)
    valid_whole = pair.whole((token_type != 3).astype(F32))
    valid_seq = valid_whole.reshape(slot_count, SEQ_LEN)
    live_col = jnp.repeat(slot_live.astype(F32), SEQ_LEN)[:, None]

    vectors = smalls[:, :6].transpose(1, 0, 2).reshape(6, width).astype(F32)
    gain_one, shift_one, proj_shift, gain_two, shift_two, fc2_shift = (
        vectors[i : i + 1] for i in range(6)
    )
    place = (jnp.arange(dp_size, dtype=jnp.int32)[:, None] == order[None, :]).astype(BF16)
    fc1_shift = smalls[:, 6:].reshape(dp_size, bias_rows * block)[:, :hidden_block]
    fc1_shift = dot_nn(place, fc1_shift).reshape(1, hidden_here)

    hat_one, inverse_one = normalize(rows_in)
    norm_one = (hat_one * gain_one + shift_one).astype(BF16)
    packed_qk = dot_nn(norm_one, query_key).astype(BF16)
    packed_v = dot_nn(norm_one, value_proj[:, :width_here]).astype(BF16)
    proj_t = value_proj[:, width_here:]
    split = (slot_count, SEQ_LEN, heads_here, HEAD_DIM)
    query = packed_qk[:, :width_here].reshape(split)
    keys = packed_qk[:, width_here:].reshape(split)
    values = packed_v.reshape(split)

    forward = [
        attend_forward(query[s], keys[s], values[s], valid_seq[s], score_scale)
        for s in range(slot_count)
    ]
    mixed = jnp.concatenate([f[0] for f in forward], axis=0).reshape(whole_rows, width_here)

    attn_out = pair.total(dot_nt(mixed, proj_t).astype(BF16))
    middle = rows_in + live_col * (attn_out + proj_shift)
    hat_two, inverse_two = normalize(middle)
    norm_two = (hat_two * gain_two + shift_two).astype(BF16)
    grad_out = grad_out_b.astype(F32)
    grad_mlp = (live_col * grad_out).astype(BF16)

    mlp_out, grad_two = 0.0, 0.0
    out_fc1, out_fc2, fc1_bias_parts = [], [], []
    block_shape = grid.factors + (block,)
    for part in range(2):
        cut = slice(part * hidden_cut, (part + 1) * hidden_cut)
        hidden_pre = dot_nn(norm_two, fc1_parts[part]) + fc1_shift[:, cut]
        hidden_act, slope = gelu_and_slope(hidden_pre)
        hidden_act = hidden_act.astype(BF16)
        mlp_out = mlp_out + dot_nt(hidden_act, fc2_parts[part])
        grad_pre = (dot_nn(grad_mlp, fc2_parts[part]) * slope).astype(BF16)
        grad_fc2 = dot_tn(grad_mlp, hidden_act).astype(BF16).reshape(block_shape + (hidden_cut,))
        grad_fc1 = dot_tn(norm_two, grad_pre).astype(BF16).reshape(block_shape + (hidden_cut,))
        fc1_bias_parts.append(jnp.sum(grad_pre, axis=0, dtype=F32))
        grad_two = grad_two + dot_nt(grad_pre, fc1_parts[part])
        out_fc1.append(grid.scatter(grad_fc1, first_order[::-1]))
        out_fc2.append(grid.scatter(grad_fc2, second_order[::-1]))
    grad_fc1_bias = jnp.concatenate(fc1_bias_parts)

    result = pair.own(middle) + pair.own(live_col) * (
        pair.own_total(mlp_out.astype(BF16)) + fc2_shift
    )
    outputs = dot_nt(result.astype(BF16), select).astype(BF16)

    grad_two = pair.total(grad_two.astype(BF16))
    grad_gain_two = jnp.sum(grad_two * hat_two, axis=0)
    grad_shift_two = jnp.sum(grad_two, axis=0)
    grad_middle = grad_out + norm_input_grad(grad_two, gain_two, hat_two, inverse_two)
    grad_branch = (live_col * grad_middle).astype(BF16)
    grad_proj_bias = jnp.sum(grad_branch, axis=0, dtype=F32)
    grad_fc2_bias = jnp.sum(grad_mlp, axis=0, dtype=F32)
    grad_proj = dot_tn(grad_branch, mixed).astype(BF16)
    grad_mixed = dot_nn(grad_branch, proj_t).astype(BF16).reshape(split)
    backward = [
        attend_backward(
            query[s], keys[s], values[s], valid_seq[s], forward[s][1], grad_mixed[s], score_scale
        )
        for s in range(slot_count)
    ]
    grad_q, grad_k, grad_v = (
        jnp.concatenate([b[i] for b in backward], axis=0).reshape(whole_rows, width_here)
        for i in range(3)
    )
    grad_qk = jnp.concatenate([grad_q, grad_k], axis=1)
    grad_weight_qk = dot_tn(norm_one, grad_qk).astype(BF16)
    grad_weight_v = dot_tn(norm_one, grad_v).astype(BF16)
    out_qk = grid.scatter(
        grad_weight_qk.reshape(block_shape + (2 * width_here,)), first_order[::-1]
    )
    out_vp = grid.scatter(
        jnp.concatenate([grad_weight_v, grad_proj], axis=1).reshape(
            block_shape + (2 * width_here,)
        ),
        second_order[::-1],
    )
    grad_one = dot_nt(grad_qk, query_key) + dot_nt(grad_v, value_proj[:, :width_here])
    grad_one = pair.own_total(grad_one.astype(BF16))
    own_hat, own_inverse = pair.own(hat_one), pair.own(inverse_one)
    grad_gain_one = pair.small_total(jnp.sum(grad_one * own_hat, axis=0))
    grad_shift_one = pair.small_total(jnp.sum(grad_one, axis=0))
    grad_rows = pair.own(grad_middle) + norm_input_grad(grad_one, gain_one, own_hat, own_inverse)
    grad_inputs = dot_nt(grad_rows.astype(BF16), select).astype(BF16)

    vector_grads = jnp.stack(
        (
            grad_gain_one,
            grad_shift_one,
            grad_proj_bias,
            grad_gain_two,
            grad_shift_two,
            grad_fc2_bias,
        )
    ).astype(BF16)
    vector_grads = vector_grads.reshape(6, dp_size, block).transpose(1, 0, 2)
    bias_grads = dot_tn(place, grad_fc1_bias.astype(BF16).reshape(dp_size, hidden_block))
    bias_grads = jnp.pad(bias_grads.astype(BF16), ((0, 0), (0, bias_pad)))
    bias_grads = bias_grads.reshape(dp_size, bias_rows, block)
    small_grads = jnp.concatenate([vector_grads, bias_grads], axis=1)
    small_grads = grid.scatter(
        small_grads.reshape(grid.factors + (6 + bias_rows, block)), second_order[::-1]
    )
    out_qkv = jnp.stack([out_qk[:, :width_here], out_qk[:, width_here:], out_vp[:, :width_here]])
    return (
        outputs,
        grad_inputs,
        small_grads[0],
        small_grads[1],
        out_qkv,
        out_vp[:, width_here:].T,
        small_grads[2],
        small_grads[3],
        small_grads[4],
        jnp.concatenate(out_fc1, axis=1),
        small_grads[6:].reshape(-1)[:hidden_block],
        jnp.concatenate(out_fc2, axis=1).T,
        small_grads[5],
    )


def solution(mesh):
    in_specs = (
        P(("dp", "tensor"), None),
        P(("dp", "tensor"), None),
        P("dp"),
        P(("dp", "tensor")),
        P("dp"),
        P("dp"),
        P(None, "dp", "tensor"),
        P("tensor", "dp"),
        P("dp"),
        P("dp"),
        P("dp"),
        P("dp", "tensor"),
        P(("tensor", "dp")),
        P("tensor", "dp"),
        P("dp"),
    )
    out_specs = (
        P(("dp", "tensor"), None),
        P(("dp", "tensor"), None),
        P("dp"),
        P("dp"),
        P(None, "dp", "tensor"),
        P("tensor", "dp"),
        P("dp"),
        P("dp"),
        P("dp"),
        P("dp", "tensor"),
        P(("tensor", "dp")),
        P("tensor", "dp"),
        P("dp"),
    )
    return jax.shard_map(
        on_device, mesh=mesh, in_specs=in_specs, out_specs=out_specs, check_vma=False
    )
```

```python
import functools

import jax
import jax.numpy as jnp
import numpy as np
from jax import lax
from jax.experimental import pallas as pl
from jax.experimental.pallas import tpu as pltpu
from jax.sharding import PartitionSpec as P

HEAD_DIM = 64
SEQ_LEN = 1104
F32 = jnp.float32
BF16 = jnp.bfloat16
MIB = 2**20


def dp_factors(size):
    if size % 8 == 0:
        return (4, 2, size // 8)
    return (1, 1, size)


class DpGrid:
    def __init__(self, size, block):
        self.size = size
        self.block = block
        self.half = block // 2
        self.factors = dp_factors(size)
        self.routes = ((2, 1), (1, 2))

    def coords(self, index):
        _, second, third = self.factors
        return (index // (second * third), (index // third) % second, index % third)

    def index(self, coords):
        _, second, third = self.factors
        return (coords[0] * second + coords[1]) * third + coords[2]

    def ahead(self, index, axis, step):
        coords = list(self.coords(index))
        coords[axis] = (coords[axis] + step) % self.factors[axis]
        return self.index(coords)

    def fetch(self, value, axis, step):
        pairs = [(self.ahead(i, axis, step), i) for i in range(self.size)]
        return lax.ppermute(value, "dp", pairs)

    def push(self, value, axis, step):
        pairs = [(i, self.ahead(i, axis, step)) for i in range(self.size)]
        return lax.ppermute(value, "dp", pairs)

    def gather(self, shard):
        along = [shard] + [self.fetch(shard, 0, s) for s in range(1, self.factors[0])]
        pieces = []
        for part, (middle, last) in enumerate(self.routes):
            rows = slice(part * self.half, (part + 1) * self.half)
            value = jnp.concatenate([a[rows] for a in along], axis=0)
            steps = range(1, self.factors[middle])
            value = jnp.concatenate([value] + [self.fetch(value, middle, s) for s in steps], axis=0)
            pieces.append(value)
            pieces.extend(self.fetch(value, last, s) for s in range(1, self.factors[last]))
        return pieces

    def scatter(self, pieces):
        pieces = list(pieces)
        halves = []
        for middle, last in self.routes:
            mine, pieces = pieces[: self.factors[last]], pieces[self.factors[last] :]
            total = mine[0].astype(F32)
            for step in range(1, self.factors[last]):
                total = total + self.push(mine[step], last, step).astype(F32)
            value = total.astype(BF16)
            rows = self.factors[0] * self.half
            total = value[:rows].astype(F32)
            for step in range(1, self.factors[middle]):
                piece = value[step * rows : (step + 1) * rows]
                total = total + self.push(piece, middle, step).astype(F32)
            halves.append(total)

        def along(step):
            rows = slice(step * self.half, (step + 1) * self.half)
            return jnp.concatenate([h[rows] for h in halves], axis=0)

        total = along(0)
        for step in range(1, self.factors[0]):
            total = total + self.push(along(step).astype(BF16), 0, step).astype(F32)
        return total

    def piece_rows(self):
        full = self.size * self.half
        rows = []
        for _, last in self.routes:
            rows.extend([full // self.factors[last]] * self.factors[last])
        return rows

    def cut(self, value, axis=0):
        edges = np.cumsum(self.piece_rows())[:-1].tolist()
        return jnp.split(value, edges, axis=axis)

    def features(self):
        here = self.coords(lax.axis_index("dp"))
        indices = []
        for part, (middle, last) in enumerate(self.routes):
            shape = (self.factors[last], self.factors[middle], self.factors[0], self.half)
            steps = [None, None, None]
            steps[last], steps[middle], steps[0], sub = (
                jnp.asarray(g.reshape(-1), jnp.int32) for g in np.indices(shape)
            )
            coords = [(h + s) % f for h, s, f in zip(here, steps, self.factors)]
            indices.append(self.index(coords) * self.block + part * self.half + sub)
        return jnp.concatenate(indices)


class TensorPair:
    def __init__(self, size, slot_count, local_rows):
        self.size = size
        self.relative = size == 2 and slot_count == 1
        self.local_rows = local_rows

    def swap(self, value):
        return lax.ppermute(value, "tensor", [(0, 1), (1, 0)])

    def whole(self, value):
        if self.relative:
            return jnp.concatenate([value, self.swap(value)], axis=0)
        return lax.all_gather(value, "tensor", axis=0, tiled=True)

    def own(self, value):
        if self.relative:
            return value[: self.local_rows]
        start = lax.axis_index("tensor") * self.local_rows
        return lax.dynamic_slice_in_dim(value, start, self.local_rows, axis=0)

    def total(self, value):
        if self.relative:
            other = self.swap(value)
            other = jnp.concatenate([other[self.local_rows :], other[: self.local_rows]], axis=0)
            return value.astype(F32) + other.astype(F32)
        return lax.psum(value.astype(F32), "tensor")

    def own_total(self, value):
        if self.relative:
            kept = value[: self.local_rows].astype(F32)
            return kept + self.swap(value[self.local_rows :]).astype(F32)
        return lax.psum_scatter(value, "tensor", scatter_dimension=0, tiled=True).astype(F32)

    def small_total(self, value):
        if self.size == 2:
            return value + self.swap(value)
        return lax.psum(value, "tensor")


def normalize(values):
    row_mean = jnp.mean(values, axis=-1, keepdims=True)
    centered = values - row_mean
    variance = jnp.mean(centered * centered, axis=-1, keepdims=True)
    inverse = lax.rsqrt(variance + 1e-05)
    return centered * inverse, inverse


def norm_input_grad(grad, gain, normed, inverse):
    scaled = grad * gain
    first = jnp.mean(scaled, axis=-1, keepdims=True)
    second = jnp.mean(scaled * normed, axis=-1, keepdims=True)
    return inverse * (scaled - first - normed * second)


def dot_nn(left, right):
    return lax.dot_general(left, right, (((1,), (0,)), ((), ())), preferred_element_type=F32)


def dot_nt(left, right):
    return lax.dot_general(left, right, (((1,), (1,)), ((), ())), preferred_element_type=F32)


def dot_tn(left, right):
    return lax.dot_general(left, right, (((0,), (0,)), ((), ())), preferred_element_type=F32)


def gelu_and_slope(values):
    cdf = 0.5 + 0.5 * lax.erf(values * (0.5**0.5))
    density = jnp.exp(-0.5 * values * values) * 0.3989422804014327
    return values * cdf, cdf + values * density


def params(limit):
    return pltpu.CompilerParams(vmem_limit_bytes=limit * MIB)


def whole_spec(array):
    return pl.BlockSpec(array.shape, lambda *grid: (0,) * len(array.shape))


def stack_rows(refs):
    return jnp.concatenate([r[...] for r in refs], axis=0)


def head_lanes(seq, head):
    lane = lax.broadcasted_iota(jnp.int32, (seq, 2 * HEAD_DIM), 1)
    mine = (lane >= HEAD_DIM) if head else (lane < HEAD_DIM)
    return mine, lane == (0 if head else HEAD_DIM)


def head_operands(query_ref, key_ref, invalid, head):
    seq = query_ref.shape[0]
    mine, extra = head_lanes(seq, head)
    one, zero = jnp.asarray(1, BF16), jnp.asarray(0, BF16)
    scaled = query_ref[...] * jnp.asarray(HEAD_DIM**-0.5, BF16)
    query = jnp.where(mine, scaled, jnp.where(extra, one, zero))
    keys = jnp.where(mine, key_ref[...], jnp.where(extra, invalid, zero))
    return query, keys


def key_column(invalid_ref):
    seq = invalid_ref.shape[-1]
    return jnp.broadcast_to(invalid_ref[0], (2 * HEAD_DIM, seq)).T.astype(BF16)


def attend_kernel(query_ref, key_ref, value_ref, invalid_ref, mixed_ref, total_ref, turned_ref):
    seq = query_ref.shape[0]
    invalid = key_column(invalid_ref)
    values = value_ref[...].T
    for head in range(2):
        rows = slice(head * HEAD_DIM, (head + 1) * HEAD_DIM)
        query, keys = head_operands(query_ref, key_ref, invalid, head)
        with_ones = jnp.concatenate([values[rows], jnp.ones((16, seq), BF16)], axis=0)
        scores = dot_nt(keys, query)
        largest = jnp.max(scores, axis=0, keepdims=True)
        weights = jnp.exp(scores - largest)
        mixed = dot_nn(with_ones, weights.astype(BF16))
        weight_sum = mixed[HEAD_DIM : HEAD_DIM + 1]
        turned_ref[rows] = mixed[:HEAD_DIM] * (1.0 / weight_sum)
        total_ref[0, 0, head : head + 1] = largest + jnp.log(weight_sum)
    mixed_ref[...] = turned_ref[...].T.astype(BF16)


def attend_back_kernel(
    query_ref,
    key_ref,
    value_ref,
    invalid_ref,
    mixed_ref,
    total_ref,
    grad_ref,
    grad_query_ref,
    grad_key_ref,
    grad_value_ref,
    turned_ref,
    prob_ref,
    score_ref,
):
    seq = query_ref.shape[0]
    invalid = key_column(invalid_ref)
    keys_turned = key_ref[...].T
    product = mixed_ref[...].astype(F32).T * grad_ref[...].astype(F32).T
    for head in range(2):
        rows = slice(head * HEAD_DIM, (head + 1) * HEAD_DIM)
        mine, _ = head_lanes(seq, head)
        query, keys = head_operands(query_ref, key_ref, invalid, head)
        grad = jnp.where(mine, grad_ref[...], jnp.asarray(0, BF16))
        row_dot = jnp.sum(product[rows], axis=0, keepdims=True)
        for start in range(0, seq, 256):
            cut = slice(start, min(start + 256, seq))
            prob = jnp.exp(dot_nt(keys, query[cut]) - total_ref[0, 0, head : head + 1, cut])
            grad_prob = dot_nt(value_ref[...], grad[cut]) - row_dot[:, cut]
            grad_score = (prob * grad_prob).astype(BF16)
            prob_ref[:, cut] = prob.astype(BF16)
            score_ref[:, cut] = grad_score
            turned_ref[rows, cut] = dot_nn(keys_turned[rows], grad_score) * HEAD_DIM**-0.5
        grad_value = dot_nn(prob_ref[...], grad)
        grad_key = dot_nn(score_ref[...], jnp.where(mine, query, jnp.asarray(0, BF16)))
        if head == 0:
            first_value, first_key = grad_value, grad_key
    grad_value_ref[...] = (first_value + grad_value).astype(BF16)
    grad_key_ref[...] = (first_key + grad_key).astype(BF16)
    grad_query_ref[...] = turned_ref[...].T.astype(BF16)


def attend_specs(pairs):
    def columns(offset):
        return pl.BlockSpec((SEQ_LEN, 2 * HEAD_DIM), lambda s, p: (s, p + offset))

    invalid = pl.BlockSpec((1, 1, SEQ_LEN), lambda s, p: (s, 0, 0))
    total = pl.BlockSpec((1, 1, 2, SEQ_LEN), lambda s, p: (s, p, 0, 0))
    return columns, invalid, total


def attend(packed, invalid):
    slots, pairs = invalid.shape[0], packed.shape[1] // (6 * HEAD_DIM)
    columns, invalid_spec, total_spec = attend_specs(pairs)
    return pl.pallas_call(
        attend_kernel,
        grid=(slots, pairs),
        in_specs=[columns(0), columns(pairs), columns(2 * pairs), invalid_spec],
        out_specs=[columns(0), total_spec],
        out_shape=[
            jax.ShapeDtypeStruct((packed.shape[0], pairs * 2 * HEAD_DIM), BF16),
            jax.ShapeDtypeStruct((slots, pairs, 2, SEQ_LEN), F32),
        ],
        scratch_shapes=[pltpu.VMEM((2 * HEAD_DIM, SEQ_LEN), F32)],
        compiler_params=params(48),
        name="attend",
    )(packed, packed, packed, invalid)


def attend_back(packed, invalid, mixed, total, grad_mixed):
    slots, pairs = invalid.shape[0], packed.shape[1] // (6 * HEAD_DIM)
    columns, invalid_spec, total_spec = attend_specs(pairs)
    return pl.pallas_call(
        attend_back_kernel,
        grid=(slots, pairs),
        in_specs=[
            columns(0),
            columns(pairs),
            columns(2 * pairs),
            invalid_spec,
            columns(0),
            total_spec,
            columns(0),
        ],
        out_specs=[columns(0)] * 3,
        out_shape=[jax.ShapeDtypeStruct(mixed.shape, BF16)] * 3,
        scratch_shapes=[
            pltpu.VMEM((2 * HEAD_DIM, SEQ_LEN), F32),
            pltpu.VMEM((SEQ_LEN, SEQ_LEN), BF16),
            pltpu.VMEM((SEQ_LEN, SEQ_LEN), BF16),
        ],
        compiler_params=params(48),
        name="attend_back",
    )(packed, packed, packed, invalid, mixed, total, grad_mixed)


def times_pieces(rows, pieces, first, count, wide, fits):
    if not fits:
        weight = jnp.concatenate(pieces, axis=0)[:, first * wide : (first + count) * wide]
        return dot_nn(rows, weight).astype(BF16)

    def kernel(rows_ref, *refs):
        refs[-1][...] = dot_nn(rows_ref[...], stack_rows(refs[:-1])).astype(BF16)

    return pl.pallas_call(
        kernel,
        grid=(count,),
        in_specs=[whole_spec(rows)]
        + [pl.BlockSpec((p.shape[0], wide), lambda j: (0, first + j)) for p in pieces],
        out_specs=pl.BlockSpec((rows.shape[0], wide), lambda j: (0, j)),
        out_shape=jax.ShapeDtypeStruct((rows.shape[0], count * wide), BF16),
        compiler_params=params(40),
        name="times_pieces",
    )(rows, *pieces)


def times_pieces_turned(columns, pieces, first, wide, fits):
    count = len(columns)
    if not fits:
        weight = jnp.concatenate(pieces, axis=0)[:, first * wide : (first + count) * wide]
        return dot_nt(jnp.concatenate(columns, axis=1), weight).astype(BF16)
    rows = columns[0].shape[0]
    starts = np.cumsum([0] + [p.shape[0] for p in pieces]).tolist()

    def kernel(*refs):
        lefts, weights, out_ref = refs[:count], refs[count:-1], refs[-1]
        for i, start in enumerate(starts[:-1]):
            total = 0.0
            for k in range(count):
                total = total + dot_nt(lefts[k][...], weights[i * count + k][...])
            out_ref[:, start : starts[i + 1]] = total.astype(BF16)

    weight_specs, weights = [], []
    for piece in pieces:
        for k in range(count):
            weight_specs.append(
                pl.BlockSpec((piece.shape[0], wide), lambda i, k=k: (0, first + k))
            )
            weights.append(piece)
    return pl.pallas_call(
        kernel,
        grid=(1,),
        in_specs=[whole_spec(c) for c in columns] + weight_specs,
        out_specs=pl.BlockSpec((rows, starts[-1]), lambda i: (0, 0)),
        out_shape=jax.ShapeDtypeStruct((rows, starts[-1]), BF16),
        compiler_params=params(48),
        name="times_pieces_turned",
    )(*columns, *weights)


def weight_grads(lefts, rights, piece_rows, fits):
    starts = np.cumsum([0] + piece_rows).tolist()
    if not fits:
        full = [dot_tn(a, b).astype(BF16) for a, b in zip(lefts, rights)]
        full = jnp.concatenate(full, axis=1)
        return [full[s:e] for s, e in zip(starts, starts[1:])]
    count = len(rights)
    wide = rights[0].shape[1]
    names = []
    for left in lefts:
        if not any(left is other for other in names):
            names.append(left)
    which = [next(i for i, o in enumerate(names) if o is left) for left in lefts]

    def kernel(*refs):
        left_refs, right_refs = refs[: len(names)], refs[len(names) : len(names) + count]
        out_refs = refs[len(names) + count :]
        for i, (start, end) in enumerate(zip(starts, starts[1:])):
            turned = [r[:, start:end].T for r in left_refs]
            for k in range(count):
                grad = dot_nn(turned[which[k]], right_refs[k][...])
                out_refs[i][:, k * wide : (k + 1) * wide] = grad.astype(BF16)

    return pl.pallas_call(
        kernel,
        grid=(1,),
        in_specs=[whole_spec(a) for a in names + list(rights)],
        out_specs=[pl.BlockSpec((r, count * wide), lambda i: (0, 0)) for r in piece_rows],
        out_shape=[jax.ShapeDtypeStruct((r, count * wide), BF16) for r in piece_rows],
        compiler_params=params(56),
        name="weight_grads",
    )(*names, *rights)


def feed_kernel(count, tile, carried, *refs):
    normed_ref, grad_ref, shift_ref = refs[:3]
    weight_refs = refs[3 : 3 + count]
    refs = refs[3 + count :]
    before, refs = (refs[:2], refs[2:]) if carried else ((), refs)
    out_ref, grad_two_ref, shift_grad_ref = refs[:3]
    weight_grad_refs = refs[3 : 3 + count]
    normed_turned, grad_turned, out_sum, grad_sum = refs[3 + count :]
    step = pl.program_id(0)

    @pl.when(step == 0)
    def _():
        normed_turned[...] = normed_ref[...].T
        grad_turned[...] = grad_ref[...].T
        if carried:
            out_sum[...] = before[0][...].astype(F32)
            grad_sum[...] = before[1][...].astype(F32)
        else:
            out_sum[...] = jnp.zeros_like(out_sum)
            grad_sum[...] = jnp.zeros_like(grad_sum)

    first = jnp.concatenate([w[:, :tile] for w in weight_refs], axis=0)
    second = jnp.concatenate([w[:, tile:] for w in weight_refs], axis=0)
    hidden = dot_nn(normed_ref[...], first) + shift_ref[...]
    hidden_act, slope = gelu_and_slope(hidden)
    hidden_act = hidden_act.astype(BF16)
    grad_pre = (dot_nn(grad_ref[...], second) * slope).astype(BF16)
    out_sum[...] += dot_nt(hidden_act, second)
    grad_sum[...] += dot_nt(grad_pre, first)
    shift_grad_ref[...] = jnp.sum(grad_pre.astype(F32), axis=0, keepdims=True)
    start = 0
    for ref in weight_grad_refs:
        rows = slice(start, start + ref.shape[0])
        ref[:, :tile] = dot_nn(normed_turned[rows], grad_pre).astype(BF16)
        ref[:, tile:] = dot_nn(grad_turned[rows], hidden_act).astype(BF16)
        start += ref.shape[0]

    @pl.when(step == pl.num_programs(0) - 1)
    def _():
        out_ref[...] = out_sum[...].astype(BF16)
        grad_two_ref[...] = grad_sum[...].astype(BF16)


def feed_tile(normed, grad, shift, pieces, first, tile, before, fits):
    rows, width = normed.shape
    steps = shift.shape[1] // tile
    if not fits:
        weight = jnp.concatenate(pieces, axis=0)[:, first * 2 * tile :]
        weight = weight[:, : steps * 2 * tile].reshape(width, steps, 2, tile)
        first_w = weight[:, :, 0].reshape(width, steps * tile)
        second_w = weight[:, :, 1].reshape(width, steps * tile)
        hidden_act, slope = gelu_and_slope(dot_nn(normed, first_w) + shift)
        hidden_act = hidden_act.astype(BF16)
        grad_pre = (dot_nn(grad, second_w) * slope).astype(BF16)
        out, grad_two = dot_nt(hidden_act, second_w), dot_nt(grad_pre, first_w)
        if before:
            out, grad_two = out + before[0].astype(F32), grad_two + before[1].astype(F32)
        grads = jnp.stack(
            [
                dot_tn(normed, grad_pre).astype(BF16).reshape(width, steps, tile),
                dot_tn(grad, hidden_act).astype(BF16).reshape(width, steps, tile),
            ],
            axis=2,
        ).reshape(width, steps * 2 * tile)
        edges = np.cumsum([p.shape[0] for p in pieces])[:-1].tolist()
        shift_grad = jnp.sum(grad_pre, axis=0, dtype=F32, keepdims=True)
        return [out.astype(BF16), grad_two.astype(BF16), shift_grad] + jnp.split(grads, edges, 0)

    def once(array):
        return pl.BlockSpec(
            array.shape, lambda j: (0,) * len(array.shape), pipeline_mode=pl.Buffered(1)
        )

    before = tuple(before)
    return pl.pallas_call(
        functools.partial(feed_kernel, len(pieces), tile, bool(before)),
        grid=(steps,),
        in_specs=[once(normed), once(grad), pl.BlockSpec((1, tile), lambda j: (0, j))]
        + [pl.BlockSpec((p.shape[0], 2 * tile), lambda j: (0, first + j)) for p in pieces]
        + [once(b) for b in before],
        out_specs=[
            pl.BlockSpec((rows, width), lambda j: (0, 0)),
            pl.BlockSpec((rows, width), lambda j: (0, 0)),
            pl.BlockSpec((1, tile), lambda j: (0, j)),
        ]
        + [pl.BlockSpec((p.shape[0], 2 * tile), lambda j: (0, j)) for p in pieces],
        out_shape=[
            jax.ShapeDtypeStruct((rows, width), BF16),
            jax.ShapeDtypeStruct((rows, width), BF16),
            jax.ShapeDtypeStruct((1, steps * tile), F32),
        ]
        + [jax.ShapeDtypeStruct((p.shape[0], steps * 2 * tile), BF16) for p in pieces],
        scratch_shapes=[
            pltpu.VMEM((width, rows), BF16),
            pltpu.VMEM((width, rows), BF16),
            pltpu.VMEM((rows, width), F32),
            pltpu.VMEM((rows, width), F32),
        ],
        compiler_params=params(60),
        name="feed_forward",
    )(normed, grad, shift, *pieces, *before)


def on_device(
    inputs,
    cotangent,
    slot_live,
    token_type,
    attn_norm_gain,
    attn_norm_bias,
    qkv_weight,
    proj_weight,
    proj_bias,
    mlp_norm_gain,
    mlp_norm_bias,
    fc1_weight,
    fc1_bias,
    fc2_weight,
    fc2_bias,
):
    dp_size = lax.axis_size("dp")
    tensor_size = lax.axis_size("tensor")
    local_rows, width = inputs.shape
    slot_count = slot_live.shape[0]
    whole_rows = local_rows * tensor_size
    block = fc1_weight.shape[0]
    width_here = qkv_weight.shape[2]
    hidden_here = fc1_weight.shape[1]
    hidden_block = fc1_bias.shape[0]
    hidden_cut = hidden_here // 2
    tile = width_here // 2
    cut_tiles = hidden_cut // tile
    fits = whole_rows <= 2048
    grid = DpGrid(dp_size, block)
    pair = TensorPair(tensor_size, slot_count, local_rows)

    qkv_shard = jnp.concatenate([qkv_weight[0], qkv_weight[1], qkv_weight[2]], axis=1)
    qkv_pieces = grid.gather(qkv_shard)
    bias_columns = -(-hidden_block // block)
    bias_pad = bias_columns * block - hidden_block
    smalls = jnp.stack(
        (attn_norm_gain, attn_norm_bias, proj_bias, mlp_norm_gain, mlp_norm_bias, fc2_bias)
    )
    bias_block = jnp.pad(fc1_bias, (0, bias_pad)).reshape(bias_columns, block)
    smalls = jnp.concatenate([smalls, bias_block], axis=0).T
    smalls = jnp.concatenate(grid.gather(smalls), axis=0).T

    fc2_turned = fc2_weight.T

    def feed_shard(part):
        columns = []
        for j in range(part * cut_tiles, (part + 1) * cut_tiles):
            columns.append(fc1_weight[:, j * tile : (j + 1) * tile])
            columns.append(fc2_turned[:, j * tile : (j + 1) * tile])
        return columns

    first_pieces = grid.gather(jnp.concatenate([proj_weight.T] + feed_shard(0), axis=1))
    second_pieces = grid.gather(jnp.concatenate(feed_shard(1), axis=1))

    features = grid.features()
    select = (jnp.arange(width, dtype=jnp.int32)[:, None] == features[None, :]).astype(BF16)
    rows_in = pair.whole(dot_nn(inputs, select).astype(BF16)).astype(F32)
    grad_out = pair.whole(dot_nn(cotangent, select).astype(BF16)).astype(F32)
    valid_whole = pair.whole((token_type != 3).astype(F32))
    invalid = jnp.where(valid_whole > 0, 0.0, -1e30).reshape(slot_count, 1, SEQ_LEN)
    live_col = jnp.repeat(slot_live.astype(F32), SEQ_LEN)[:, None]

    gain_one, shift_one, proj_shift, gain_two, shift_two, fc2_shift = (
        smalls[i : i + 1].astype(F32) for i in range(6)
    )
    fc1_shift = dot_nt(smalls[6:], select).reshape(bias_columns, dp_size, block)
    fc1_shift = fc1_shift.transpose(1, 0, 2).reshape(dp_size, bias_columns * block)
    fc1_shift = fc1_shift[:, :hidden_block].reshape(1, hidden_here)

    hat_one, inverse_one = normalize(rows_in)
    norm_one = (hat_one * gain_one + shift_one).astype(BF16)
    packed = times_pieces(norm_one, qkv_pieces, 0, 3, width_here, fits)
    mixed, total = attend(packed, invalid)

    attn_out = pair.total(times_pieces_turned([mixed], first_pieces, 0, width_here, fits))
    middle = rows_in + live_col * (attn_out + proj_shift)
    hat_two, inverse_two = normalize(middle)
    norm_two = (hat_two * gain_two + shift_two).astype(BF16)
    grad_mlp = (live_col * grad_out).astype(BF16)

    shifts = fc1_shift[:, :hidden_cut], fc1_shift[:, hidden_cut:]
    feed_a = feed_tile(norm_two, grad_mlp, shifts[0], first_pieces, 1, tile, (), fits)
    feed_b = feed_tile(norm_two, grad_mlp, shifts[1], second_pieces, 0, tile, feed_a[:2], fits)
    mlp_out, grad_two = feed_b[:2]
    grad_fc1_bias = jnp.concatenate([feed_a[2], feed_b[2]], axis=1)
    out_feed = jnp.concatenate([grid.scatter(feed_a[3:]), grid.scatter(feed_b[3:])], axis=1)
    out_feed = out_feed.reshape(block, 2 * cut_tiles, 2, tile)
    out_fc1 = out_feed[:, :, 0].reshape(block, hidden_here)
    out_fc2 = out_feed[:, :, 1].reshape(block, hidden_here).T

    result = pair.own(middle) + pair.own(live_col) * (pair.own_total(mlp_out) + fc2_shift)
    outputs = dot_nt(result.astype(BF16), select).astype(BF16)

    grad_two = pair.total(grad_two)
    grad_gain_two = jnp.sum(grad_two * hat_two, axis=0)
    grad_shift_two = jnp.sum(grad_two, axis=0)
    grad_middle = grad_out + norm_input_grad(grad_two, gain_two, hat_two, inverse_two)
    grad_branch = (live_col * grad_middle).astype(BF16)
    grad_proj_bias = jnp.sum(grad_branch, axis=0, dtype=F32)
    grad_fc2_bias = jnp.sum(grad_mlp, axis=0, dtype=F32)
    grad_mixed = times_pieces(grad_branch, first_pieces, 0, 1, width_here, fits)
    grad_packed = attend_back(packed, invalid, mixed, total, grad_mixed)

    out_attn = grid.scatter(
        weight_grads(
            (norm_one, norm_one, norm_one, grad_branch),
            tuple(grad_packed) + (mixed,),
            grid.piece_rows(),
            fits,
        )
    )
    out_attn = out_attn.reshape(block, 4, width_here)
    grad_one = pair.own_total(
        times_pieces_turned(list(grad_packed), qkv_pieces, 0, width_here, fits)
    )
    own_hat, own_inverse = pair.own(hat_one), pair.own(inverse_one)
    grad_gain_one = pair.small_total(jnp.sum(grad_one * own_hat, axis=0))
    grad_shift_one = pair.small_total(jnp.sum(grad_one, axis=0))
    grad_rows = pair.own(grad_middle) + norm_input_grad(grad_one, gain_one, own_hat, own_inverse)
    grad_inputs = dot_nt(grad_rows.astype(BF16), select).astype(BF16)

    vector_grads = jnp.stack(
        (
            grad_gain_one,
            grad_shift_one,
            grad_proj_bias,
            grad_gain_two,
            grad_shift_two,
            grad_fc2_bias,
        )
    ).astype(BF16)
    bias_grads = grad_fc1_bias.astype(BF16).reshape(dp_size, hidden_block)
    bias_grads = jnp.pad(bias_grads, ((0, 0), (0, bias_pad))).reshape(dp_size, bias_columns, block)
    bias_grads = dot_nn(bias_grads.transpose(1, 0, 2).reshape(bias_columns, width), select)
    small_grads = jnp.concatenate([vector_grads, bias_grads.astype(BF16)], axis=0)
    small_grads = grid.scatter(grid.cut(small_grads.T)).T
    return (
        outputs,
        grad_inputs,
        small_grads[0],
        small_grads[1],
        out_attn[:, :3].transpose(1, 0, 2),
        out_attn[:, 3].T,
        small_grads[2],
        small_grads[3],
        small_grads[4],
        out_fc1,
        small_grads[6:].reshape(-1)[:hidden_block],
        out_fc2,
        small_grads[5],
    )


def solution(mesh):
    in_specs = (
        P(("dp", "tensor"), None),
        P(("dp", "tensor"), None),
        P("dp"),
        P(("dp", "tensor")),
        P("dp"),
        P("dp"),
        P(None, "dp", "tensor"),
        P("tensor", "dp"),
        P("dp"),
        P("dp"),
        P("dp"),
        P("dp", "tensor"),
        P(("tensor", "dp")),
        P("tensor", "dp"),
        P("dp"),
    )
    out_specs = (
        P(("dp", "tensor"), None),
        P(("dp", "tensor"), None),
        P("dp"),
        P("dp"),
        P(None, "dp", "tensor"),
        P("tensor", "dp"),
        P("dp"),
        P("dp"),
        P("dp"),
        P("dp", "tensor"),
        P(("tensor", "dp")),
        P("tensor", "dp"),
        P("dp"),
    )
    return jax.shard_map(
        on_device, mesh=mesh, in_specs=in_specs, out_specs=out_specs, check_vma=False
    )
```

```python
import functools

import jax
import jax.numpy as jnp
import numpy as np
from jax import lax
from jax.experimental import pallas as pl
from jax.experimental.pallas import tpu as pltpu
from jax.sharding import PartitionSpec as P

HEAD_DIM = 64
SEQ_LEN = 1104
F32 = jnp.float32
BF16 = jnp.bfloat16
MIB = 2**20


def dp_factors(size):
    if size % 8 == 0:
        return (4, 2, size // 8)
    return (1, 1, size)


class DpGrid:
    def __init__(self, size, block):
        self.size = size
        self.block = block
        self.half = block // 2
        self.factors = dp_factors(size)
        self.routes = ((2, 1), (1, 2))

    def coords(self, index):
        _, second, third = self.factors
        return (index // (second * third), (index // third) % second, index % third)

    def index(self, coords):
        _, second, third = self.factors
        return (coords[0] * second + coords[1]) * third + coords[2]

    def ahead(self, index, axis, step):
        coords = list(self.coords(index))
        coords[axis] = (coords[axis] + step) % self.factors[axis]
        return self.index(coords)

    def fetch(self, value, axis, step):
        pairs = [(self.ahead(i, axis, step), i) for i in range(self.size)]
        return lax.ppermute(value, "dp", pairs)

    def push(self, value, axis, step):
        pairs = [(i, self.ahead(i, axis, step)) for i in range(self.size)]
        return lax.ppermute(value, "dp", pairs)

    def spread(self, shard):
        with jax.named_scope("gather_z"):
            return [shard] + [self.fetch(shard, 0, s) for s in range(1, self.factors[0])]

    def middle(self, along):
        halves = []
        for part, (middle, _) in enumerate(self.routes):
            rows = slice(part * self.half, (part + 1) * self.half)
            value = jnp.concatenate([a[..., rows, :] for a in along], axis=-2)
            steps = range(1, self.factors[middle])
            with jax.named_scope("gather_middle"):
                halves.append([value] + [self.fetch(value, middle, s) for s in steps])
        return halves

    def finish(self, halves):
        pieces = []
        for (_, last), parts in zip(self.routes, halves):
            value = jnp.concatenate(parts, axis=-2)
            pieces.append(value)
            with jax.named_scope("gather_last"):
                pieces.extend(self.fetch(value, last, s) for s in range(1, self.factors[last]))
        return pieces

    def gather(self, shard):
        return self.finish(self.middle(self.spread(shard)))

    def spread_middle(self, shard):
        parts = []
        for part, (middle, _) in enumerate(self.routes):
            value = shard[..., part * self.half : (part + 1) * self.half, :]
            with jax.named_scope("gather_middle"):
                steps = range(1, self.factors[middle])
                parts.append([value] + [self.fetch(value, middle, s) for s in steps])
        return parts

    def steps(self, value, axis, steps):
        with jax.named_scope("gather_step"):
            return [self.fetch(value, axis, s) for s in steps if s < self.factors[axis]]

    def halves_of(self, along, counts):
        halves, start = [], 0
        for count in counts:
            rows = slice(start, start + count * self.half)
            start += count * self.half
            value = jnp.stack([a[..., rows, :] for a in along], axis=-3)
            lead, wide = value.shape[:-3], value.shape[-1]
            value = value.reshape(lead + (self.factors[0], count, self.half, wide))
            value = jnp.swapaxes(value, -4, -3)
            halves.append([value.reshape(lead + (-1, wide))])
        return halves

    def reduce_last(self, pieces):
        pieces, halves = list(pieces), []
        for _, last in self.routes:
            mine, pieces = pieces[: self.factors[last]], pieces[self.factors[last] :]
            with jax.named_scope("reduce_last"):
                sent = [self.push(mine[s], last, s) for s in range(1, self.factors[last])]
            halves.append([mine[0]] + sent)
        return halves

    def reduce_middle(self, halves):
        rows, out = self.factors[0] * self.half, []
        for (middle, _), parts in zip(self.routes, halves):
            cut = [
                sum(p[..., s * rows : (s + 1) * rows, :].astype(F32) for p in parts).astype(BF16)
                for s in range(self.factors[middle])
            ]
            with jax.named_scope("reduce_middle"):
                sent = [self.push(cut[s], middle, s) for s in range(1, self.factors[middle])]
            out.append([cut[0]] + sent)
        return out

    def reduce_first(self, halves):
        def along(step):
            rows = slice(step * self.half, (step + 1) * self.half)
            totals = [sum(p[..., rows, :].astype(F32) for p in parts) for parts in halves]
            return jnp.concatenate(totals, axis=-2)

        sent = [along(s).astype(BF16) for s in range(1, self.factors[0])]
        with jax.named_scope("reduce_z"):
            sent = [self.push(p, 0, s) for s, p in enumerate(sent, 1)]
        return [along(0)] + sent

    def reduce_end(self, parts):
        return sum(p.astype(F32) for p in parts)

    def scatter(self, pieces):
        return self.reduce_end(self.reduce_first(self.reduce_middle(self.reduce_last(pieces))))

    def gather_small(self, value, axes):
        for axis in axes:
            with jax.named_scope("gather_small"):
                parts = [value] + [self.fetch(value, axis, s) for s in range(1, self.factors[axis])]
            value = jnp.concatenate(parts, axis=0)
        return value

    def small_in_order(self, value):
        zeroth, second, third = self.factors
        value = value.reshape((zeroth, third, second, value.shape[1], 2, self.half))
        first_half = value[..., 0, :].transpose(3, 2, 1, 0, 4)
        second_half = value[..., 1, :].transpose(3, 1, 2, 0, 4)
        count = value.shape[3]
        return jnp.concatenate(
            [first_half.reshape(count, -1), second_half.reshape(count, -1)], axis=1
        )

    def blocks_of(self, value):
        count, full = value.shape
        second, third = self.factors[1], self.factors[2]
        first_half = value[:, : full // 2].reshape(count, second, third, self.factors[0], self.half)
        second_half = value[:, full // 2 :].reshape(count, third, second, self.factors[0], self.half)
        return jnp.concatenate(
            [first_half.transpose(2, 1, 3, 0, 4), second_half.transpose(1, 2, 3, 0, 4)], axis=-1
        )

    def reduce_small(self, value, axis):
        value = value.astype(BF16)
        total = value[0].astype(F32)
        with jax.named_scope("reduce_small"):
            for step in range(1, self.factors[axis]):
                total = total + self.push(value[step], axis, step).astype(F32)
        return total

    def piece_rows(self):
        full = self.size * self.half
        rows = []
        for _, last in self.routes:
            rows.extend([full // self.factors[last]] * self.factors[last])
        return rows

    def cut(self, value, axis=0):
        edges = np.cumsum(self.piece_rows())[:-1].tolist()
        return jnp.split(value, edges, axis=axis)

    def places(self):
        return (self.features()[:: self.half] // self.half).astype(jnp.int32)

    def features(self):
        here = self.coords(lax.axis_index("dp"))
        indices = []
        for part, (middle, last) in enumerate(self.routes):
            shape = (self.factors[last], self.factors[middle], self.factors[0], self.half)
            steps = [None, None, None]
            steps[last], steps[middle], steps[0], sub = (
                jnp.asarray(g.reshape(-1), jnp.int32) for g in np.indices(shape)
            )
            coords = [(h + s) % f for h, s, f in zip(here, steps, self.factors)]
            indices.append(self.index(coords) * self.block + part * self.half + sub)
        return jnp.concatenate(indices)


class TensorPair:
    def __init__(self, size, slot_count, local_rows):
        self.size = size
        self.relative = size == 2 and slot_count == 1
        self.local_rows = local_rows

    def swap(self, value):
        return lax.ppermute(value, "tensor", [(0, 1), (1, 0)])

    def parts(self, value):
        if self.relative:
            return [value, self.swap(value)]
        return [lax.all_gather(value, "tensor", axis=0, tiled=True)]

    def whole(self, value):
        return jnp.concatenate(self.parts(value), axis=0)

    def own(self, value):
        if self.relative:
            return value[: self.local_rows]
        start = lax.axis_index("tensor") * self.local_rows
        return lax.dynamic_slice_in_dim(value, start, self.local_rows, axis=0)

    def both(self, value):
        if self.relative:
            return value, self.swap(value)
        return lax.psum(value.astype(F32), "tensor"), jnp.zeros((1, value.shape[1]), F32)

    def own_total(self, value):
        if self.relative:
            kept = value[: self.local_rows].astype(F32)
            return kept + self.swap(value[self.local_rows :]).astype(F32)
        return lax.psum_scatter(value, "tensor", scatter_dimension=0, tiled=True).astype(F32)

    def own_both(self, value):
        if self.relative:
            return value[: self.local_rows], self.swap(value[self.local_rows :])
        total = lax.psum_scatter(value, "tensor", scatter_dimension=0, tiled=True)
        return total, jnp.zeros((1, value.shape[1]), F32)

    def small_total(self, value):
        if self.size == 2:
            return value + self.swap(value)
        return lax.psum(value, "tensor")


def join(*groups):
    flat, tree = jax.tree.flatten(groups)
    return jax.tree.unflatten(tree, lax.optimization_barrier(tuple(flat)))


def normalize(values):
    row_mean = jnp.mean(values, axis=-1, keepdims=True)
    centered = values - row_mean
    variance = jnp.mean(centered * centered, axis=-1, keepdims=True)
    inverse = lax.rsqrt(variance + 1e-05)
    return centered * inverse, inverse


def norm_input_grad(grad, gain, normed, inverse):
    scaled = grad * gain
    first = jnp.mean(scaled, axis=-1, keepdims=True)
    second = jnp.mean(scaled * normed, axis=-1, keepdims=True)
    return inverse * (scaled - first - normed * second)


def dot_nn(left, right):
    return lax.dot_general(left, right, (((1,), (0,)), ((), ())), preferred_element_type=F32)


def dot_nt(left, right):
    return lax.dot_general(left, right, (((1,), (1,)), ((), ())), preferred_element_type=F32)


def dot_tn(left, right):
    return lax.dot_general(left, right, (((0,), (0,)), ((), ())), preferred_element_type=F32)


def gelu_and_slope(values):
    cdf = 0.5 + 0.5 * lax.erf(values * (0.5**0.5))
    density = jnp.exp(-0.5 * values * values) * 0.3989422804014327
    return values * cdf, cdf + values * density


def params(limit):
    return pltpu.CompilerParams(vmem_limit_bytes=limit * MIB)


def cost(micros):
    return pl.CostEstimate(
        flops=int(micros * 1e9), transcendentals=0, bytes_accessed=int(micros * 1e6)
    )


def whole_spec(array):
    return pl.BlockSpec(array.shape, lambda *grid: (0,) * len(array.shape))


def stack_rows(refs):
    return jnp.concatenate([r[...] for r in refs], axis=0)


def head_lanes(seq, head):
    lane = lax.broadcasted_iota(jnp.int32, (seq, 2 * HEAD_DIM), 1)
    mine = (lane >= HEAD_DIM) if head else (lane < HEAD_DIM)
    return mine, lane == (0 if head else HEAD_DIM)


def head_operands(query_ref, key_ref, invalid, head):
    seq = query_ref.shape[0]
    mine, extra = head_lanes(seq, head)
    one, zero = jnp.asarray(1, BF16), jnp.asarray(0, BF16)
    scaled = query_ref[...] * jnp.asarray(HEAD_DIM**-0.5, BF16)
    query = jnp.where(mine, scaled, jnp.where(extra, one, zero))
    keys = jnp.where(mine, key_ref[...], jnp.where(extra, invalid, zero))
    return query, keys


def key_column(invalid_ref):
    seq = invalid_ref.shape[-1]
    return jnp.broadcast_to(invalid_ref[0], (2 * HEAD_DIM, seq)).T.astype(BF16)


def attend_kernel(query_ref, key_ref, value_ref, invalid_ref, mixed_ref, total_ref, turned_ref):
    seq = query_ref.shape[0]
    invalid = key_column(invalid_ref)
    values = value_ref[...].T
    for head in range(2):
        rows = slice(head * HEAD_DIM, (head + 1) * HEAD_DIM)
        query, keys = head_operands(query_ref, key_ref, invalid, head)
        with_ones = jnp.concatenate([values[rows], jnp.ones((16, seq), BF16)], axis=0)
        scores = dot_nt(keys, query)
        largest = jnp.max(scores, axis=0, keepdims=True)
        weights = jnp.exp(scores - largest)
        mixed = dot_nn(with_ones, weights.astype(BF16))
        weight_sum = mixed[HEAD_DIM : HEAD_DIM + 1]
        turned_ref[rows] = mixed[:HEAD_DIM] * (1.0 / weight_sum)
        total_ref[0, 0, head : head + 1] = largest + jnp.log(weight_sum)
    mixed_ref[...] = turned_ref[...].T.astype(BF16)


def attend_back_kernel(
    query_ref,
    key_ref,
    value_ref,
    invalid_ref,
    mixed_ref,
    total_ref,
    grad_ref,
    grad_query_ref,
    grad_key_ref,
    grad_value_ref,
    turned_ref,
    prob_ref,
    score_ref,
):
    seq = query_ref.shape[0]
    invalid = key_column(invalid_ref)
    keys_turned = key_ref[...].T
    product = mixed_ref[...].astype(F32).T * grad_ref[...].astype(F32).T
    for head in range(2):
        rows = slice(head * HEAD_DIM, (head + 1) * HEAD_DIM)
        mine, _ = head_lanes(seq, head)
        query, keys = head_operands(query_ref, key_ref, invalid, head)
        grad = jnp.where(mine, grad_ref[...], jnp.asarray(0, BF16))
        row_dot = jnp.sum(product[rows], axis=0, keepdims=True)
        for start in range(0, seq, 256):
            cut = slice(start, min(start + 256, seq))
            prob = jnp.exp(dot_nt(keys, query[cut]) - total_ref[0, 0, head : head + 1, cut])
            grad_prob = dot_nt(value_ref[...], grad[cut]) - row_dot[:, cut]
            grad_score = (prob * grad_prob).astype(BF16)
            prob_ref[:, cut] = prob.astype(BF16)
            score_ref[:, cut] = grad_score
            turned_ref[rows, cut] = dot_nn(keys_turned[rows], grad_score) * HEAD_DIM**-0.5
        grad_value = dot_nn(prob_ref[...], grad)
        grad_key = dot_nn(score_ref[...], jnp.where(mine, query, jnp.asarray(0, BF16)))
        if head == 0:
            first_value, first_key = grad_value, grad_key
    grad_value_ref[...] = (first_value + grad_value).astype(BF16)
    grad_key_ref[...] = (first_key + grad_key).astype(BF16)
    grad_query_ref[...] = turned_ref[...].T.astype(BF16)


def attend_specs():
    def columns(offset):
        return pl.BlockSpec((SEQ_LEN, 2 * HEAD_DIM), lambda s, p: (s, p + offset))

    invalid = pl.BlockSpec((1, 1, SEQ_LEN), lambda s, p: (s, 0, 0))
    total = pl.BlockSpec((1, 1, 2, SEQ_LEN), lambda s, p: (s, p, 0, 0))
    return columns, invalid, total


def attend(packed, invalid, first, count):
    slots, pairs = invalid.shape[0], packed.shape[1] // (6 * HEAD_DIM)
    columns, invalid_spec, total_spec = attend_specs()
    return pl.pallas_call(
        attend_kernel,
        grid=(slots, count),
        in_specs=[columns(first), columns(pairs + first), columns(2 * pairs + first), invalid_spec],
        out_specs=[columns(0), total_spec],
        out_shape=[
            jax.ShapeDtypeStruct((packed.shape[0], count * 2 * HEAD_DIM), BF16),
            jax.ShapeDtypeStruct((slots, count, 2, SEQ_LEN), F32),
        ],
        scratch_shapes=[pltpu.VMEM((2 * HEAD_DIM, SEQ_LEN), F32)],
        compiler_params=params(48),
        cost_estimate=cost(4 * slots * count),
        name="attend",
    )(packed, packed, packed, invalid)


def attend_back(packed, invalid, mixed, total, grad_mixed, first, count):
    slots, pairs = invalid.shape[0], packed.shape[1] // (6 * HEAD_DIM)
    columns, invalid_spec, _ = attend_specs()
    return pl.pallas_call(
        attend_back_kernel,
        grid=(slots, count),
        in_specs=[
            columns(first),
            columns(pairs + first),
            columns(2 * pairs + first),
            invalid_spec,
            columns(first),
            pl.BlockSpec((1, 1, 2, SEQ_LEN), lambda s, p: (s, p + first, 0, 0)),
            columns(first),
        ],
        out_specs=[columns(0)] * 3,
        out_shape=[jax.ShapeDtypeStruct((mixed.shape[0], count * 2 * HEAD_DIM), BF16)] * 3,
        scratch_shapes=[
            pltpu.VMEM((2 * HEAD_DIM, SEQ_LEN), F32),
            pltpu.VMEM((SEQ_LEN, SEQ_LEN), BF16),
            pltpu.VMEM((SEQ_LEN, SEQ_LEN), BF16),
        ],
        compiler_params=params(48),
        cost_estimate=cost(9 * slots * count),
        name="attend_back",
    )(packed, packed, packed, invalid, mixed, total, grad_mixed)


def joined(pieces, first, count):
    return jnp.concatenate(
        [jnp.concatenate([p[g] for p in pieces], axis=0) for g in range(first, first + count)],
        axis=1,
    )


def times_pieces(rows, pieces, first, count, fits):
    if not fits:
        return dot_nn(rows, joined(pieces, first, count)).astype(BF16)
    wide = pieces[0].shape[2]

    def kernel(rows_ref, *refs):
        weight = jnp.concatenate([r[0] for r in refs[:-1]], axis=0)
        refs[-1][...] = dot_nn(rows_ref[...], weight).astype(BF16)

    return pl.pallas_call(
        kernel,
        grid=(count,),
        in_specs=[whole_spec(rows)]
        + [pl.BlockSpec((1, p.shape[1], wide), lambda j: (first + j, 0, 0)) for p in pieces],
        out_specs=pl.BlockSpec((rows.shape[0], wide), lambda j: (0, j)),
        out_shape=jax.ShapeDtypeStruct((rows.shape[0], count * wide), BF16),
        compiler_params=params(40),
        cost_estimate=cost(2 * count),
        name="times_pieces",
    )(rows, *pieces)


def times_pieces_turned(columns, pieces, places, fits):
    count = len(columns)
    rows, wide = columns[0].shape
    if not fits:
        weight = [joined(pieces, g, 1)[:, c * wide : (c + 1) * wide] for g, c in places]
        total = dot_nt(jnp.concatenate(columns, axis=1), jnp.concatenate(weight, axis=1))
        return total.astype(BF16)
    starts = np.cumsum([0] + [p.shape[1] for p in pieces]).tolist()

    def kernel(*refs):
        lefts, weights, out_ref = refs[:count], refs[count:-1], refs[-1]
        for i, start in enumerate(starts[:-1]):
            total = 0.0
            for k in range(count):
                total = total + dot_nt(lefts[k][...], weights[i * count + k][0])
            out_ref[:, start : starts[i + 1]] = total.astype(BF16)

    def place_spec(piece, group, column):
        return pl.BlockSpec((1, piece.shape[1], wide), lambda i: (group, 0, column))

    return pl.pallas_call(
        kernel,
        grid=(1,),
        in_specs=[whole_spec(c) for c in columns] + [place_spec(p, *q) for p in pieces for q in places],
        out_specs=pl.BlockSpec((rows, starts[-1]), lambda i: (0, 0)),
        out_shape=jax.ShapeDtypeStruct((rows, starts[-1]), BF16),
        compiler_params=params(48),
        cost_estimate=cost(1 + count),
        name="times_pieces_turned",
    )(*columns, *[p for p in pieces for _ in places])


def weight_grads(lefts, rights, piece_rows, fits):
    starts = np.cumsum([0] + piece_rows).tolist()
    if not fits:
        full = jnp.stack([dot_tn(a, b).astype(BF16) for a, b in zip(lefts, rights)])
        return [full[:, s:e] for s, e in zip(starts, starts[1:])]
    count = len(rights)
    wide = rights[0].shape[1]
    names = []
    for left in lefts:
        if not any(left is other for other in names):
            names.append(left)
    which = [next(i for i, o in enumerate(names) if o is left) for left in lefts]

    def kernel(*refs):
        left_refs, right_refs = refs[: len(names)], refs[len(names) : len(names) + count]
        out_refs = refs[len(names) + count :]
        for i, (start, end) in enumerate(zip(starts, starts[1:])):
            turned = [r[:, start:end].T for r in left_refs]
            for k in range(count):
                out_refs[i][k] = dot_nn(turned[which[k]], right_refs[k][...]).astype(BF16)

    return pl.pallas_call(
        kernel,
        grid=(1,),
        in_specs=[whole_spec(a) for a in names + list(rights)],
        out_specs=[pl.BlockSpec((count, r, wide), lambda i: (0, 0, 0)) for r in piece_rows],
        out_shape=[jax.ShapeDtypeStruct((count, r, wide), BF16) for r in piece_rows],
        compiler_params=params(56),
        cost_estimate=cost(1 + 1.5 * count),
        name="weight_grads",
    )(*names, *rights)


def joined_rows(parts):
    return parts[0] if len(parts) == 1 else jnp.concatenate(parts, axis=0)


def first_norm(rows_in, gain, bias, fits):
    width = rows_in[0].shape[1]
    rows = sum(p.shape[0] for p in rows_in)

    def work(values, gain, bias):
        normed, _ = normalize(values.astype(F32))
        return (normed * gain + bias).astype(BF16)

    if not fits:
        return work(joined_rows(rows_in), gain, bias)

    def kernel(*refs):
        gain, bias, out_ref = refs[-3][...], refs[-2][...], refs[-1]
        start = 0
        for ref in refs[:-3]:
            out_ref[start : start + ref.shape[0]] = work(ref[...], gain, bias)
            start += ref.shape[0]

    return pl.pallas_call(
        kernel,
        out_shape=jax.ShapeDtypeStruct((rows, width), BF16),
        compiler_params=params(40),
        cost_estimate=cost(3),
        name="first_norm",
    )(*rows_in, gain, bias)


def second_norm(rows_in, live, mine, other, shift, gain, bias, fits):
    rows, width = mine.shape

    def work(rows_in, live, mine, other, shift, gain, bias):
        branch = mine.astype(F32) + other.astype(F32) + shift
        middle = rows_in.astype(F32) + live * branch
        normed, _ = normalize(middle)
        return middle, (normed * gain + bias).astype(BF16)

    if not fits:
        return work(joined_rows(rows_in), live, mine, other, shift, gain, bias)
    half = rows // 2

    def kernel(own_ref, next_ref, live_ref, mine_ref, other_ref, *refs):
        vectors = [r[...] for r in refs[:3]]
        for i, ref in enumerate((own_ref, next_ref)):
            cut, turned = slice(i * half, (i + 1) * half), slice((1 - i) * half, (2 - i) * half)
            refs[3][cut], refs[4][cut] = work(
                ref[...], live_ref[cut], mine_ref[cut], other_ref[turned], *vectors
            )

    return pl.pallas_call(
        kernel,
        out_shape=[
            jax.ShapeDtypeStruct((rows, width), F32),
            jax.ShapeDtypeStruct((rows, width), BF16),
        ],
        compiler_params=params(40),
        cost_estimate=cost(4),
        name="second_norm",
    )(*rows_in, live, mine, other, shift, gain, bias)


def norm_back(grad_out, live, mine, other, middle, gain, fits):
    rows, width = middle.shape

    def work(grad_out, live, mine, other, middle, gain):
        grad_out = grad_out.astype(F32)
        grad = mine.astype(F32) + other.astype(F32)
        normed, inverse = normalize(middle)
        grad_middle = grad_out + norm_input_grad(grad, gain, normed, inverse)
        grad_branch = (live * grad_middle).astype(BF16)
        sums = [grad * normed, grad, grad_branch.astype(F32), grad_out]
        sums = jnp.concatenate([jnp.sum(s, axis=0, keepdims=True) for s in sums], axis=0)
        return grad_middle, grad_branch, sums

    if not fits:
        return work(joined_rows(grad_out), live, mine, other, middle, gain)
    half = rows // 2

    def kernel(own_ref, next_ref, live_ref, mine_ref, other_ref, middle_ref, gain_ref, *refs):
        total = 0.0
        for i, ref in enumerate((own_ref, next_ref)):
            cut, turned = slice(i * half, (i + 1) * half), slice((1 - i) * half, (2 - i) * half)
            refs[0][cut], refs[1][cut], sums = work(
                ref[...],
                live_ref[cut],
                mine_ref[cut],
                other_ref[turned],
                middle_ref[cut],
                gain_ref[...],
            )
            total = total + sums
        refs[2][...] = total

    return pl.pallas_call(
        kernel,
        out_shape=[
            jax.ShapeDtypeStruct((rows, width), F32),
            jax.ShapeDtypeStruct((rows, width), BF16),
            jax.ShapeDtypeStruct((4, width), F32),
        ],
        compiler_params=params(48),
        cost_estimate=cost(7),
        name="norm_back",
    )(*grad_out, live, mine, other, middle, gain)


def first_norm_back(grad_middle, rest, mine, other, rows_in, gain, fits):
    rows, width = rows_in.shape

    def work(grad_middle, rest, mine, other, rows_in, gain):
        grad = mine.astype(F32) + other.astype(F32)
        normed, inverse = normalize(rows_in.astype(F32))
        grad_rows = grad_middle + rest.astype(F32) + norm_input_grad(grad, gain, normed, inverse)
        sums = [jnp.sum(s, axis=0, keepdims=True) for s in (grad * normed, grad)]
        return grad_rows.astype(BF16), jnp.concatenate(sums, axis=0)

    if not fits:
        return work(grad_middle, rest, mine, other, rows_in, gain)

    def kernel(*refs):
        refs[-2][...], refs[-1][...] = work(*[r[...] for r in refs[:-2]])

    own = pl.BlockSpec((rows, width), lambda i: (0, 0))
    return pl.pallas_call(
        kernel,
        grid=(1,),
        in_specs=[own] * 5 + [pl.BlockSpec((1, width), lambda i: (0, 0))],
        out_specs=[own, pl.BlockSpec((2, width), lambda i: (0, 0))],
        out_shape=[
            jax.ShapeDtypeStruct((rows, width), BF16),
            jax.ShapeDtypeStruct((2, width), F32),
        ],
        compiler_params=params(40),
        cost_estimate=cost(4),
        name="first_norm_back",
    )(grad_middle, rest, mine, other, rows_in, gain)


def feed_kernel(counts, carried, plain, scattered, places_ref, *refs):
    halves, pieces, grad_pieces = counts
    normed_ref, shift_ref, grad_refs = refs[0], refs[1], refs[2 : 2 + halves]
    refs = refs[2 + halves :]
    first_refs, second_refs, refs = refs[:pieces], refs[pieces : 2 * pieces], refs[2 * pieces :]
    before, refs = (refs[:2], refs[2:]) if carried else ((), refs)
    out_ref, grad_two_ref, shift_grad_ref = refs[:3]
    weight_grad_refs = refs[3 : 3 + grad_pieces]
    grad_ref, normed_turned, grad_turned, out_sum, grad_sum = refs[3 + grad_pieces :]
    step = pl.program_id(0)
    blocks = places_ref.shape[0]
    size = normed_ref.shape[1] // blocks

    def place(i):
        return pl.ds(pl.multiple_of(places_ref[i] * size, size), size)

    @pl.when(step == 0)
    def _():
        start = 0
        for ref in grad_refs:
            grad_ref[start : start + ref.shape[0]] = ref[...]
            start += ref.shape[0]
        if scattered:
            for i in range(blocks):
                rows = slice(i * size, (i + 1) * size)
                normed_turned[place(i)] = normed_ref[:, rows].T
                grad_turned[place(i)] = grad_ref[:, rows].T
        else:
            normed_turned[...] = normed_ref[...].T
            grad_turned[...] = grad_ref[...].T
        if carried:
            out_sum[...] = before[0][...].astype(F32)
            grad_sum[...] = before[1][...].astype(F32)
        else:
            out_sum[...] = jnp.zeros_like(out_sum)
            grad_sum[...] = jnp.zeros_like(grad_sum)

    if plain:
        first = jnp.concatenate([first_refs[0][place(i)] for i in range(blocks)], axis=0)
        second = jnp.concatenate([second_refs[0][place(i)] for i in range(blocks)], axis=0)
    else:
        first = jnp.concatenate([w[0] for w in first_refs], axis=0)
        second = jnp.concatenate([w[0] for w in second_refs], axis=0)
    hidden = dot_nn(normed_ref[...], first) + shift_ref[...]
    hidden_act, slope = gelu_and_slope(hidden)
    hidden_act = hidden_act.astype(BF16)
    grad_pre = (dot_nn(grad_ref[...], second) * slope).astype(BF16)
    out_sum[...] += dot_nt(hidden_act, second)
    grad_sum[...] += dot_nt(grad_pre, first)
    shift_grad_ref[...] = jnp.sum(grad_pre.astype(F32), axis=0, keepdims=True)
    if scattered:
        weight_grad_refs[0][...] = dot_nn(normed_turned[...], grad_pre).astype(BF16)
        weight_grad_refs[1][...] = dot_nn(grad_turned[...], hidden_act).astype(BF16)
    else:
        start = 0
        for ref in weight_grad_refs:
            rows = slice(start, start + ref.shape[2])
            ref[0, 0] = dot_nn(normed_turned[rows], grad_pre).astype(BF16)
            ref[1, 0] = dot_nn(grad_turned[rows], hidden_act).astype(BF16)
            start += ref.shape[2]

    @pl.when(step == pl.num_programs(0) - 1)
    def _():
        out_ref[...] = out_sum[...].astype(BF16)
        grad_two_ref[...] = grad_sum[...].astype(BF16)


def feed_forward(normed, grads, shift, weight, places, piece_rows, before, fits):
    rows, width = normed.shape
    plain, scattered = not isinstance(weight, list), piece_rows is None
    units = shift.shape[1]
    wide = units if plain else weight[0].shape[2]
    groups = units // wide
    if not fits:
        size = width // places.shape[0]
        order = (places[:, None] * size + jnp.arange(size)[None, :]).reshape(-1)
        if plain:
            both = jnp.take(weight, order, axis=0)
            first_w, second_w = both[:, :units], both[:, units:]
        else:
            first_w, second_w = joined(weight, 0, groups), joined(weight, groups, groups)
        grad = jnp.concatenate(grads, axis=0)
        hidden_act, slope = gelu_and_slope(dot_nn(normed, first_w) + shift)
        hidden_act = hidden_act.astype(BF16)
        grad_pre = (dot_nn(grad, second_w) * slope).astype(BF16)
        out, grad_two = dot_nt(hidden_act, second_w), dot_nt(grad_pre, first_w)
        if before:
            out, grad_two = out + before[0].astype(F32), grad_two + before[1].astype(F32)
        outs = [dot_tn(normed, grad_pre).astype(BF16), dot_tn(grad, hidden_act).astype(BF16)]
        if scattered:
            outs = [jnp.zeros_like(g).at[order].set(g) for g in outs]
        else:
            size = units // 2
            outs = jnp.stack([g[:, k * size : (k + 1) * size] for g in outs for k in range(2)])
            outs = jnp.split(outs, np.cumsum(piece_rows)[:-1].tolist(), 1)
        shift_grad = jnp.sum(grad_pre, axis=0, dtype=F32, keepdims=True)
        return [out.astype(BF16), grad_two.astype(BF16), shift_grad] + outs

    tile = min(256, units // 2)
    per = wide // tile
    pieces = [weight] if plain else weight

    def once(array):
        return pl.BlockSpec(
            array.shape, lambda j, p: (0,) * len(array.shape), pipeline_mode=pl.Buffered(1)
        )

    def weight_spec(piece, second):
        if plain:
            return pl.BlockSpec((width, tile), lambda j, p: (0, second * per + j))
        return pl.BlockSpec(
            (1, piece.shape[1], tile), lambda j, p: (second * groups + j // per, 0, j % per)
        )

    if scattered:
        grad_specs = [pl.BlockSpec((width, tile), lambda j, p: (0, j))] * 2
        grad_shapes = [jax.ShapeDtypeStruct((width, units), BF16)] * 2
    else:
        half = units // 2
        split = half // tile
        grad_specs = [
            pl.BlockSpec((2, 1, r, tile), lambda j, p: (0, j // split, 0, j % split))
            for r in piece_rows
        ]
        grad_shapes = [jax.ShapeDtypeStruct((2, 2, r, half), BF16) for r in piece_rows]
    before = tuple(before)
    outs = pl.pallas_call(
        functools.partial(
            feed_kernel,
            (len(grads), len(pieces), len(grad_shapes)),
            bool(before),
            plain,
            scattered,
        ),
        grid_spec=pltpu.PrefetchScalarGridSpec(
            num_scalar_prefetch=1,
            grid=(units // tile,),
            in_specs=[once(normed), pl.BlockSpec((1, tile), lambda j, p: (0, j))]
            + [once(g) for g in grads]
            + [weight_spec(p, 0) for p in pieces]
            + [weight_spec(p, 1) for p in pieces]
            + [once(b) for b in before],
            out_specs=[
                pl.BlockSpec((rows, width), lambda j, p: (0, 0)),
                pl.BlockSpec((rows, width), lambda j, p: (0, 0)),
                pl.BlockSpec((1, tile), lambda j, p: (0, j)),
            ]
            + grad_specs,
            scratch_shapes=[
                pltpu.VMEM((rows, width), BF16),
                pltpu.VMEM((width, rows), BF16),
                pltpu.VMEM((width, rows), BF16),
                pltpu.VMEM((rows, width), F32),
                pltpu.VMEM((rows, width), F32),
            ],
        ),
        out_shape=[
            jax.ShapeDtypeStruct((rows, width), BF16),
            jax.ShapeDtypeStruct((rows, width), BF16),
            jax.ShapeDtypeStruct((1, units), F32),
        ]
        + grad_shapes,
        compiler_params=params(60),
        cost_estimate=cost(6.3 * (units // tile)),
        name="feed_forward",
    )(places, normed, shift, *grads, *pieces, *pieces, *before)
    outs = list(outs)
    if not scattered:
        outs[3:] = [g.reshape((4,) + g.shape[2:]) for g in outs[3:]]
    return outs


def on_device(
    inputs,
    cotangent,
    slot_live,
    token_type,
    attn_norm_gain,
    attn_norm_bias,
    qkv_weight,
    proj_weight,
    proj_bias,
    mlp_norm_gain,
    mlp_norm_bias,
    fc1_weight,
    fc1_bias,
    fc2_weight,
    fc2_bias,
):
    dp_size = lax.axis_size("dp")
    tensor_size = lax.axis_size("tensor")
    local_rows, width = inputs.shape
    slot_count = slot_live.shape[0]
    whole_rows = local_rows * tensor_size
    block = fc1_weight.shape[0]
    width_here = qkv_weight.shape[2]
    hidden_here = fc1_weight.shape[1]
    hidden_block = fc1_bias.shape[0]
    hidden_cut = hidden_here // 2
    fits = whole_rows <= 2048
    grid = DpGrid(dp_size, block)
    pair = TensorPair(tensor_size, slot_count, local_rows)
    half_cut = hidden_cut // 2

    bias_columns = -(-hidden_block // block)
    bias_pad = bias_columns * block - hidden_block
    smalls = jnp.stack(
        (attn_norm_gain, attn_norm_bias, proj_bias, mlp_norm_gain, mlp_norm_bias, fc2_bias)
    )
    bias_block = jnp.pad(fc1_bias, (0, bias_pad)).reshape(bias_columns, block)
    smalls = jnp.concatenate([smalls, bias_block], axis=0)
    fc2_turned = fc2_weight.T
    cuts = slice(0, hidden_cut), slice(hidden_cut, hidden_here)
    groups = [
        w[:, start : start + half_cut]
        for w in (fc1_weight, fc2_turned)
        for start in (0, half_cut)
    ]
    first_shard = jnp.stack(groups)
    second_shard = jnp.stack(
        [
            w[:, start : start + half_cut]
            for w in (fc1_weight, fc2_turned)
            for start in (hidden_cut, hidden_cut + half_cut)
        ]
    )
    attn_shard = jnp.concatenate([qkv_weight, proj_weight.T[None]], axis=0)

    attn_along = grid.spread(attn_shard)
    smalls = grid.gather_small(smalls[None], (1, 2))
    second_parts = grid.spread_middle(second_shard)
    attn_along, smalls, second_parts, first_shard, inputs, cotangent = join(
        attn_along, smalls, second_parts, first_shard, inputs, cotangent
    )

    attn_halves = grid.middle(attn_along)
    first_along = [first_shard] + grid.steps(first_shard, 0, (1,))
    smalls = grid.gather_small(smalls, (0,))
    features, places = grid.features(), grid.places()
    select = (jnp.arange(width, dtype=jnp.int32)[:, None] == features[None, :]).astype(BF16)
    own_in = dot_nn(inputs, select).astype(BF16)
    rows_in = pair.parts(own_in)
    own_grad = dot_nn(cotangent, select)
    live_col = jnp.repeat(slot_live.astype(F32), SEQ_LEN)[:, None]
    own_live = pair.own(live_col)
    grad_mlp = pair.parts((own_live * own_grad).astype(BF16))
    rest_grad = ((1.0 - own_live) * own_grad).astype(BF16)
    valid_whole = pair.whole((token_type != 3).astype(F32))
    invalid = jnp.where(valid_whole > 0, 0.0, -1e30).reshape(slot_count, 1, SEQ_LEN)
    attn_halves, first_along = join(attn_halves, first_along)

    attn_pieces = grid.finish(attn_halves)
    first_along += grid.steps(first_along[0], 0, (2, 3))
    smalls = grid.small_in_order(smalls)
    gain_one, shift_one, proj_shift, gain_two, shift_two, fc2_shift = (
        smalls[i : i + 1].astype(F32) for i in range(6)
    )
    fc1_shift = dot_nt(smalls[6:], select).reshape(bias_columns, dp_size, block)
    fc1_shift = fc1_shift.transpose(1, 0, 2).reshape(dp_size, bias_columns * block)
    fc1_shift = fc1_shift[:, :hidden_block].reshape(1, hidden_here)
    norm_one = first_norm(rows_in, gain_one, shift_one, fits)
    attn_pieces, first_along, norm_one, second_parts, grad_mlp, invalid = join(
        attn_pieces, first_along, norm_one, second_parts, grad_mlp, invalid
    )

    first_halves = grid.middle(first_along)
    second_own = jnp.concatenate(second_parts[0] + second_parts[1], axis=-2)
    second_counts = [len(p) for p in second_parts]
    second_near = grid.steps(second_own, 0, (1, 3))
    packed = times_pieces(norm_one, attn_pieces, 0, 3, fits)
    pairs = width_here // (2 * HEAD_DIM)
    parts = 2 if pairs % 2 == 0 else 1
    share = pairs // parts
    mixed, total = attend(packed, invalid, 0, pairs)
    first_halves, second_near, second_own, mixed, total, packed, attn_pieces, norm_one = join(
        first_halves, second_near, second_own, mixed, total, packed, attn_pieces, norm_one
    )

    first_pieces = grid.finish(first_halves)
    second_far = grid.steps(second_own, 0, (2,))
    attn_out = times_pieces_turned([mixed], attn_pieces, [(3, 0)], fits)
    middle, norm_two = second_norm(
        rows_in, live_col, *pair.both(attn_out), proj_shift, gain_two, shift_two, fits
    )
    first_pieces, second_far, middle, norm_two = join(first_pieces, second_far, middle, norm_two)

    second_along = [second_own] + second_near[:1] + second_far + second_near[1:]
    second_pieces = grid.finish(grid.halves_of(second_along, second_counts))
    piece_rows = grid.piece_rows()
    shifts = [fc1_shift[:, :hidden_cut], fc1_shift[:, hidden_cut:]]
    feed_a = feed_forward(
        norm_two, grad_mlp, shifts[0], first_pieces, places, piece_rows, (), fits
    )
    second_pieces, feed_a, norm_two = join(second_pieces, feed_a, norm_two)

    last_a = grid.reduce_last(feed_a[3:])
    feed_b = feed_forward(
        norm_two, grad_mlp, shifts[1], second_pieces, places, piece_rows, feed_a[:2], fits
    )
    grad_fc1_bias = jnp.concatenate([feed_a[2], feed_b[2]], axis=1)
    last_a, feed_b = join(last_a, feed_b)
    mlp_out, grad_two = feed_b[:2]

    middle_a = grid.reduce_middle(last_a)
    grad_middle, grad_branch, sums = norm_back(
        grad_mlp, live_col, *pair.both(grad_two), middle, gain_two, fits
    )
    grad_mixed = times_pieces(grad_branch, attn_pieces, 3, 1, fits)
    middle_a, grad_mixed, pieces_b, grad_middle, grad_branch = join(
        middle_a, grad_mixed, feed_b[3:], grad_middle, grad_branch
    )

    def back(part):
        return attend_back(packed, invalid, mixed, total, grad_mixed, part * share, share)

    def grads(part, columns):
        lefts, rights = (norm_one,) * 3, tuple(columns)
        if part == 0:
            cut = width_here // parts
            lefts = lefts + (grad_branch,) * parts
            rights = rights + tuple(mixed[:, p * cut : (p + 1) * cut] for p in range(parts))
        return weight_grads(lefts, rights, piece_rows, fits)

    last_b = grid.reduce_last(pieces_b)
    first_a = grid.reduce_first(middle_a)
    columns = back(0)
    last_b, first_a, columns, grad_mixed = join(last_b, first_a, columns, grad_mixed)

    middle_b = grid.reduce_middle(last_b)
    pieces_c = grads(0, columns)
    middle_b, pieces_c, grad_mixed = join(middle_b, pieces_c, grad_mixed)

    last_c = grid.reduce_last(pieces_c)
    first_b = grid.reduce_first(middle_b)
    if parts == 2:
        more = back(1)
        last_c, first_b, more = join(last_c, first_b, more)
        columns = columns + more
    else:
        last_c, first_b = join(last_c, first_b)

    middle_c = grid.reduce_middle(last_c)
    places_c = [(j, p) for p in range(parts) for j in range(3)]
    if parts == 2:
        pieces_d = grads(1, more)
        pieces_d, columns = join(pieces_d, columns)
        last_d = grid.reduce_last(pieces_d)
    grad_one = times_pieces_turned(columns, attn_pieces, places_c, fits)
    middle_c, grad_one, mlp_out = join(middle_c, grad_one, mlp_out)

    first_c = grid.reduce_first(middle_c)
    grad_rows, sums_one = first_norm_back(
        pair.own(grad_middle), rest_grad, *pair.own_both(grad_one), own_in, gain_one, fits
    )
    sums_one = pair.small_total(sums_one)
    mlp_out = pair.own_total(mlp_out)
    first_a, first_b = grid.reduce_end(first_a), grid.reduce_end(first_b)
    if parts == 2:
        last_d, sums_one, grad_rows = join(last_d, sums_one, grad_rows)
        middle_d = grid.reduce_middle(last_d)
    bias_grads = grad_fc1_bias.astype(BF16).reshape(dp_size, hidden_block)
    bias_grads = jnp.pad(bias_grads, ((0, 0), (0, bias_pad))).reshape(dp_size, bias_columns, block)
    bias_grads = dot_nn(bias_grads.transpose(1, 0, 2).reshape(bias_columns, width), select)
    small_grads = jnp.concatenate([sums_one, sums, bias_grads], axis=0)
    small_grads = grid.blocks_of(small_grads)
    small_grads = grid.reduce_small(small_grads, 2)
    small_grads = grid.reduce_small(small_grads, 1)
    grad_inputs = dot_nt(grad_rows, select).astype(BF16)
    if parts == 2:
        first_c, middle_d, small_grads = join(first_c, middle_d, small_grads)
        first_d = grid.reduce_first(middle_d)
    else:
        first_c, small_grads = join(first_c, small_grads)
    small_grads = grid.reduce_small(small_grads, 0)
    result = pair.own(middle) + own_live * (mlp_out + fc2_shift)
    outputs = dot_nt(result.astype(BF16), select).astype(BF16)
    out_fc1 = jnp.concatenate([first_a[0], first_a[1], first_b[0], first_b[1]], axis=1)
    out_fc2 = jnp.concatenate([first_a[2], first_a[3], first_b[2], first_b[3]], axis=1)
    out_c = grid.reduce_end(first_c)
    out_qkv = out_c[:3]
    if parts == 2:
        out_qkv = jnp.concatenate([out_qkv, grid.reduce_end(first_d)], axis=2)
    out_proj = jnp.concatenate([out_c[3 + p] for p in range(parts)], axis=1)
    return (
        outputs,
        grad_inputs,
        small_grads[0],
        small_grads[1],
        out_qkv,
        out_proj.T,
        small_grads[4],
        small_grads[2],
        small_grads[3],
        out_fc1,
        small_grads[6:].reshape(-1)[:hidden_block],
        out_fc2.T,
        small_grads[5],
    )


def solution(mesh):
    in_specs = (
        P(("dp", "tensor"), None),
        P(("dp", "tensor"), None),
        P("dp"),
        P(("dp", "tensor")),
        P("dp"),
        P("dp"),
        P(None, "dp", "tensor"),
        P("tensor", "dp"),
        P("dp"),
        P("dp"),
        P("dp"),
        P("dp", "tensor"),
        P(("tensor", "dp")),
        P("tensor", "dp"),
        P("dp"),
    )
    out_specs = (
        P(("dp", "tensor"), None),
        P(("dp", "tensor"), None),
        P("dp"),
        P("dp"),
        P(None, "dp", "tensor"),
        P("tensor", "dp"),
        P("dp"),
        P("dp"),
        P("dp"),
        P("dp", "tensor"),
        P(("tensor", "dp")),
        P("tensor", "dp"),
        P("dp"),
    )
    return jax.shard_map(
        on_device, mesh=mesh, in_specs=in_specs, out_specs=out_specs, check_vma=False
    )
```

```python
import functools

import jax
import jax.numpy as jnp
import numpy as np
from jax import lax
from jax.experimental import pallas as pl
from jax.experimental.pallas import tpu as pltpu
from jax.sharding import PartitionSpec as P

HEAD_DIM = 64
SEQ_LEN = 1104
F32 = jnp.float32
BF16 = jnp.bfloat16
MIB = 2**20


def dp_factors(size):
    if size % 8 == 0:
        return (4, 2, size // 8)
    return (1, 1, size)


class DpGrid:
    def __init__(self, size, block):
        self.size = size
        self.block = block
        self.half = block // 2
        self.factors = dp_factors(size)
        self.routes = ((2, 1), (1, 2))

    def coords(self, index):
        _, second, third = self.factors
        return (index // (second * third), (index // third) % second, index % third)

    def index(self, coords):
        _, second, third = self.factors
        return (coords[0] * second + coords[1]) * third + coords[2]

    def ahead(self, index, axis, step):
        coords = list(self.coords(index))
        coords[axis] = (coords[axis] + step) % self.factors[axis]
        return self.index(coords)

    def fetch(self, value, axis, step):
        pairs = [(self.ahead(i, axis, step), i) for i in range(self.size)]
        return lax.ppermute(value, "dp", pairs)

    def push(self, value, axis, step):
        pairs = [(i, self.ahead(i, axis, step)) for i in range(self.size)]
        return lax.ppermute(value, "dp", pairs)

    def spread(self, shard):
        with jax.named_scope("gather_z"):
            return [shard] + [self.fetch(shard, 0, s) for s in range(1, self.factors[0])]

    def middle(self, along):
        halves = []
        for part, (middle, _) in enumerate(self.routes):
            rows = slice(part * self.half, (part + 1) * self.half)
            value = jnp.concatenate([a[..., rows, :] for a in along], axis=-2)
            steps = range(1, self.factors[middle])
            with jax.named_scope("gather_middle"):
                halves.append([value] + [self.fetch(value, middle, s) for s in steps])
        return halves

    def finish(self, halves):
        pieces = []
        for (_, last), parts in zip(self.routes, halves):
            value = jnp.concatenate(parts, axis=-2)
            pieces.append(value)
            with jax.named_scope("gather_last"):
                pieces.extend(self.fetch(value, last, s) for s in range(1, self.factors[last]))
        return pieces

    def gather(self, shard):
        return self.finish(self.middle(self.spread(shard)))

    def spread_middle(self, shard):
        parts = []
        for part, (middle, _) in enumerate(self.routes):
            value = shard[..., part * self.half : (part + 1) * self.half, :]
            with jax.named_scope("gather_middle"):
                steps = range(1, self.factors[middle])
                parts.append([value] + [self.fetch(value, middle, s) for s in steps])
        return parts

    def steps(self, value, axis, steps):
        with jax.named_scope("gather_step"):
            return [self.fetch(value, axis, s) for s in steps if s < self.factors[axis]]

    def halves_of(self, along, counts):
        halves, start = [], 0
        for count in counts:
            rows = slice(start, start + count * self.half)
            start += count * self.half
            value = jnp.stack([a[..., rows, :] for a in along], axis=-3)
            lead, wide = value.shape[:-3], value.shape[-1]
            value = value.reshape(lead + (self.factors[0], count, self.half, wide))
            value = jnp.swapaxes(value, -4, -3)
            halves.append([value.reshape(lead + (-1, wide))])
        return halves

    def reduce_last(self, pieces):
        pieces, halves = list(pieces), []
        for _, last in self.routes:
            mine, pieces = pieces[: self.factors[last]], pieces[self.factors[last] :]
            with jax.named_scope("reduce_last"):
                sent = [self.push(mine[s], last, s) for s in range(1, self.factors[last])]
            halves.append([mine[0]] + sent)
        return halves

    def reduce_middle(self, halves):
        rows, out = self.factors[0] * self.half, []
        for (middle, _), parts in zip(self.routes, halves):
            cut = [
                sum(p[..., s * rows : (s + 1) * rows, :].astype(F32) for p in parts).astype(BF16)
                for s in range(self.factors[middle])
            ]
            with jax.named_scope("reduce_middle"):
                sent = [self.push(cut[s], middle, s) for s in range(1, self.factors[middle])]
            out.append([cut[0]] + sent)
        return out

    def first_pieces(self, halves):
        def along(step):
            rows = slice(step * self.half, (step + 1) * self.half)
            totals = [sum(p[..., rows, :].astype(F32) for p in parts) for parts in halves]
            return jnp.concatenate(totals, axis=-2)

        return [along(0)] + [along(s).astype(BF16) for s in range(1, self.factors[0])]

    def send_first(self, pieces, steps):
        with jax.named_scope("reduce_z"):
            return [self.push(pieces[s], 0, s) for s in steps if s < len(pieces)]

    def reduce_first(self, halves):
        pieces = self.first_pieces(halves)
        return pieces[:1] + self.send_first(pieces, (1, 2, 3))

    def reduce_end(self, parts):
        return sum(p.astype(F32) for p in parts)

    def scatter(self, pieces):
        return self.reduce_end(self.reduce_first(self.reduce_middle(self.reduce_last(pieces))))

    def gather_small(self, value, axes):
        for axis in axes:
            with jax.named_scope("gather_small"):
                parts = [value] + [self.fetch(value, axis, s) for s in range(1, self.factors[axis])]
            value = jnp.concatenate(parts, axis=0)
        return value

    def small_in_order(self, value):
        zeroth, second, third = self.factors
        value = value.reshape((third, second, zeroth, value.shape[1], 2, self.half))
        first_half = value[..., 0, :].transpose(3, 1, 0, 2, 4)
        second_half = value[..., 1, :].transpose(3, 0, 1, 2, 4)
        count = value.shape[3]
        return jnp.concatenate(
            [first_half.reshape(count, -1), second_half.reshape(count, -1)], axis=1
        )

    def blocks_of(self, value):
        count, full = value.shape
        second, third = self.factors[1], self.factors[2]
        first_half = value[:, : full // 2].reshape(count, second, third, self.factors[0], self.half)
        second_half = value[:, full // 2 :].reshape(count, third, second, self.factors[0], self.half)
        return jnp.concatenate(
            [first_half.transpose(2, 1, 3, 0, 4), second_half.transpose(1, 2, 3, 0, 4)], axis=-1
        )

    def reduce_small(self, value, axis):
        value = value.astype(BF16)
        total = value[0].astype(F32)
        with jax.named_scope("reduce_small"):
            for step in range(1, self.factors[axis]):
                total = total + self.push(value[step], axis, step).astype(F32)
        return total

    def piece_rows(self):
        full = self.size * self.half
        rows = []
        for _, last in self.routes:
            rows.extend([full // self.factors[last]] * self.factors[last])
        return rows

    def cut(self, value, axis=0):
        edges = np.cumsum(self.piece_rows())[:-1].tolist()
        return jnp.split(value, edges, axis=axis)

    def places(self):
        return (self.features()[:: self.half] // self.half).astype(jnp.int32)

    def features(self):
        here = self.coords(lax.axis_index("dp"))
        indices = []
        for part, (middle, last) in enumerate(self.routes):
            shape = (self.factors[last], self.factors[middle], self.factors[0], self.half)
            steps = [None, None, None]
            steps[last], steps[middle], steps[0], sub = (
                jnp.asarray(g.reshape(-1), jnp.int32) for g in np.indices(shape)
            )
            coords = [(h + s) % f for h, s, f in zip(here, steps, self.factors)]
            indices.append(self.index(coords) * self.block + part * self.half + sub)
        return jnp.concatenate(indices)


class TensorPair:
    def __init__(self, size, slot_count, local_rows):
        self.size = size
        self.relative = size == 2 and slot_count == 1
        self.local_rows = local_rows

    def swap(self, value):
        return lax.ppermute(value, "tensor", [(0, 1), (1, 0)])

    def parts(self, value):
        if self.relative:
            return [value, self.swap(value)]
        return [lax.all_gather(value, "tensor", axis=0, tiled=True)]

    def whole(self, value):
        return jnp.concatenate(self.parts(value), axis=0)

    def own(self, value):
        if self.relative:
            return value[: self.local_rows]
        start = lax.axis_index("tensor") * self.local_rows
        return lax.dynamic_slice_in_dim(value, start, self.local_rows, axis=0)

    def both(self, value):
        if self.relative:
            return value, self.swap(value)
        return lax.psum(value.astype(F32), "tensor"), jnp.zeros((1, value.shape[1]), F32)

    def own_total(self, value):
        if self.relative:
            kept = value[: self.local_rows].astype(F32)
            return kept + self.swap(value[self.local_rows :]).astype(F32)
        return lax.psum_scatter(value, "tensor", scatter_dimension=0, tiled=True).astype(F32)

    def own_both(self, halves):
        if self.relative:
            return halves[0], self.swap(halves[1])
        value = jnp.concatenate(halves, axis=0)
        total = lax.psum_scatter(value, "tensor", scatter_dimension=0, tiled=True)
        return total, jnp.zeros((1, value.shape[1]), F32)

    def small_total(self, value):
        if self.size == 2:
            return value + self.swap(value)
        return lax.psum(value, "tensor")


def join(*groups):
    flat, tree = jax.tree.flatten(groups)
    return jax.tree.unflatten(tree, lax.optimization_barrier(tuple(flat)))


def normalize(values):
    row_mean = jnp.mean(values, axis=-1, keepdims=True)
    centered = values - row_mean
    variance = jnp.mean(centered * centered, axis=-1, keepdims=True)
    inverse = lax.rsqrt(variance + 1e-05)
    return centered * inverse, inverse


def norm_input_grad(grad, gain, normed, inverse):
    scaled = grad * gain
    first = jnp.mean(scaled, axis=-1, keepdims=True)
    second = jnp.mean(scaled * normed, axis=-1, keepdims=True)
    return inverse * (scaled - first - normed * second)


def dot_nn(left, right):
    return lax.dot_general(left, right, (((1,), (0,)), ((), ())), preferred_element_type=F32)


def dot_nt(left, right):
    return lax.dot_general(left, right, (((1,), (1,)), ((), ())), preferred_element_type=F32)


def dot_tn(left, right):
    return lax.dot_general(left, right, (((0,), (0,)), ((), ())), preferred_element_type=F32)


def gelu_and_slope(values):
    cdf = 0.5 + 0.5 * lax.erf(values * (0.5**0.5))
    density = jnp.exp(-0.5 * values * values) * 0.3989422804014327
    return values * cdf, cdf + values * density


def params(limit):
    return pltpu.CompilerParams(vmem_limit_bytes=limit * MIB)


def cost(micros):
    return pl.CostEstimate(
        flops=int(micros * 1e9), transcendentals=0, bytes_accessed=int(micros * 1e6)
    )


def whole_spec(array):
    return pl.BlockSpec(array.shape, lambda *grid: (0,) * len(array.shape))


def stack_rows(refs):
    return jnp.concatenate([r[...] for r in refs], axis=0)


def head_lanes(seq, head):
    lane = lax.broadcasted_iota(jnp.int32, (seq, 2 * HEAD_DIM), 1)
    mine = (lane >= HEAD_DIM) if head else (lane < HEAD_DIM)
    return mine, lane == (0 if head else HEAD_DIM)


def head_operands(query_ref, key_ref, invalid, head):
    seq = query_ref.shape[0]
    mine, extra = head_lanes(seq, head)
    one, zero = jnp.asarray(1, BF16), jnp.asarray(0, BF16)
    scaled = query_ref[...] * jnp.asarray(HEAD_DIM**-0.5, BF16)
    query = jnp.where(mine, scaled, jnp.where(extra, one, zero))
    keys = jnp.where(mine, key_ref[...], jnp.where(extra, invalid, zero))
    return query, keys


def key_column(invalid_ref):
    seq = invalid_ref.shape[-1]
    return jnp.broadcast_to(invalid_ref[0], (2 * HEAD_DIM, seq)).T.astype(BF16)


def attend_kernel(query_ref, key_ref, value_ref, invalid_ref, mixed_ref, total_ref, turned_ref):
    seq = query_ref.shape[0]
    invalid = key_column(invalid_ref)
    values = value_ref[...].T
    for head in range(2):
        rows = slice(head * HEAD_DIM, (head + 1) * HEAD_DIM)
        query, keys = head_operands(query_ref, key_ref, invalid, head)
        with_ones = jnp.concatenate([values[rows], jnp.ones((16, seq), BF16)], axis=0)
        scores = dot_nt(keys, query)
        largest = jnp.max(scores, axis=0, keepdims=True)
        weights = jnp.exp(scores - largest)
        mixed = dot_nn(with_ones, weights.astype(BF16))
        weight_sum = mixed[HEAD_DIM : HEAD_DIM + 1]
        turned_ref[rows] = mixed[:HEAD_DIM] * (1.0 / weight_sum)
        total_ref[0, 0, head : head + 1] = largest + jnp.log(weight_sum)
    mixed_ref[...] = turned_ref[...].T.astype(BF16)


def attend_back_kernel(
    query_ref,
    key_ref,
    value_ref,
    invalid_ref,
    mixed_ref,
    total_ref,
    grad_ref,
    grad_query_ref,
    grad_key_ref,
    grad_value_ref,
    turned_ref,
    prob_ref,
    score_ref,
):
    seq = query_ref.shape[0]
    invalid = key_column(invalid_ref)
    keys_turned = key_ref[...].T
    product = mixed_ref[...].astype(F32).T * grad_ref[...].astype(F32).T
    for head in range(2):
        rows = slice(head * HEAD_DIM, (head + 1) * HEAD_DIM)
        mine, _ = head_lanes(seq, head)
        query, keys = head_operands(query_ref, key_ref, invalid, head)
        grad = jnp.where(mine, grad_ref[...], jnp.asarray(0, BF16))
        row_dot = jnp.sum(product[rows], axis=0, keepdims=True)
        for start in range(0, seq, 256):
            cut = slice(start, min(start + 256, seq))
            prob = jnp.exp(dot_nt(keys, query[cut]) - total_ref[0, 0, head : head + 1, cut])
            grad_prob = dot_nt(value_ref[...], grad[cut]) - row_dot[:, cut]
            grad_score = (prob * grad_prob).astype(BF16)
            prob_ref[:, cut] = prob.astype(BF16)
            score_ref[:, cut] = grad_score
            turned_ref[rows, cut] = dot_nn(keys_turned[rows], grad_score) * HEAD_DIM**-0.5
        grad_value = dot_nn(prob_ref[...], grad)
        grad_key = dot_nn(score_ref[...], jnp.where(mine, query, jnp.asarray(0, BF16)))
        if head == 0:
            first_value, first_key = grad_value, grad_key
    grad_value_ref[...] = (first_value + grad_value).astype(BF16)
    grad_key_ref[...] = (first_key + grad_key).astype(BF16)
    grad_query_ref[...] = turned_ref[...].T.astype(BF16)


def attend_specs():
    def columns(offset):
        return pl.BlockSpec((SEQ_LEN, 2 * HEAD_DIM), lambda s, p: (s, p + offset))

    invalid = pl.BlockSpec((1, 1, SEQ_LEN), lambda s, p: (s, 0, 0))
    total = pl.BlockSpec((1, 1, 2, SEQ_LEN), lambda s, p: (s, p, 0, 0))
    return columns, invalid, total


def attend(packed, invalid, first, count):
    slots, pairs = invalid.shape[0], packed.shape[1] // (6 * HEAD_DIM)
    columns, invalid_spec, total_spec = attend_specs()
    return pl.pallas_call(
        attend_kernel,
        grid=(slots, count),
        in_specs=[columns(first), columns(pairs + first), columns(2 * pairs + first), invalid_spec],
        out_specs=[columns(0), total_spec],
        out_shape=[
            jax.ShapeDtypeStruct((packed.shape[0], count * 2 * HEAD_DIM), BF16),
            jax.ShapeDtypeStruct((slots, count, 2, SEQ_LEN), F32),
        ],
        scratch_shapes=[pltpu.VMEM((2 * HEAD_DIM, SEQ_LEN), F32)],
        compiler_params=params(48),
        cost_estimate=cost(4 * slots * count),
        name="attend",
    )(packed, packed, packed, invalid)


def attend_back(packed, invalid, mixed, total, grad_mixed, first, count):
    slots, pairs = invalid.shape[0], packed.shape[1] // (6 * HEAD_DIM)
    columns, invalid_spec, total_spec = attend_specs()
    return pl.pallas_call(
        attend_back_kernel,
        grid=(slots, count),
        in_specs=[
            columns(first),
            columns(pairs + first),
            columns(2 * pairs + first),
            invalid_spec,
            columns(0),
            total_spec,
            columns(first),
        ],
        out_specs=[columns(0)] * 3,
        out_shape=[jax.ShapeDtypeStruct((mixed.shape[0], count * 2 * HEAD_DIM), BF16)] * 3,
        scratch_shapes=[
            pltpu.VMEM((2 * HEAD_DIM, SEQ_LEN), F32),
            pltpu.VMEM((SEQ_LEN, SEQ_LEN), BF16),
            pltpu.VMEM((SEQ_LEN, SEQ_LEN), BF16),
        ],
        compiler_params=params(48),
        cost_estimate=cost(9 * slots * count),
        name="attend_back",
    )(packed, packed, packed, invalid, mixed, total, grad_mixed)


def joined(pieces, first, count):
    return jnp.concatenate(
        [jnp.concatenate([p[g] for p in pieces], axis=0) for g in range(first, first + count)],
        axis=1,
    )


def times_pieces(rows, pieces, first, count, fits):
    if not fits:
        return dot_nn(rows, joined(pieces, first, count)).astype(BF16)
    wide = pieces[0].shape[2]

    def kernel(rows_ref, *refs):
        weight = jnp.concatenate([r[0] for r in refs[:-1]], axis=0)
        refs[-1][...] = dot_nn(rows_ref[...], weight).astype(BF16)

    return pl.pallas_call(
        kernel,
        grid=(count,),
        in_specs=[whole_spec(rows)]
        + [pl.BlockSpec((1, p.shape[1], wide), lambda j: (first + j, 0, 0)) for p in pieces],
        out_specs=pl.BlockSpec((rows.shape[0], wide), lambda j: (0, j)),
        out_shape=jax.ShapeDtypeStruct((rows.shape[0], count * wide), BF16),
        compiler_params=params(40),
        cost_estimate=cost(2 * count),
        name="times_pieces",
    )(rows, *pieces)


def times_pieces_turned(columns, pieces, places, fits, cuts=1):
    count = len(columns)
    rows, wide = columns[0].shape
    if not fits:
        weight = [joined(pieces, g, 1)[:, c * wide : (c + 1) * wide] for g, c in places]
        total = dot_nt(jnp.concatenate(columns, axis=1), jnp.concatenate(weight, axis=1))
        return jnp.split(total.astype(BF16), cuts) if cuts > 1 else total.astype(BF16)
    starts = np.cumsum([0] + [p.shape[1] for p in pieces]).tolist()

    def kernel(*refs):
        lefts, weights, out_refs = refs[:count], refs[count:-cuts], refs[-cuts:]
        left = jnp.concatenate([r[...] for r in lefts], axis=1)
        weight = jnp.concatenate(
            [
                jnp.concatenate([r[0] for r in weights[i * count : (i + 1) * count]], axis=1)
                for i in range(len(pieces))
            ],
            axis=0,
        )
        for k, out_ref in enumerate(out_refs):
            cut = slice(k * rows // cuts, (k + 1) * rows // cuts)
            out_ref[...] = dot_nt(left[cut], weight).astype(BF16)

    def place_spec(piece, group, column):
        return pl.BlockSpec((1, piece.shape[1], wide), lambda i: (group, 0, column))

    outs = pl.pallas_call(
        kernel,
        grid=(1,),
        in_specs=[whole_spec(c) for c in columns] + [place_spec(p, *q) for p in pieces for q in places],
        out_specs=[pl.BlockSpec((rows // cuts, starts[-1]), lambda i: (0, 0))] * cuts,
        out_shape=[jax.ShapeDtypeStruct((rows // cuts, starts[-1]), BF16)] * cuts,
        compiler_params=params(48),
        cost_estimate=cost(1 + count),
        name="times_pieces_turned",
    )(*columns, *[p for p in pieces for _ in places])
    return outs if cuts > 1 else outs[0]


def weight_grads(lefts, rights, piece_rows, fits):
    starts = np.cumsum([0] + piece_rows).tolist()
    if not fits:
        full = jnp.stack([dot_tn(a, b).astype(BF16) for a, b in zip(lefts, rights)])
        return [full[:, s:e] for s, e in zip(starts, starts[1:])]
    count = len(rights)
    wide = rights[0].shape[1]
    names = []
    for left in lefts:
        if not any(left is other for other in names):
            names.append(left)
    which = [next(i for i, o in enumerate(names) if o is left) for left in lefts]

    def kernel(*refs):
        left_refs, right_refs = refs[: len(names)], refs[len(names) : len(names) + count]
        out_refs = refs[len(names) + count :]
        turned = [r[...].T for r in left_refs]
        for k in range(count):
            product = dot_nn(turned[which[k]], right_refs[k][...]).astype(BF16)
            for i, (start, end) in enumerate(zip(starts, starts[1:])):
                out_refs[i][k] = product[start:end]

    return pl.pallas_call(
        kernel,
        grid=(1,),
        in_specs=[whole_spec(a) for a in names + list(rights)],
        out_specs=[pl.BlockSpec((count, r, wide), lambda i: (0, 0, 0)) for r in piece_rows],
        out_shape=[jax.ShapeDtypeStruct((count, r, wide), BF16) for r in piece_rows],
        compiler_params=params(56),
        cost_estimate=cost(1 + 1.5 * count),
        name="weight_grads",
    )(*names, *rights)


def joined_rows(parts):
    return parts[0] if len(parts) == 1 else jnp.concatenate(parts, axis=0)


def first_norm(rows_in, gain, bias, fits):
    width = rows_in[0].shape[1]
    rows = sum(p.shape[0] for p in rows_in)

    def work(values, gain, bias):
        normed, _ = normalize(values.astype(F32))
        return (normed * gain + bias).astype(BF16)

    if not fits:
        return work(joined_rows(rows_in), gain, bias)

    def kernel(*refs):
        gain, bias, out_ref = refs[-3][...], refs[-2][...], refs[-1]
        start = 0
        for ref in refs[:-3]:
            out_ref[start : start + ref.shape[0]] = work(ref[...], gain, bias)
            start += ref.shape[0]

    return pl.pallas_call(
        kernel,
        out_shape=jax.ShapeDtypeStruct((rows, width), BF16),
        compiler_params=params(40),
        cost_estimate=cost(3),
        name="first_norm",
    )(*rows_in, gain, bias)


def second_norm(rows_in, live, mine, other, shift, gain, bias, fits):
    rows, width = mine.shape

    def work(rows_in, live, mine, other, shift, gain, bias):
        branch = mine.astype(F32) + other.astype(F32) + shift
        middle = rows_in.astype(F32) + live * branch
        normed, _ = normalize(middle)
        return middle, (normed * gain + bias).astype(BF16)

    if not fits:
        return work(joined_rows(rows_in), live, mine, other, shift, gain, bias)
    half = rows // 2

    def kernel(own_ref, next_ref, *refs):
        rows_in = jnp.where(pl.program_id(0) == 0, own_ref[...], next_ref[...])
        refs[-2][...], refs[-1][...] = work(rows_in, *[r[...] for r in refs[:-2]])

    def block(columns, place=lambda i: i):
        return pl.BlockSpec((half, columns), lambda i: (place(i), 0))

    return pl.pallas_call(
        kernel,
        grid=(2,),
        in_specs=[
            block(width, lambda i: 0),
            block(width, lambda i: 0),
            block(1),
            block(width),
            block(width, lambda i: 1 - i),
        ]
        + [whole_spec(shift)] * 3,
        out_specs=[block(width), block(width)],
        out_shape=[
            jax.ShapeDtypeStruct((rows, width), F32),
            jax.ShapeDtypeStruct((rows, width), BF16),
        ],
        compiler_params=params(40),
        cost_estimate=cost(4),
        name="second_norm",
    )(*rows_in, live, mine, other, shift, gain, bias)


def norm_back(grad_out, live, mine, other, middle, gain, fits):
    rows, width = middle.shape

    def work(grad_out, live, mine, other, middle, gain):
        grad_out = grad_out.astype(F32)
        grad = mine.astype(F32) + other.astype(F32)
        normed, inverse = normalize(middle)
        grad_middle = grad_out + norm_input_grad(grad, gain, normed, inverse)
        grad_branch = (live * grad_middle).astype(BF16)
        sums = [grad * normed, grad, grad_branch.astype(F32), grad_out]
        sums = jnp.concatenate([jnp.sum(s, axis=0, keepdims=True) for s in sums], axis=0)
        return grad_middle, grad_branch, sums

    if not fits:
        return work(joined_rows(grad_out), live, mine, other, middle, gain)
    half = rows // 2

    def kernel(own_ref, next_ref, live_ref, mine_ref, other_ref, middle_ref, gain_ref, *refs):
        step = pl.program_id(0)
        grad = jnp.where(step == 0, own_ref[...], next_ref[...])
        rest = [r[...] for r in (live_ref, mine_ref, other_ref, middle_ref, gain_ref)]
        grad_middle, refs[1][...], sums = work(grad, *rest)

        @pl.when(step == 0)
        def _():
            refs[0][...] = grad_middle
            refs[2][...] = sums

        @pl.when(step == 1)
        def _():
            refs[2][...] += sums

    def block(columns, place=lambda i: i):
        return pl.BlockSpec((half, columns), lambda i: (place(i), 0))

    return pl.pallas_call(
        kernel,
        grid=(2,),
        in_specs=[
            block(width, lambda i: 0),
            block(width, lambda i: 0),
            block(1),
            block(width),
            block(width, lambda i: 1 - i),
            block(width),
            whole_spec(gain),
        ],
        out_specs=[
            block(width, lambda i: 0),
            block(width),
            pl.BlockSpec((4, width), lambda i: (0, 0)),
        ],
        out_shape=[
            jax.ShapeDtypeStruct((half, width), F32),
            jax.ShapeDtypeStruct((rows, width), BF16),
            jax.ShapeDtypeStruct((4, width), F32),
        ],
        compiler_params=params(40),
        cost_estimate=cost(7),
        name="norm_back",
    )(*grad_out, live, mine, other, middle, gain)


def first_norm_back(grad_middle, rest, mine, other, rows_in, gain, fits):
    rows, width = rows_in.shape

    def work(grad_middle, rest, mine, other, rows_in, gain):
        grad = mine.astype(F32) + other.astype(F32)
        normed, inverse = normalize(rows_in.astype(F32))
        grad_rows = grad_middle + rest.astype(F32) + norm_input_grad(grad, gain, normed, inverse)
        sums = [jnp.sum(s, axis=0, keepdims=True) for s in (grad * normed, grad)]
        return grad_rows.astype(BF16), jnp.concatenate(sums, axis=0)

    if not fits:
        return work(grad_middle, rest, mine, other, rows_in, gain)

    def kernel(*refs):
        refs[-2][...], refs[-1][...] = work(*[r[...] for r in refs[:-2]])

    own = pl.BlockSpec((rows, width), lambda i: (0, 0))
    return pl.pallas_call(
        kernel,
        grid=(1,),
        in_specs=[own] * 5 + [pl.BlockSpec((1, width), lambda i: (0, 0))],
        out_specs=[own, pl.BlockSpec((2, width), lambda i: (0, 0))],
        out_shape=[
            jax.ShapeDtypeStruct((rows, width), BF16),
            jax.ShapeDtypeStruct((2, width), F32),
        ],
        compiler_params=params(40),
        cost_estimate=cost(4),
        name="first_norm_back",
    )(grad_middle, rest, mine, other, rows_in, gain)


def feed_kernel(counts, carried, plain, scattered, places_ref, *refs):
    halves, pieces, grad_pieces = counts
    normed_ref, shift_ref, grad_refs = refs[0], refs[1], refs[2 : 2 + halves]
    refs = refs[2 + halves :]
    first_refs, second_refs, refs = refs[:pieces], refs[pieces : 2 * pieces], refs[2 * pieces :]
    before, refs = (refs[:2], refs[2:]) if carried else ((), refs)
    out_ref, grad_two_ref, shift_grad_ref = refs[:3]
    weight_grad_refs = refs[3 : 3 + grad_pieces]
    grad_ref, normed_turned, grad_turned, out_sum, grad_sum = refs[3 + grad_pieces :]
    step = pl.program_id(0)
    blocks = places_ref.shape[0]
    size = normed_ref.shape[1] // blocks

    def place(i):
        return pl.ds(pl.multiple_of(places_ref[i] * size, size), size)

    @pl.when(step == 0)
    def _():
        start = 0
        for ref in grad_refs:
            grad_ref[start : start + ref.shape[0]] = ref[...]
            start += ref.shape[0]
        if scattered:
            for i in range(blocks):
                rows = slice(i * size, (i + 1) * size)
                normed_turned[place(i)] = normed_ref[:, rows].T
                grad_turned[place(i)] = grad_ref[:, rows].T
        else:
            normed_turned[...] = normed_ref[...].T
            grad_turned[...] = grad_ref[...].T

    if plain:
        first = jnp.concatenate([first_refs[0][place(i)] for i in range(blocks)], axis=0)
        second = jnp.concatenate([second_refs[0][place(i)] for i in range(blocks)], axis=0)
    else:
        first = jnp.concatenate([w[0] for w in first_refs], axis=0)
        second = jnp.concatenate([w[0] for w in second_refs], axis=0)
    hidden = dot_nn(normed_ref[...], first) + shift_ref[...]
    hidden_act, slope = gelu_and_slope(hidden)
    hidden_act = hidden_act.astype(BF16)
    grad_pre = (dot_nn(grad_ref[...], second) * slope).astype(BF16)
    shift_grad_ref[...] = jnp.sum(grad_pre.astype(F32), axis=0, keepdims=True)
    last = pl.num_programs(0) - 1
    products = (
        (out_sum, out_ref, hidden_act, second, before[:1]),
        (grad_sum, grad_two_ref, grad_pre, first, before[1:]),
    )

    @pl.when(step == 0)
    def _():
        for sum_ref, _, left, right, start in products:
            product = dot_nt(left, right)
            sum_ref[...] = product + start[0][...].astype(F32) if carried else product

    @pl.when((step > 0) & (step < last))
    def _():
        for sum_ref, _, left, right, _ in products:
            sum_ref[...] += dot_nt(left, right)

    @pl.when(step == last)
    def _():
        for sum_ref, end_ref, left, right, _ in products:
            end_ref[...] = (sum_ref[...] + dot_nt(left, right)).astype(BF16)

    if scattered:
        weight_grad_refs[0][...] = dot_nn(normed_turned[...], grad_pre).astype(BF16)
        weight_grad_refs[1][...] = dot_nn(grad_turned[...], hidden_act).astype(BF16)
    else:
        for k, (left, right) in enumerate(
            ((normed_turned, grad_pre), (grad_turned, hidden_act))
        ):
            product, start = dot_nn(left[...], right).astype(BF16), 0
            for ref in weight_grad_refs:
                ref[k, 0] = product[start : start + ref.shape[2]]
                start += ref.shape[2]


def feed_forward(normed, grads, shift, weight, places, piece_rows, before, fits):
    rows, width = normed.shape
    plain, scattered = not isinstance(weight, list), piece_rows is None
    units = shift.shape[1]
    wide = units if plain else weight[0].shape[2]
    groups = units // wide
    if not fits:
        size = width // places.shape[0]
        order = (places[:, None] * size + jnp.arange(size)[None, :]).reshape(-1)
        if plain:
            both = jnp.take(weight, order, axis=0)
            first_w, second_w = both[:, :units], both[:, units:]
        else:
            first_w, second_w = joined(weight, 0, groups), joined(weight, groups, groups)
        grad = jnp.concatenate(grads, axis=0)
        hidden_act, slope = gelu_and_slope(dot_nn(normed, first_w) + shift)
        hidden_act = hidden_act.astype(BF16)
        grad_pre = (dot_nn(grad, second_w) * slope).astype(BF16)
        out, grad_two = dot_nt(hidden_act, second_w), dot_nt(grad_pre, first_w)
        if before:
            out, grad_two = out + before[0].astype(F32), grad_two + before[1].astype(F32)
        outs = [dot_tn(normed, grad_pre).astype(BF16), dot_tn(grad, hidden_act).astype(BF16)]
        if scattered:
            outs = [jnp.zeros_like(g).at[order].set(g) for g in outs]
        else:
            size = units // 2
            outs = jnp.stack([g[:, k * size : (k + 1) * size] for g in outs for k in range(2)])
            outs = jnp.split(outs, np.cumsum(piece_rows)[:-1].tolist(), 1)
        shift_grad = jnp.sum(grad_pre, axis=0, dtype=F32, keepdims=True)
        return [out.astype(BF16), grad_two.astype(BF16), shift_grad] + outs

    tile = units // 2
    per = wide // tile
    pieces = [weight] if plain else weight

    def once(array):
        return pl.BlockSpec(
            array.shape, lambda j, p: (0,) * len(array.shape), pipeline_mode=pl.Buffered(1)
        )

    def weight_spec(piece, second):
        if plain:
            return pl.BlockSpec((width, tile), lambda j, p: (0, second * per + j))
        return pl.BlockSpec(
            (1, piece.shape[1], tile), lambda j, p: (second * groups + j // per, 0, j % per)
        )

    if scattered:
        grad_specs = [pl.BlockSpec((width, tile), lambda j, p: (0, j))] * 2
        grad_shapes = [jax.ShapeDtypeStruct((width, units), BF16)] * 2
    else:
        half = units // 2
        split = half // tile
        grad_specs = [
            pl.BlockSpec((2, 1, r, tile), lambda j, p: (0, j // split, 0, j % split))
            for r in piece_rows
        ]
        grad_shapes = [jax.ShapeDtypeStruct((2, 2, r, half), BF16) for r in piece_rows]
    before = tuple(before)
    outs = pl.pallas_call(
        functools.partial(
            feed_kernel,
            (len(grads), len(pieces), len(grad_shapes)),
            bool(before),
            plain,
            scattered,
        ),
        grid_spec=pltpu.PrefetchScalarGridSpec(
            num_scalar_prefetch=1,
            grid=(units // tile,),
            in_specs=[once(normed), pl.BlockSpec((1, tile), lambda j, p: (0, j))]
            + [once(g) for g in grads]
            + [weight_spec(p, 0) for p in pieces]
            + [weight_spec(p, 1) for p in pieces]
            + [once(b) for b in before],
            out_specs=[
                pl.BlockSpec((rows, width), lambda j, p: (0, 0)),
                pl.BlockSpec((rows, width), lambda j, p: (0, 0)),
                pl.BlockSpec((1, tile), lambda j, p: (0, j)),
            ]
            + grad_specs,
            scratch_shapes=[
                pltpu.VMEM((rows, width), BF16),
                pltpu.VMEM((width, rows), BF16),
                pltpu.VMEM((width, rows), BF16),
                pltpu.VMEM((rows, width), F32),
                pltpu.VMEM((rows, width), F32),
            ],
        ),
        out_shape=[
            jax.ShapeDtypeStruct((rows, width), BF16),
            jax.ShapeDtypeStruct((rows, width), BF16),
            jax.ShapeDtypeStruct((1, units), F32),
        ]
        + grad_shapes,
        compiler_params=params(52),
        cost_estimate=cost(25),
        name="feed_forward",
    )(places, normed, shift, *grads, *pieces, *pieces, *before)
    outs = list(outs)
    if not scattered:
        outs[3:] = [g.reshape((4,) + g.shape[2:]) for g in outs[3:]]
    return outs


def on_device(
    inputs,
    cotangent,
    slot_live,
    token_type,
    attn_norm_gain,
    attn_norm_bias,
    qkv_weight,
    proj_weight,
    proj_bias,
    mlp_norm_gain,
    mlp_norm_bias,
    fc1_weight,
    fc1_bias,
    fc2_weight,
    fc2_bias,
):
    dp_size = lax.axis_size("dp")
    tensor_size = lax.axis_size("tensor")
    local_rows, width = inputs.shape
    slot_count = slot_live.shape[0]
    whole_rows = local_rows * tensor_size
    block = fc1_weight.shape[0]
    width_here = qkv_weight.shape[2]
    hidden_here = fc1_weight.shape[1]
    hidden_block = fc1_bias.shape[0]
    hidden_cut = hidden_here // 2
    fits = whole_rows <= 2048
    grid = DpGrid(dp_size, block)
    pair = TensorPair(tensor_size, slot_count, local_rows)
    half_cut = hidden_cut // 2

    bias_columns = -(-hidden_block // block)
    bias_pad = bias_columns * block - hidden_block
    smalls = jnp.stack(
        (attn_norm_gain, attn_norm_bias, proj_bias, mlp_norm_gain, mlp_norm_bias, fc2_bias)
    )
    bias_block = jnp.pad(fc1_bias, (0, bias_pad)).reshape(bias_columns, block)
    smalls = jnp.concatenate([smalls, bias_block], axis=0)
    fc2_turned = fc2_weight.T
    cuts = slice(0, hidden_cut), slice(hidden_cut, hidden_here)
    groups = [
        w[:, start : start + half_cut]
        for w in (fc1_weight, fc2_turned)
        for start in (0, half_cut)
    ]
    first_shard = jnp.stack(groups)
    second_shard = jnp.stack(
        [
            w[:, start : start + half_cut]
            for w in (fc1_weight, fc2_turned)
            for start in (hidden_cut, hidden_cut + half_cut)
        ]
    )
    attn_shard = jnp.concatenate([qkv_weight, proj_weight.T[None]], axis=0)
    count = smalls.shape[0]
    spare = ((0, 3), (0, 0), (0, width_here - block))
    attn_shard = jnp.concatenate([attn_shard, jnp.pad(smalls[None], spare)], axis=1)

    attn_along = grid.spread(attn_shard)
    smalls = jnp.stack([a[0, block:, :block] for a in attn_along])
    second_parts = grid.spread_middle(second_shard)
    attn_along, smalls, second_parts, first_shard, inputs, cotangent = join(
        attn_along, smalls, second_parts, first_shard, inputs, cotangent
    )

    attn_halves = grid.middle(attn_along)
    smalls = grid.gather_small(smalls, (1, 2))
    second_own = jnp.concatenate(second_parts[0] + second_parts[1], axis=-2)
    second_counts = [len(p) for p in second_parts]
    features, places = grid.features(), grid.places()
    select = (jnp.arange(width, dtype=jnp.int32)[:, None] == features[None, :]).astype(BF16)
    own_in = dot_nn(inputs, select).astype(BF16)
    own_in, first_shard = join(own_in, first_shard)
    first_along = [first_shard] + grid.steps(first_shard, 0, (1,))
    rows_in = pair.parts(own_in)
    own_grad = dot_nn(cotangent, select)
    live_col = jnp.repeat(slot_live.astype(F32), SEQ_LEN)[:, None]
    own_live = pair.own(live_col)
    grad_mlp = pair.parts((own_live * own_grad).astype(BF16))
    rest_grad = ((1.0 - own_live) * own_grad).astype(BF16)
    valid_whole = pair.whole((token_type != 3).astype(F32))
    invalid = jnp.where(valid_whole > 0, 0.0, -1e30).reshape(slot_count, 1, SEQ_LEN)
    attn_halves, first_along, second_own, smalls = join(
        attn_halves, first_along, second_own, smalls
    )

    attn_pieces = grid.finish(attn_halves)
    first_along += grid.steps(first_along[0], 0, (2, 3))
    smalls = grid.small_in_order(smalls)
    gain_one, shift_one, proj_shift, gain_two, shift_two, fc2_shift = (
        smalls[i : i + 1].astype(F32) for i in range(6)
    )
    fc1_shift = dot_nt(smalls[6:], select).reshape(bias_columns, dp_size, block)
    fc1_shift = fc1_shift.transpose(1, 0, 2).reshape(dp_size, bias_columns * block)
    fc1_shift = fc1_shift[:, :hidden_block].reshape(1, hidden_here)
    norm_one = first_norm(rows_in, gain_one, shift_one, fits)
    attn_pieces, first_along, norm_one, second_own, grad_mlp, invalid = join(
        attn_pieces, first_along, norm_one, second_own, grad_mlp, invalid
    )

    first_halves = grid.middle(first_along)
    second_along = [second_own] + grid.steps(second_own, 0, (1,))
    packed = times_pieces(norm_one, attn_pieces, 0, 3, fits)
    pairs = width_here // (2 * HEAD_DIM)
    parts = 2 if pairs % 2 == 0 else 1
    share = pairs // parts
    forward = [attend(packed, invalid, 0, share)]
    first_halves, second_along, forward, packed, attn_pieces, norm_one = join(
        first_halves, second_along, forward, packed, attn_pieces, norm_one
    )

    first_pieces = grid.finish(first_halves)
    second_along += grid.steps(second_along[0], 0, (2,))
    if parts == 2:
        forward = forward + [attend(packed, invalid, share, share)]
    mixed = [f[0] for f in forward]
    attn_out = times_pieces_turned(mixed, attn_pieces, [(3, p) for p in range(parts)], fits)
    first_pieces, second_along, attn_out = join(first_pieces, second_along, attn_out)

    second_along += grid.steps(second_along[0], 0, (3,))
    middle, norm_two = second_norm(
        rows_in, live_col, *pair.both(attn_out), proj_shift, gain_two, shift_two, fits
    )
    first_pieces, second_along, middle, norm_two = join(
        first_pieces, second_along, middle, norm_two
    )

    second_pieces = grid.finish(grid.halves_of(second_along, second_counts))
    piece_rows = grid.piece_rows()
    shifts = [fc1_shift[:, :hidden_cut], fc1_shift[:, hidden_cut:]]
    feed_a = feed_forward(
        norm_two, grad_mlp, shifts[0], first_pieces, places, piece_rows, (), fits
    )
    second_pieces, feed_a, norm_two = join(second_pieces, feed_a, norm_two)

    last_a = grid.reduce_last(feed_a[3:])
    feed_b = feed_forward(
        norm_two, grad_mlp, shifts[1], second_pieces, places, piece_rows, feed_a[:2], fits
    )
    grad_fc1_bias = jnp.concatenate([feed_a[2], feed_b[2]], axis=1)
    last_a, feed_b = join(last_a, feed_b)
    mlp_out, grad_two = feed_b[:2]

    middle_a = grid.reduce_middle(last_a)
    grad_middle, grad_branch, sums = norm_back(
        grad_mlp, live_col, *pair.both(grad_two), middle, gain_two, fits
    )
    grad_branch, pieces_b = join(grad_branch, feed_b[3:])
    last_b = grid.reduce_last(pieces_b)
    grad_mixed = times_pieces(grad_branch, attn_pieces, 3, 1, fits)
    middle_a, grad_mixed, mlp_out = join(middle_a, grad_mixed, mlp_out)

    def back(part):
        return attend_back(packed, invalid, *forward[part], grad_mixed, part * share, share)

    def grads(part, columns):
        lefts, rights = (norm_one,) * 3, tuple(columns)
        if part == 0:
            lefts, rights = lefts + (grad_branch,) * parts, rights + tuple(mixed)
        return weight_grads(lefts, rights, piece_rows, fits)

    pieces_a = grid.first_pieces(middle_a)
    first_a = grid.send_first(pieces_a, (1, 3))
    columns = back(0)
    mlp_out = pair.own_total(mlp_out)
    last_b, first_a, pieces_a, columns, grad_mixed, mlp_out = join(
        last_b, first_a, pieces_a, columns, grad_mixed, mlp_out
    )

    middle_b = grid.reduce_middle(last_b)
    first_a = pieces_a[:1] + first_a + grid.send_first(pieces_a, (2,))
    pieces_c = grads(0, columns)
    middle_b, pieces_c, grad_mixed, first_a = join(middle_b, pieces_c, grad_mixed, first_a)

    last_c = grid.reduce_last(pieces_c)
    pieces_b = grid.first_pieces(middle_b)
    first_b = grid.send_first(pieces_b, (1, 3))
    pieces_d, places_c = (), [(j, p) for p in range(parts) for j in range(3)]
    if parts == 2:
        more = back(1)
        last_c, first_b, pieces_b, more = join(last_c, first_b, pieces_b, more)
        columns = columns + more
        pieces_d = grads(1, more)

    middle_c = grid.reduce_middle(last_c)
    first_b = pieces_b[:1] + first_b + grid.send_first(pieces_b, (2,))
    grad_one = times_pieces_turned(columns, attn_pieces, places_c, fits, 2)
    middle_c, first_b, pieces_d, grad_one = join(middle_c, first_b, pieces_d, grad_one)

    last_d = grid.reduce_last(pieces_d) if parts == 2 else ()
    first_c = grid.reduce_first(middle_c)
    grad_rows, sums_one = first_norm_back(
        grad_middle if fits else pair.own(grad_middle),
        rest_grad,
        *pair.own_both(grad_one),
        own_in,
        gain_one,
        fits,
    )
    sums_one = pair.small_total(sums_one)
    last_d, sums_one, grad_rows = join(last_d, sums_one, grad_rows)

    middle_d = grid.reduce_middle(last_d) if parts == 2 else ()
    bias_grads = grad_fc1_bias.astype(BF16).reshape(dp_size, hidden_block)
    bias_grads = jnp.pad(bias_grads, ((0, 0), (0, bias_pad))).reshape(dp_size, bias_columns, block)
    bias_grads = dot_nn(bias_grads.transpose(1, 0, 2).reshape(bias_columns, width), select)
    small_grads = jnp.concatenate([sums_one, sums, bias_grads], axis=0)
    small_grads = grid.blocks_of(small_grads)
    small_grads = grid.reduce_small(small_grads, 2)
    small_grads = grid.reduce_small(small_grads, 1)
    middle_d, small_grads, first_c, grad_rows, mlp_out = join(
        middle_d, small_grads, first_c, grad_rows, mlp_out
    )

    if parts == 2:
        count, lanes = small_grads.shape[1], middle_d[0][0].shape[2]
        spare = ((0, 2), (0, 0), (0, lanes - block))
        pieces_d = [
            jnp.concatenate([p, jnp.pad(g.astype(p.dtype)[None], spare)], axis=1)
            for p, g in zip(grid.first_pieces(middle_d), small_grads)
        ]
        sum_d = grid.reduce_end(pieces_d[:1] + grid.send_first(pieces_d, (1, 2, 3)))
        sum_d, small_grads = sum_d[:, :block], sum_d[0, block:, :block]
    else:
        small_grads = grid.reduce_small(small_grads, 0)
    grad_inputs = dot_nt(grad_rows, select).astype(BF16)
    result = pair.own(middle) + own_live * (mlp_out + fc2_shift)
    outputs = dot_nt(result.astype(BF16), select).astype(BF16)
    first_a, first_b = grid.reduce_end(first_a), grid.reduce_end(first_b)
    out_fc1 = jnp.concatenate([first_a[0], first_a[1], first_b[0], first_b[1]], axis=1)
    out_fc2 = jnp.concatenate([first_a[2], first_a[3], first_b[2], first_b[3]], axis=1)
    out_c = grid.reduce_end(first_c)
    out_qkv = out_c[:3]
    if parts == 2:
        out_qkv = jnp.concatenate([out_qkv, sum_d], axis=2)
    out_proj = jnp.concatenate([out_c[3 + p] for p in range(parts)], axis=1)
    return (
        outputs,
        grad_inputs,
        small_grads[0],
        small_grads[1],
        out_qkv,
        out_proj.T,
        small_grads[4],
        small_grads[2],
        small_grads[3],
        out_fc1,
        small_grads[6:].reshape(-1)[:hidden_block],
        out_fc2.T,
        small_grads[5],
    )


def solution(mesh):
    in_specs = (
        P(("dp", "tensor"), None),
        P(("dp", "tensor"), None),
        P("dp"),
        P(("dp", "tensor")),
        P("dp"),
        P("dp"),
        P(None, "dp", "tensor"),
        P("tensor", "dp"),
        P("dp"),
        P("dp"),
        P("dp"),
        P("dp", "tensor"),
        P(("tensor", "dp")),
        P("tensor", "dp"),
        P("dp"),
    )
    out_specs = (
        P(("dp", "tensor"), None),
        P(("dp", "tensor"), None),
        P("dp"),
        P("dp"),
        P(None, "dp", "tensor"),
        P("tensor", "dp"),
        P("dp"),
        P("dp"),
        P("dp"),
        P("dp", "tensor"),
        P(("tensor", "dp")),
        P("tensor", "dp"),
        P("dp"),
    )
    return jax.shard_map(
        on_device, mesh=mesh, in_specs=in_specs, out_specs=out_specs, check_vma=False
    )
```

```python
import functools

import jax
import jax.numpy as jnp
import numpy as np
from jax import lax
from jax.experimental import pallas as pl
from jax.experimental.pallas import tpu as pltpu
from jax.sharding import PartitionSpec as P

HEAD_DIM = 64
SEQ_LEN = 1104
F32 = jnp.float32
BF16 = jnp.bfloat16
MIB = 2**20


def dp_factors(size):
    if size % 8 == 0:
        return (4, 2, size // 8)
    return (1, 1, size)


class DpGrid:
    def __init__(self, size, block):
        self.size = size
        self.block = block
        self.half = block // 2
        self.factors = dp_factors(size)
        self.routes = ((2, 1), (1, 2))

    def coords(self, index):
        _, second, third = self.factors
        return (index // (second * third), (index // third) % second, index % third)

    def index(self, coords):
        _, second, third = self.factors
        return (coords[0] * second + coords[1]) * third + coords[2]

    def ahead(self, index, axis, step):
        coords = list(self.coords(index))
        coords[axis] = (coords[axis] + step) % self.factors[axis]
        return self.index(coords)

    def fetch(self, value, axis, step):
        pairs = [(self.ahead(i, axis, step), i) for i in range(self.size)]
        return lax.ppermute(value, "dp", pairs)

    def push(self, value, axis, step):
        pairs = [(i, self.ahead(i, axis, step)) for i in range(self.size)]
        return lax.ppermute(value, "dp", pairs)

    def spread(self, shard):
        with jax.named_scope("gather_z"):
            return [shard] + [self.fetch(shard, 0, s) for s in range(1, self.factors[0])]

    def middle(self, along):
        halves = []
        for part, (middle, _) in enumerate(self.routes):
            rows = slice(part * self.half, (part + 1) * self.half)
            value = jnp.concatenate([a[..., rows, :] for a in along], axis=-2)
            steps = range(1, self.factors[middle])
            with jax.named_scope("gather_middle"):
                halves.append([value] + [self.fetch(value, middle, s) for s in steps])
        return halves

    def finish(self, halves):
        pieces = []
        for (_, last), parts in zip(self.routes, halves):
            value = jnp.concatenate(parts, axis=-2)
            pieces.append(value)
            with jax.named_scope("gather_last"):
                pieces.extend(self.fetch(value, last, s) for s in range(1, self.factors[last]))
        return pieces

    def gather(self, shard):
        return self.finish(self.middle(self.spread(shard)))

    def spread_middle(self, shard):
        parts = []
        for part, (middle, _) in enumerate(self.routes):
            value = shard[..., part * self.half : (part + 1) * self.half, :]
            with jax.named_scope("gather_middle"):
                steps = range(1, self.factors[middle])
                parts.append([value] + [self.fetch(value, middle, s) for s in steps])
        return parts

    def steps(self, value, axis, steps):
        with jax.named_scope("gather_step"):
            return [self.fetch(value, axis, s) for s in steps if s < self.factors[axis]]

    def halves_of(self, along, counts):
        halves, start = [], 0
        for count in counts:
            rows = slice(start, start + count * self.half)
            start += count * self.half
            value = jnp.stack([a[..., rows, :] for a in along], axis=-3)
            lead, wide = value.shape[:-3], value.shape[-1]
            value = value.reshape(lead + (self.factors[0], count, self.half, wide))
            value = jnp.swapaxes(value, -4, -3)
            halves.append([value.reshape(lead + (-1, wide))])
        return halves

    def reduce_last(self, pieces):
        pieces, halves = list(pieces), []
        for _, last in self.routes:
            mine, pieces = pieces[: self.factors[last]], pieces[self.factors[last] :]
            with jax.named_scope("reduce_last"):
                sent = [self.push(mine[s], last, s) for s in range(1, self.factors[last])]
            halves.append([mine[0]] + sent)
        return halves

    def reduce_middle(self, halves):
        rows, out = self.factors[0] * self.half, []
        for (middle, _), parts in zip(self.routes, halves):
            cut = [
                sum(p[..., s * rows : (s + 1) * rows, :].astype(F32) for p in parts).astype(BF16)
                for s in range(self.factors[middle])
            ]
            with jax.named_scope("reduce_middle"):
                sent = [self.push(cut[s], middle, s) for s in range(1, self.factors[middle])]
            out.append([cut[0]] + sent)
        return out

    def first_pieces(self, halves):
        def along(step):
            rows = slice(step * self.half, (step + 1) * self.half)
            totals = [sum(p[..., rows, :].astype(F32) for p in parts) for parts in halves]
            return jnp.concatenate(totals, axis=-2)

        return [along(0)] + [along(s).astype(BF16) for s in range(1, self.factors[0])]

    def send_first(self, pieces, steps):
        with jax.named_scope("reduce_z"):
            return [self.push(pieces[s], 0, s) for s in steps if s < len(pieces)]

    def reduce_first(self, halves):
        pieces = self.first_pieces(halves)
        return pieces[:1] + self.send_first(pieces, (1, 2, 3))

    def reduce_end(self, parts):
        return sum(p.astype(F32) for p in parts)

    def scatter(self, pieces):
        return self.reduce_end(self.reduce_first(self.reduce_middle(self.reduce_last(pieces))))

    def gather_small(self, value, axes):
        for axis in axes:
            with jax.named_scope("gather_small"):
                parts = [value] + [self.fetch(value, axis, s) for s in range(1, self.factors[axis])]
            value = jnp.concatenate(parts, axis=0)
        return value

    def small_in_order(self, value):
        zeroth, second, third = self.factors
        value = value.reshape((third, second, zeroth, value.shape[1], 2, self.half))
        first_half = value[..., 0, :].transpose(3, 1, 0, 2, 4)
        second_half = value[..., 1, :].transpose(3, 0, 1, 2, 4)
        count = value.shape[3]
        return jnp.concatenate(
            [first_half.reshape(count, -1), second_half.reshape(count, -1)], axis=1
        )

    def blocks_of(self, value):
        count, full = value.shape
        second, third = self.factors[1], self.factors[2]
        first_half = value[:, : full // 2].reshape(count, second, third, self.factors[0], self.half)
        second_half = value[:, full // 2 :].reshape(count, third, second, self.factors[0], self.half)
        return jnp.concatenate(
            [first_half.transpose(2, 1, 3, 0, 4), second_half.transpose(1, 2, 3, 0, 4)], axis=-1
        )

    def reduce_small(self, value, axis):
        value = value.astype(BF16)
        total = value[0].astype(F32)
        with jax.named_scope("reduce_small"):
            for step in range(1, self.factors[axis]):
                total = total + self.push(value[step], axis, step).astype(F32)
        return total

    def piece_rows(self):
        full = self.size * self.half
        rows = []
        for _, last in self.routes:
            rows.extend([full // self.factors[last]] * self.factors[last])
        return rows

    def cut(self, value, axis=0):
        edges = np.cumsum(self.piece_rows())[:-1].tolist()
        return jnp.split(value, edges, axis=axis)

    def places(self):
        return (self.features()[:: self.half] // self.half).astype(jnp.int32)

    def features(self):
        here = self.coords(lax.axis_index("dp"))
        indices = []
        for part, (middle, last) in enumerate(self.routes):
            shape = (self.factors[last], self.factors[middle], self.factors[0], self.half)
            steps = [None, None, None]
            steps[last], steps[middle], steps[0], sub = (
                jnp.asarray(g.reshape(-1), jnp.int32) for g in np.indices(shape)
            )
            coords = [(h + s) % f for h, s, f in zip(here, steps, self.factors)]
            indices.append(self.index(coords) * self.block + part * self.half + sub)
        return jnp.concatenate(indices)


class TensorPair:
    def __init__(self, size, slot_count, local_rows):
        self.size = size
        self.relative = size == 2 and slot_count == 1
        self.local_rows = local_rows

    def swap(self, value):
        return lax.ppermute(value, "tensor", [(0, 1), (1, 0)])

    def parts(self, value):
        if self.relative:
            return [value, self.swap(value)]
        return [lax.all_gather(value, "tensor", axis=0, tiled=True)]

    def whole(self, value):
        return jnp.concatenate(self.parts(value), axis=0)

    def own(self, value):
        if self.relative:
            return value[: self.local_rows]
        start = lax.axis_index("tensor") * self.local_rows
        return lax.dynamic_slice_in_dim(value, start, self.local_rows, axis=0)

    def both(self, value):
        if self.relative:
            return value, self.swap(value)
        return lax.psum(value.astype(F32), "tensor"), jnp.zeros((1, value.shape[1]), F32)

    def own_total(self, value):
        if self.relative:
            kept = value[: self.local_rows].astype(F32)
            return kept + self.swap(value[self.local_rows :]).astype(F32)
        return lax.psum_scatter(value, "tensor", scatter_dimension=0, tiled=True).astype(F32)

    def own_both(self, halves):
        if self.relative:
            return halves[0], self.swap(halves[1])
        value = jnp.concatenate(halves, axis=0)
        total = lax.psum_scatter(value, "tensor", scatter_dimension=0, tiled=True)
        return total, jnp.zeros((1, value.shape[1]), F32)

    def small_total(self, value):
        if self.size == 2:
            return value + self.swap(value)
        return lax.psum(value, "tensor")


def join(*groups):
    flat, tree = jax.tree.flatten(groups)
    return jax.tree.unflatten(tree, lax.optimization_barrier(tuple(flat)))


def normalize(values):
    row_mean = jnp.mean(values, axis=-1, keepdims=True)
    centered = values - row_mean
    variance = jnp.mean(centered * centered, axis=-1, keepdims=True)
    inverse = lax.rsqrt(variance + 1e-05)
    return centered * inverse, inverse


def norm_input_grad(grad, gain, normed, inverse):
    scaled = grad * gain
    first = jnp.mean(scaled, axis=-1, keepdims=True)
    second = jnp.mean(scaled * normed, axis=-1, keepdims=True)
    return inverse * (scaled - first - normed * second)


def dot_nn(left, right):
    return lax.dot_general(left, right, (((1,), (0,)), ((), ())), preferred_element_type=F32)


def dot_nt(left, right):
    return lax.dot_general(left, right, (((1,), (1,)), ((), ())), preferred_element_type=F32)


def dot_tn(left, right):
    return lax.dot_general(left, right, (((0,), (0,)), ((), ())), preferred_element_type=F32)


def gelu_and_slope(values):
    cdf = 0.5 + 0.5 * lax.erf(values * (0.5**0.5))
    density = jnp.exp(-0.5 * values * values) * 0.3989422804014327
    return values * cdf, cdf + values * density


def params(limit):
    return pltpu.CompilerParams(vmem_limit_bytes=limit * MIB)


def cost(micros):
    return pl.CostEstimate(
        flops=int(micros * 1e9), transcendentals=0, bytes_accessed=int(micros * 1e6)
    )


def whole_spec(array):
    return pl.BlockSpec(array.shape, lambda *grid: (0,) * len(array.shape))


def stack_rows(refs):
    return jnp.concatenate([r[...] for r in refs], axis=0)


def head_lanes(seq, head):
    lane = lax.broadcasted_iota(jnp.int32, (seq, 2 * HEAD_DIM), 1)
    mine = (lane >= HEAD_DIM) if head else (lane < HEAD_DIM)
    return mine, lane == (0 if head else HEAD_DIM)


def head_operands(query_ref, key_ref, invalid, head):
    seq = query_ref.shape[0]
    mine, extra = head_lanes(seq, head)
    one, zero = jnp.asarray(1, BF16), jnp.asarray(0, BF16)
    scaled = query_ref[...] * jnp.asarray(HEAD_DIM**-0.5, BF16)
    query = jnp.where(mine, scaled, jnp.where(extra, one, zero))
    keys = jnp.where(mine, key_ref[...], jnp.where(extra, invalid, zero))
    return query, keys


def key_column(invalid_ref):
    seq = invalid_ref.shape[-1]
    return jnp.broadcast_to(invalid_ref[0], (2 * HEAD_DIM, seq)).T.astype(BF16)


def attend_kernel(query_ref, key_ref, value_ref, invalid_ref, mixed_ref, total_ref, turned_ref):
    seq = query_ref.shape[0]
    invalid = key_column(invalid_ref)
    values = value_ref[...].T
    for head in range(2):
        rows = slice(head * HEAD_DIM, (head + 1) * HEAD_DIM)
        query, keys = head_operands(query_ref, key_ref, invalid, head)
        with_ones = jnp.concatenate([values[rows], jnp.ones((16, seq), BF16)], axis=0)
        scores = dot_nt(keys, query)
        largest = jnp.max(scores, axis=0, keepdims=True)
        weights = jnp.exp(scores - largest)
        mixed = dot_nn(with_ones, weights.astype(BF16))
        weight_sum = mixed[HEAD_DIM : HEAD_DIM + 1]
        turned_ref[rows] = mixed[:HEAD_DIM] * (1.0 / weight_sum)
        total_ref[0, 0, head : head + 1] = largest + jnp.log(weight_sum)
    mixed_ref[...] = turned_ref[...].T.astype(BF16)


def attend_back_kernel(
    query_ref,
    key_ref,
    value_ref,
    invalid_ref,
    mixed_ref,
    total_ref,
    grad_ref,
    grad_query_ref,
    grad_key_ref,
    grad_value_ref,
    turned_ref,
    prob_ref,
    score_ref,
):
    seq = query_ref.shape[0]
    invalid = key_column(invalid_ref)
    keys_turned = key_ref[...].T
    product = mixed_ref[...].astype(F32).T * grad_ref[...].astype(F32).T
    for head in range(2):
        rows = slice(head * HEAD_DIM, (head + 1) * HEAD_DIM)
        mine, _ = head_lanes(seq, head)
        query, keys = head_operands(query_ref, key_ref, invalid, head)
        grad = jnp.where(mine, grad_ref[...], jnp.asarray(0, BF16))
        row_dot = jnp.sum(product[rows], axis=0, keepdims=True)
        for start in range(0, seq, 256):
            cut = slice(start, min(start + 256, seq))
            prob = jnp.exp(dot_nt(keys, query[cut]) - total_ref[0, 0, head : head + 1, cut])
            grad_prob = dot_nt(value_ref[...], grad[cut]) - row_dot[:, cut]
            grad_score = (prob * grad_prob).astype(BF16)
            prob_ref[:, cut] = prob.astype(BF16)
            score_ref[:, cut] = grad_score
            turned_ref[rows, cut] = dot_nn(keys_turned[rows], grad_score) * HEAD_DIM**-0.5
        grad_value = dot_nn(prob_ref[...], grad)
        grad_key = dot_nn(score_ref[...], jnp.where(mine, query, jnp.asarray(0, BF16)))
        if head == 0:
            first_value, first_key = grad_value, grad_key
    grad_value_ref[...] = (first_value + grad_value).astype(BF16)
    grad_key_ref[...] = (first_key + grad_key).astype(BF16)
    grad_query_ref[...] = turned_ref[...].T.astype(BF16)


def attend_specs():
    def columns(offset):
        return pl.BlockSpec((SEQ_LEN, 2 * HEAD_DIM), lambda s, p: (s, p + offset))

    invalid = pl.BlockSpec((1, 1, SEQ_LEN), lambda s, p: (s, 0, 0))
    total = pl.BlockSpec((1, 1, 2, SEQ_LEN), lambda s, p: (s, p, 0, 0))
    return columns, invalid, total


def attend(packed, invalid, first, count):
    slots, pairs = invalid.shape[0], packed.shape[1] // (6 * HEAD_DIM)
    columns, invalid_spec, total_spec = attend_specs()
    return pl.pallas_call(
        attend_kernel,
        grid=(slots, count),
        in_specs=[columns(first), columns(pairs + first), columns(2 * pairs + first), invalid_spec],
        out_specs=[columns(0), total_spec],
        out_shape=[
            jax.ShapeDtypeStruct((packed.shape[0], count * 2 * HEAD_DIM), BF16),
            jax.ShapeDtypeStruct((slots, count, 2, SEQ_LEN), F32),
        ],
        scratch_shapes=[pltpu.VMEM((2 * HEAD_DIM, SEQ_LEN), F32)],
        compiler_params=params(14),
        cost_estimate=cost(4 * slots * count),
        name="attend",
    )(packed, packed, packed, invalid)


def attend_back(packed, invalid, mixed, total, grad_mixed, first, count):
    slots, pairs = invalid.shape[0], packed.shape[1] // (6 * HEAD_DIM)
    columns, invalid_spec, _ = attend_specs()
    return pl.pallas_call(
        attend_back_kernel,
        grid=(slots, count),
        in_specs=[
            columns(first),
            columns(pairs + first),
            columns(2 * pairs + first),
            invalid_spec,
            columns(first),
            pl.BlockSpec((1, 1, 2, SEQ_LEN), lambda s, p: (s, p + first, 0, 0)),
            columns(first),
        ],
        out_specs=[columns(0)] * 3,
        out_shape=[jax.ShapeDtypeStruct((mixed.shape[0], count * 2 * HEAD_DIM), BF16)] * 3,
        scratch_shapes=[
            pltpu.VMEM((2 * HEAD_DIM, SEQ_LEN), F32),
            pltpu.VMEM((SEQ_LEN, SEQ_LEN), BF16),
            pltpu.VMEM((SEQ_LEN, SEQ_LEN), BF16),
        ],
        compiler_params=params(22),
        cost_estimate=cost(9 * slots * count),
        name="attend_back",
    )(packed, packed, packed, invalid, mixed, total, grad_mixed)


def joined(pieces, first, count):
    return jnp.concatenate(
        [jnp.concatenate([p[g] for p in pieces], axis=0) for g in range(first, first + count)],
        axis=1,
    )


def times_pieces(rows, pieces, first, count, fits):
    if not fits:
        return dot_nn(rows, joined(pieces, first, count)).astype(BF16)
    wide = pieces[0].shape[2]

    def kernel(rows_ref, *refs):
        weight = jnp.concatenate([r[0] for r in refs[:-1]], axis=0)
        refs[-1][...] = dot_nn(rows_ref[...], weight).astype(BF16)

    return pl.pallas_call(
        kernel,
        grid=(count,),
        in_specs=[whole_spec(rows)]
        + [pl.BlockSpec((1, p.shape[1], wide), lambda j: (first + j, 0, 0)) for p in pieces],
        out_specs=pl.BlockSpec((rows.shape[0], wide), lambda j: (0, j)),
        out_shape=jax.ShapeDtypeStruct((rows.shape[0], count * wide), BF16),
        compiler_params=params(12),
        cost_estimate=cost(2 * count),
        name="times_pieces",
    )(rows, *pieces)


def times_pieces_turned(columns, pieces, places, fits, cuts=1):
    count = len(columns)
    rows, wide = columns[0].shape
    if not fits:
        weight = [joined(pieces, g, 1)[:, c * wide : (c + 1) * wide] for g, c in places]
        total = dot_nt(jnp.concatenate(columns, axis=1), jnp.concatenate(weight, axis=1))
        return jnp.split(total.astype(BF16), cuts) if cuts > 1 else total.astype(BF16)
    starts = np.cumsum([0] + [p.shape[1] for p in pieces]).tolist()

    def kernel(*refs):
        lefts, weights, out_refs = refs[:count], refs[count:-cuts], refs[-cuts:]
        left = jnp.concatenate([r[...] for r in lefts], axis=1)
        weight = jnp.concatenate(
            [
                jnp.concatenate([r[0] for r in weights[i * count : (i + 1) * count]], axis=1)
                for i in range(len(pieces))
            ],
            axis=0,
        )
        for k, out_ref in enumerate(out_refs):
            cut = slice(k * rows // cuts, (k + 1) * rows // cuts)
            out_ref[...] = dot_nt(left[cut], weight).astype(BF16)

    def place_spec(piece, group, column):
        return pl.BlockSpec((1, piece.shape[1], wide), lambda i: (group, 0, column))

    outs = pl.pallas_call(
        kernel,
        grid=(1,),
        in_specs=[whole_spec(c) for c in columns] + [place_spec(p, *q) for p in pieces for q in places],
        out_specs=[pl.BlockSpec((rows // cuts, starts[-1]), lambda i: (0, 0))] * cuts,
        out_shape=[jax.ShapeDtypeStruct((rows // cuts, starts[-1]), BF16)] * cuts,
        compiler_params=params(16),
        cost_estimate=cost(1 + count),
        name="times_pieces_turned",
    )(*columns, *[p for p in pieces for _ in places])
    return outs if cuts > 1 else outs[0]


def weight_grads(lefts, rights, piece_rows, fits):
    wide = rights[0].shape[1]
    rights = [r if isinstance(r, tuple) else (r, 0) for r in rights]
    starts = np.cumsum([0] + piece_rows).tolist()
    if not fits:
        blocks = [a[:, c * wide : (c + 1) * wide] for a, c in rights]
        full = jnp.stack([dot_tn(a, b).astype(BF16) for a, b in zip(lefts, blocks)])
        return [full[:, s:e] for s, e in zip(starts, starts[1:])]
    count = len(rights)
    names = []
    for left in lefts:
        if not any(left is other for other in names):
            names.append(left)
    which = [next(i for i, o in enumerate(names) if o is left) for left in lefts]

    def kernel(*refs):
        left_refs, right_refs = refs[: len(names)], refs[len(names) : len(names) + count]
        out_refs = refs[len(names) + count :]
        turned = [r[...].T for r in left_refs]
        for k in range(count):
            product = dot_nn(turned[which[k]], right_refs[k][...]).astype(BF16)
            for i, (start, end) in enumerate(zip(starts, starts[1:])):
                out_refs[i][k] = product[start:end]

    return pl.pallas_call(
        kernel,
        grid=(1,),
        in_specs=[whole_spec(a) for a in names]
        + [pl.BlockSpec((a.shape[0], wide), lambda i, c=c: (0, c)) for a, c in rights],
        out_specs=[pl.BlockSpec((count, r, wide), lambda i: (0, 0, 0)) for r in piece_rows],
        out_shape=[jax.ShapeDtypeStruct((count, r, wide), BF16) for r in piece_rows],
        compiler_params=params(20),
        cost_estimate=cost(1 + 1.5 * count),
        name="weight_grads",
    )(*names, *[a for a, _ in rights])


def joined_rows(parts):
    return parts[0] if len(parts) == 1 else jnp.concatenate(parts, axis=0)


def first_norm(rows_in, gain, bias, fits):
    width = rows_in[0].shape[1]
    rows = sum(p.shape[0] for p in rows_in)

    def work(values, gain, bias):
        normed, _ = normalize(values.astype(F32))
        return (normed * gain + bias).astype(BF16)

    if not fits:
        return work(joined_rows(rows_in), gain, bias)

    def kernel(*refs):
        gain, bias, out_ref = refs[-3][...], refs[-2][...], refs[-1]
        start = 0
        for ref in refs[:-3]:
            out_ref[start : start + ref.shape[0]] = work(ref[...], gain, bias)
            start += ref.shape[0]

    return pl.pallas_call(
        kernel,
        out_shape=jax.ShapeDtypeStruct((rows, width), BF16),
        compiler_params=params(12),
        cost_estimate=cost(3),
        name="first_norm",
    )(*rows_in, gain, bias)


def second_norm(rows_in, live, mine, other, shift, gain, bias, fits):
    rows, width = mine.shape

    def work(rows_in, live, mine, other, shift, gain, bias):
        branch = mine.astype(F32) + other.astype(F32) + shift
        middle = rows_in.astype(F32) + live * branch
        normed, _ = normalize(middle)
        return middle, (normed * gain + bias).astype(BF16)

    if not fits:
        return work(joined_rows(rows_in), live, mine, other, shift, gain, bias)
    half = rows // 2

    def kernel(own_ref, next_ref, *refs):
        rows_in = jnp.where(pl.program_id(0) == 0, own_ref[...], next_ref[...])
        refs[-2][...], refs[-1][...] = work(rows_in, *[r[...] for r in refs[:-2]])

    def block(columns, place=lambda i: i):
        return pl.BlockSpec((half, columns), lambda i: (place(i), 0))

    return pl.pallas_call(
        kernel,
        grid=(2,),
        in_specs=[
            block(width, lambda i: 0),
            block(width, lambda i: 0),
            block(1),
            block(width),
            block(width, lambda i: 1 - i),
        ]
        + [whole_spec(shift)] * 3,
        out_specs=[block(width), block(width)],
        out_shape=[
            pltpu.HBM((rows, width), F32),
            jax.ShapeDtypeStruct((rows, width), BF16),
        ],
        compiler_params=params(40),
        cost_estimate=cost(4),
        name="second_norm",
    )(*rows_in, live, mine, other, shift, gain, bias)


def norm_back(grad_out, live, mine, other, middle, gain, fits):
    rows, width = middle.shape

    def work(grad_out, live, mine, other, middle, gain):
        grad_out = grad_out.astype(F32)
        grad = mine.astype(F32) + other.astype(F32)
        normed, inverse = normalize(middle)
        grad_middle = grad_out + norm_input_grad(grad, gain, normed, inverse)
        grad_branch = (live * grad_middle).astype(BF16)
        sums = [grad * normed, grad, grad_branch.astype(F32), grad_out]
        sums = jnp.concatenate([jnp.sum(s, axis=0, keepdims=True) for s in sums], axis=0)
        return grad_middle, grad_branch, sums

    if not fits:
        return work(joined_rows(grad_out), live, mine, other, middle, gain)
    half = rows // 2

    def kernel(own_ref, next_ref, live_ref, mine_ref, other_ref, middle_ref, gain_ref, *refs):
        step = pl.program_id(0)
        grad = jnp.where(step == 0, own_ref[...], next_ref[...])
        rest = [r[...] for r in (live_ref, mine_ref, other_ref, middle_ref, gain_ref)]
        grad_middle, refs[1][...], sums = work(grad, *rest)

        @pl.when(step == 0)
        def _():
            refs[0][...] = grad_middle
            refs[2][...] = sums

        @pl.when(step == 1)
        def _():
            refs[2][...] += sums

    def block(columns, place=lambda i: i):
        return pl.BlockSpec((half, columns), lambda i: (place(i), 0))

    return pl.pallas_call(
        kernel,
        grid=(2,),
        in_specs=[
            block(width, lambda i: 0),
            block(width, lambda i: 0),
            block(1),
            block(width),
            block(width, lambda i: 1 - i),
            block(width),
            whole_spec(gain),
        ],
        out_specs=[
            block(width, lambda i: 0),
            block(width),
            pl.BlockSpec((4, width), lambda i: (0, 0)),
        ],
        out_shape=[
            jax.ShapeDtypeStruct((half, width), F32),
            jax.ShapeDtypeStruct((rows, width), BF16),
            jax.ShapeDtypeStruct((4, width), F32),
        ],
        compiler_params=params(44),
        cost_estimate=cost(7),
        name="norm_back",
    )(*grad_out, live, mine, other, middle, gain)


def first_norm_back(grad_middle, rest, mine, other, rows_in, gain, fits):
    rows, width = rows_in.shape

    def work(grad_middle, rest, mine, other, rows_in, gain):
        grad = mine.astype(F32) + other.astype(F32)
        normed, inverse = normalize(rows_in.astype(F32))
        grad_rows = grad_middle + rest.astype(F32) + norm_input_grad(grad, gain, normed, inverse)
        sums = [jnp.sum(s, axis=0, keepdims=True) for s in (grad * normed, grad)]
        return grad_rows.astype(BF16), jnp.concatenate(sums, axis=0)

    if not fits:
        return work(grad_middle, rest, mine, other, rows_in, gain)

    def kernel(*refs):
        refs[-2][...], refs[-1][...] = work(*[r[...] for r in refs[:-2]])

    own = pl.BlockSpec((rows, width), lambda i: (0, 0))
    return pl.pallas_call(
        kernel,
        grid=(1,),
        in_specs=[own] * 5 + [pl.BlockSpec((1, width), lambda i: (0, 0))],
        out_specs=[own, pl.BlockSpec((2, width), lambda i: (0, 0))],
        out_shape=[
            jax.ShapeDtypeStruct((rows, width), BF16),
            jax.ShapeDtypeStruct((2, width), F32),
        ],
        compiler_params=params(14),
        cost_estimate=cost(4),
        name="first_norm_back",
    )(grad_middle, rest, mine, other, rows_in, gain)


def feed_kernel(counts, carried, plain, scattered, places_ref, *refs):
    halves, pieces, grad_pieces = counts
    normed_ref, shift_ref, grad_refs = refs[0], refs[1], refs[2 : 2 + halves]
    refs = refs[2 + halves :]
    first_refs, second_refs, refs = refs[:pieces], refs[pieces : 2 * pieces], refs[2 * pieces :]
    before, refs = (refs[:2], refs[2:]) if carried else ((), refs)
    out_ref, grad_two_ref, shift_grad_ref = refs[:3]
    weight_grad_refs = refs[3 : 3 + grad_pieces]
    grad_ref, normed_turned, grad_turned, out_sum, grad_sum = refs[3 + grad_pieces :]
    step = pl.program_id(0)
    blocks = places_ref.shape[0]
    size = normed_ref.shape[1] // blocks

    def place(i):
        return pl.ds(pl.multiple_of(places_ref[i] * size, size), size)

    @pl.when(step == 0)
    def _():
        start = 0
        for ref in grad_refs:
            grad_ref[start : start + ref.shape[0]] = ref[...]
            start += ref.shape[0]
        if scattered:
            for i in range(blocks):
                rows = slice(i * size, (i + 1) * size)
                normed_turned[place(i)] = normed_ref[:, rows].T
                grad_turned[place(i)] = grad_ref[:, rows].T
        else:
            normed_turned[...] = normed_ref[...].T
            grad_turned[...] = grad_ref[...].T

    if plain:
        first = jnp.concatenate([first_refs[0][place(i)] for i in range(blocks)], axis=0)
        second = jnp.concatenate([second_refs[0][place(i)] for i in range(blocks)], axis=0)
    else:
        first = jnp.concatenate([w[0] for w in first_refs], axis=0)
        second = jnp.concatenate([w[0] for w in second_refs], axis=0)
    hidden = dot_nn(normed_ref[...], first) + shift_ref[...]
    hidden_act, slope = gelu_and_slope(hidden)
    hidden_act = hidden_act.astype(BF16)
    grad_pre = (dot_nn(grad_ref[...], second) * slope).astype(BF16)
    shift_grad_ref[...] = jnp.sum(grad_pre.astype(F32), axis=0, keepdims=True)
    last = pl.num_programs(0) - 1
    products = (
        (out_sum, out_ref, hidden_act, second, before[:1]),
        (grad_sum, grad_two_ref, grad_pre, first, before[1:]),
    )

    @pl.when(step == 0)
    def _():
        for sum_ref, _, left, right, start in products:
            product = dot_nt(left, right)
            sum_ref[...] = product + start[0][...].astype(F32) if carried else product

    @pl.when(step == last)
    def _():
        for sum_ref, end_ref, left, right, _ in products:
            end_ref[...] = (sum_ref[...] + dot_nt(left, right)).astype(BF16)

    if scattered:
        weight_grad_refs[0][...] = dot_nn(normed_turned[...], grad_pre).astype(BF16)
        weight_grad_refs[1][...] = dot_nn(grad_turned[...], hidden_act).astype(BF16)
    else:
        for k, (left, right) in enumerate(
            ((normed_turned, grad_pre), (grad_turned, hidden_act))
        ):
            product, start = dot_nn(left[...], right).astype(BF16), 0
            for ref in weight_grad_refs:
                ref[k, 0] = product[start : start + ref.shape[2]]
                start += ref.shape[2]


def feed_forward(normed, grads, shift, weight, places, piece_rows, before, fits):
    rows, width = normed.shape
    plain, scattered = not isinstance(weight, list), piece_rows is None
    units = shift.shape[1]
    wide = units if plain else weight[0].shape[2]
    groups = units // wide
    if not fits:
        size = width // places.shape[0]
        order = (places[:, None] * size + jnp.arange(size)[None, :]).reshape(-1)
        if plain:
            both = jnp.take(weight, order, axis=0)
            first_w, second_w = both[:, :units], both[:, units:]
        else:
            first_w, second_w = joined(weight, 0, groups), joined(weight, groups, groups)
        grad = jnp.concatenate(grads, axis=0)
        hidden_act, slope = gelu_and_slope(dot_nn(normed, first_w) + shift)
        hidden_act = hidden_act.astype(BF16)
        grad_pre = (dot_nn(grad, second_w) * slope).astype(BF16)
        out, grad_two = dot_nt(hidden_act, second_w), dot_nt(grad_pre, first_w)
        if before:
            out, grad_two = out + before[0].astype(F32), grad_two + before[1].astype(F32)
        outs = [dot_tn(normed, grad_pre).astype(BF16), dot_tn(grad, hidden_act).astype(BF16)]
        if scattered:
            outs = [jnp.zeros_like(g).at[order].set(g) for g in outs]
        else:
            size = units // 2
            outs = jnp.stack([g[:, k * size : (k + 1) * size] for g in outs for k in range(2)])
            outs = jnp.split(outs, np.cumsum(piece_rows)[:-1].tolist(), 1)
        shift_grad = jnp.sum(grad_pre, axis=0, dtype=F32, keepdims=True)
        return [out.astype(BF16), grad_two.astype(BF16), shift_grad] + outs

    tile = units // 2
    per = wide // tile
    pieces = [weight] if plain else weight

    def once(array):
        return pl.BlockSpec(
            array.shape, lambda j, p: (0,) * len(array.shape), pipeline_mode=pl.Buffered(1)
        )

    def weight_spec(piece, second):
        if plain:
            return pl.BlockSpec((width, tile), lambda j, p: (0, second * per + j))
        return pl.BlockSpec(
            (1, piece.shape[1], tile), lambda j, p: (second * groups + j // per, 0, j % per)
        )

    if scattered:
        grad_specs = [pl.BlockSpec((width, tile), lambda j, p: (0, j))] * 2
        grad_shapes = [jax.ShapeDtypeStruct((width, units), BF16)] * 2
    else:
        half = units // 2
        split = half // tile
        grad_specs = [
            pl.BlockSpec((2, 1, r, tile), lambda j, p: (0, j // split, 0, j % split))
            for r in piece_rows
        ]
        grad_shapes = [pltpu.HBM((2, 2, r, half), BF16) for r in piece_rows]
    before = tuple(before)
    outs = pl.pallas_call(
        functools.partial(
            feed_kernel,
            (len(grads), len(pieces), len(grad_shapes)),
            bool(before),
            plain,
            scattered,
        ),
        grid_spec=pltpu.PrefetchScalarGridSpec(
            num_scalar_prefetch=1,
            grid=(units // tile,),
            in_specs=[once(normed), pl.BlockSpec((1, tile), lambda j, p: (0, j))]
            + [once(g) for g in grads]
            + [weight_spec(p, 0) for p in pieces]
            + [weight_spec(p, 1) for p in pieces]
            + [once(b) for b in before],
            out_specs=[
                pl.BlockSpec((rows, width), lambda j, p: (0, 0)),
                pl.BlockSpec((rows, width), lambda j, p: (0, 0)),
                pl.BlockSpec((1, tile), lambda j, p: (0, j)),
            ]
            + grad_specs,
            scratch_shapes=[
                pltpu.VMEM((rows, width), BF16),
                pltpu.VMEM((width, rows), BF16),
                pltpu.VMEM((width, rows), BF16),
                pltpu.VMEM((rows, width), F32),
                pltpu.VMEM((rows, width), F32),
            ],
        ),
        out_shape=[
            jax.ShapeDtypeStruct((rows, width), BF16),
            jax.ShapeDtypeStruct((rows, width), BF16),
            jax.ShapeDtypeStruct((1, units), F32),
        ]
        + grad_shapes,
        compiler_params=params(44),
        cost_estimate=cost(25),
        name="feed_forward",
    )(places, normed, shift, *grads, *pieces, *pieces, *before)
    outs = list(outs)
    if not scattered:
        outs[3:] = [g.reshape((4,) + g.shape[2:]) for g in outs[3:]]
    return outs


def on_device(
    inputs,
    cotangent,
    slot_live,
    token_type,
    attn_norm_gain,
    attn_norm_bias,
    qkv_weight,
    proj_weight,
    proj_bias,
    mlp_norm_gain,
    mlp_norm_bias,
    fc1_weight,
    fc1_bias,
    fc2_weight,
    fc2_bias,
):
    dp_size = lax.axis_size("dp")
    tensor_size = lax.axis_size("tensor")
    local_rows, width = inputs.shape
    slot_count = slot_live.shape[0]
    whole_rows = local_rows * tensor_size
    block = fc1_weight.shape[0]
    width_here = qkv_weight.shape[2]
    hidden_here = fc1_weight.shape[1]
    hidden_block = fc1_bias.shape[0]
    hidden_cut = hidden_here // 2
    fits = whole_rows <= 2048
    grid = DpGrid(dp_size, block)
    pair = TensorPair(tensor_size, slot_count, local_rows)
    half_cut = hidden_cut // 2

    bias_columns = -(-hidden_block // block)
    bias_pad = bias_columns * block - hidden_block
    smalls = jnp.stack(
        (attn_norm_gain, attn_norm_bias, proj_bias, mlp_norm_gain, mlp_norm_bias, fc2_bias)
    )
    bias_block = jnp.pad(fc1_bias, (0, bias_pad)).reshape(bias_columns, block)
    smalls = jnp.concatenate([smalls, bias_block], axis=0)
    fc2_turned = fc2_weight.T
    cuts = slice(0, hidden_cut), slice(hidden_cut, hidden_here)
    groups = [
        w[:, start : start + half_cut]
        for w in (fc1_weight, fc2_turned)
        for start in (0, half_cut)
    ]
    first_shard = jnp.stack(groups)
    second_shard = jnp.stack(
        [
            w[:, start : start + half_cut]
            for w in (fc1_weight, fc2_turned)
            for start in (hidden_cut, hidden_cut + half_cut)
        ]
    )
    attn_shard = jnp.concatenate([qkv_weight, proj_weight.T[None]], axis=0)
    count = smalls.shape[0]
    spare = ((0, 3), (0, 0), (0, width_here - block))
    attn_shard = jnp.concatenate([attn_shard, jnp.pad(smalls[None], spare)], axis=1)

    attn_along = grid.spread(attn_shard)
    smalls = jnp.stack([a[0, block:, :block] for a in attn_along])
    second_parts = grid.spread_middle(second_shard)
    attn_along, smalls, second_parts, first_shard, inputs, cotangent = join(
        attn_along, smalls, second_parts, first_shard, inputs, cotangent
    )

    attn_halves = grid.middle(attn_along)
    smalls = grid.gather_small(smalls, (1, 2))
    second_own = jnp.concatenate(second_parts[0] + second_parts[1], axis=-2)
    second_counts = [len(p) for p in second_parts]
    features, places = grid.features(), grid.places()
    select = (jnp.arange(width, dtype=jnp.int32)[:, None] == features[None, :]).astype(BF16)
    own_in = dot_nn(inputs, select).astype(BF16)
    own_in, first_shard = join(own_in, first_shard)
    first_along = [first_shard] + grid.steps(first_shard, 0, (1,))
    rows_in = pair.parts(own_in)
    own_grad = dot_nn(cotangent, select)
    live_col = jnp.repeat(slot_live.astype(F32), SEQ_LEN)[:, None]
    own_live = pair.own(live_col)
    grad_mlp = pair.parts((own_live * own_grad).astype(BF16))
    rest_grad = ((1.0 - own_live) * own_grad).astype(BF16)
    valid_whole = pair.whole((token_type != 3).astype(F32))
    invalid = jnp.where(valid_whole > 0, 0.0, -1e30).reshape(slot_count, 1, SEQ_LEN)
    attn_halves, first_along, second_own, smalls = join(
        attn_halves, first_along, second_own, smalls
    )

    attn_pieces = grid.finish(attn_halves)
    first_along += grid.steps(first_along[0], 0, (2, 3))
    smalls = grid.small_in_order(smalls)
    gain_one, shift_one, proj_shift, gain_two, shift_two, fc2_shift = (
        smalls[i : i + 1].astype(F32) for i in range(6)
    )
    fc1_shift = dot_nt(smalls[6:], select).reshape(bias_columns, dp_size, block)
    fc1_shift = fc1_shift.transpose(1, 0, 2).reshape(dp_size, bias_columns * block)
    fc1_shift = fc1_shift[:, :hidden_block].reshape(1, hidden_here)
    norm_one = first_norm(rows_in, gain_one, shift_one, fits)
    attn_pieces, first_along, norm_one, second_own, grad_mlp, invalid = join(
        attn_pieces, first_along, norm_one, second_own, grad_mlp, invalid
    )

    first_halves = grid.middle(first_along)
    second_along = [second_own] + grid.steps(second_own, 0, (1,))
    packed = times_pieces(norm_one, attn_pieces, 0, 3, fits)
    pairs = width_here // (2 * HEAD_DIM)
    parts = 2 if pairs % 2 == 0 else 1
    share = pairs // parts
    first_halves, second_along, packed, attn_pieces, norm_one = join(
        first_halves, second_along, packed, attn_pieces, norm_one
    )

    first_pieces = grid.finish(first_halves)
    second_along += grid.steps(second_along[0], 0, (2,))
    mixed, total = attend(packed, invalid, 0, pairs)
    attn_out = times_pieces_turned([mixed], attn_pieces, [(3, 0)], fits)
    first_pieces, second_along, attn_out = join(first_pieces, second_along, attn_out)

    second_along += grid.steps(second_along[0], 0, (3,))
    middle, norm_two = second_norm(
        rows_in, live_col, *pair.both(attn_out), proj_shift, gain_two, shift_two, fits
    )
    first_pieces, second_along, middle, norm_two = join(
        first_pieces, second_along, middle, norm_two
    )

    second_pieces = grid.finish(grid.halves_of(second_along, second_counts))
    piece_rows = grid.piece_rows()
    shifts = [fc1_shift[:, :hidden_cut], fc1_shift[:, hidden_cut:]]
    feed_a = feed_forward(
        norm_two, grad_mlp, shifts[0], first_pieces, places, piece_rows, (), fits
    )
    second_pieces, feed_a, norm_two = join(second_pieces, feed_a, norm_two)

    last_a = grid.reduce_last(feed_a[3:])
    feed_b = feed_forward(
        norm_two, grad_mlp, shifts[1], second_pieces, places, piece_rows, feed_a[:2], fits
    )
    grad_fc1_bias = jnp.concatenate([feed_a[2], feed_b[2]], axis=1)
    last_a, feed_b = join(last_a, feed_b)
    mlp_out, grad_two = feed_b[:2]

    middle_a = grid.reduce_middle(last_a)
    grad_middle, grad_branch, sums = norm_back(
        grad_mlp, live_col, *pair.both(grad_two), middle, gain_two, fits
    )
    grad_branch, pieces_b = join(grad_branch, feed_b[3:])
    last_b = grid.reduce_last(pieces_b)
    grad_mixed = times_pieces(grad_branch, attn_pieces, 3, 1, fits)
    middle_a, grad_mixed, mlp_out = join(middle_a, grad_mixed, mlp_out)

    def back(part):
        packed_late, mixed_late, total_late, late = join(packed, mixed, total, grad_mixed)
        return attend_back(
            packed_late, invalid, mixed_late, total_late, late, part * share, share
        )

    def grads(part, columns):
        lefts, rights = (norm_one,) * 3, tuple(columns)
        if part == 0:
            lefts = lefts + (grad_branch,) * parts
            rights = rights + tuple((mixed, p) for p in range(parts))
        return weight_grads(lefts, rights, piece_rows, fits)

    pieces_a = grid.first_pieces(middle_a)
    first_a = grid.send_first(pieces_a, (1, 3))
    columns = back(0)
    mlp_out = pair.own_total(mlp_out)
    last_b, first_a, pieces_a, columns, grad_mixed, mlp_out = join(
        last_b, first_a, pieces_a, columns, grad_mixed, mlp_out
    )

    middle_b = grid.reduce_middle(last_b)
    first_a = pieces_a[:1] + first_a + grid.send_first(pieces_a, (2,))
    pieces_c = grads(0, columns)
    middle_b, pieces_c, grad_mixed, first_a = join(middle_b, pieces_c, grad_mixed, first_a)

    last_c = grid.reduce_last(pieces_c)
    pieces_b = grid.first_pieces(middle_b)
    first_b = grid.send_first(pieces_b, (1, 3))
    pieces_d, places_c = (), [(j, p) for p in range(parts) for j in range(3)]
    if parts == 2:
        more = back(1)
        last_c, first_b, pieces_b, more = join(last_c, first_b, pieces_b, more)
        columns = columns + more
        pieces_d = grads(1, more)

    middle_c = grid.reduce_middle(last_c)
    first_b = pieces_b[:1] + first_b + grid.send_first(pieces_b, (2,))
    grad_one = times_pieces_turned(columns, attn_pieces, places_c, fits, 2)
    middle_c, first_b, pieces_d, grad_one = join(middle_c, first_b, pieces_d, grad_one)

    last_d = grid.reduce_last(pieces_d) if parts == 2 else ()
    first_c = grid.reduce_first(middle_c)
    grad_rows, sums_one = first_norm_back(
        grad_middle if fits else pair.own(grad_middle),
        rest_grad,
        *pair.own_both(grad_one),
        own_in,
        gain_one,
        fits,
    )
    sums_one = pair.small_total(sums_one)
    last_d, sums_one, grad_rows = join(last_d, sums_one, grad_rows)

    middle_d = grid.reduce_middle(last_d) if parts == 2 else ()
    bias_grads = grad_fc1_bias.astype(BF16).reshape(dp_size, hidden_block)
    bias_grads = jnp.pad(bias_grads, ((0, 0), (0, bias_pad))).reshape(dp_size, bias_columns, block)
    bias_grads = dot_nn(bias_grads.transpose(1, 0, 2).reshape(bias_columns, width), select)
    small_grads = jnp.concatenate([sums_one, sums, bias_grads], axis=0)
    small_grads = grid.blocks_of(small_grads)
    small_grads, grad_rows, _ = join(small_grads, grad_rows, [m[0] for m in middle_d])
    grad_inputs = dot_nt(grad_rows, select).astype(BF16)
    small_grads = grid.reduce_small(small_grads, 2)
    small_grads = grid.reduce_small(small_grads, 1)
    middle_d, small_grads, first_c, grad_inputs, mlp_out = join(
        middle_d, small_grads, first_c, grad_inputs, mlp_out
    )

    if parts == 2:
        count, lanes = small_grads.shape[1], middle_d[0][0].shape[2]
        spare = ((0, 2), (0, 0), (0, lanes - block))
        pieces_d = [
            jnp.concatenate([p, jnp.pad(g.astype(p.dtype)[None], spare)], axis=1)
            for p, g in zip(grid.first_pieces(middle_d), small_grads)
        ]
        sum_d = grid.reduce_end(pieces_d[:1] + grid.send_first(pieces_d, (1, 2, 3)))
        sum_d, small_grads = sum_d[:, :block], sum_d[0, block:, :block]
    else:
        small_grads = grid.reduce_small(small_grads, 0)
    result = pair.own(middle) + own_live * (mlp_out + fc2_shift)
    outputs = dot_nt(result.astype(BF16), select).astype(BF16)
    first_a, first_b = grid.reduce_end(first_a), grid.reduce_end(first_b)
    out_fc1 = jnp.concatenate([first_a[0], first_a[1], first_b[0], first_b[1]], axis=1)
    out_fc2 = jnp.concatenate([first_a[2], first_a[3], first_b[2], first_b[3]], axis=1)
    out_c = grid.reduce_end(first_c)
    out_qkv = out_c[:3]
    if parts == 2:
        out_qkv = jnp.concatenate([out_qkv, sum_d], axis=2)
    out_proj = jnp.concatenate([out_c[3 + p] for p in range(parts)], axis=1)
    return (
        outputs,
        grad_inputs,
        small_grads[0],
        small_grads[1],
        out_qkv,
        out_proj.T,
        small_grads[4],
        small_grads[2],
        small_grads[3],
        out_fc1,
        small_grads[6:].reshape(-1)[:hidden_block],
        out_fc2.T,
        small_grads[5],
    )


def solution(mesh):
    in_specs = (
        P(("dp", "tensor"), None),
        P(("dp", "tensor"), None),
        P("dp"),
        P(("dp", "tensor")),
        P("dp"),
        P("dp"),
        P(None, "dp", "tensor"),
        P("tensor", "dp"),
        P("dp"),
        P("dp"),
        P("dp"),
        P("dp", "tensor"),
        P(("tensor", "dp")),
        P("tensor", "dp"),
        P("dp"),
    )
    out_specs = (
        P(("dp", "tensor"), None),
        P(("dp", "tensor"), None),
        P("dp"),
        P("dp"),
        P(None, "dp", "tensor"),
        P("tensor", "dp"),
        P("dp"),
        P("dp"),
        P("dp"),
        P("dp", "tensor"),
        P(("tensor", "dp")),
        P("tensor", "dp"),
        P("dp"),
    )
    return jax.shard_map(
        on_device, mesh=mesh, in_specs=in_specs, out_specs=out_specs, check_vma=False
    )
```

```python
import functools

import jax
import jax.numpy as jnp
import numpy as np
from jax import lax
from jax.experimental import pallas as pl
from jax.experimental.pallas import tpu as pltpu
from jax.sharding import PartitionSpec as P

HEAD_DIM = 64
SEQ_LEN = 1104
F32 = jnp.float32
BF16 = jnp.bfloat16
MIB = 2**20


def dp_factors(size):
    if size % 8 == 0:
        return (4, 2, size // 8)
    return (1, 1, size)


class DpGrid:
    def __init__(self, size, block):
        self.size = size
        self.block = block
        self.half = block // 2
        self.factors = dp_factors(size)
        self.routes = ((2, 1), (1, 2))

    def coords(self, index):
        _, second, third = self.factors
        return (index // (second * third), (index // third) % second, index % third)

    def index(self, coords):
        _, second, third = self.factors
        return (coords[0] * second + coords[1]) * third + coords[2]

    def ahead(self, index, axis, step):
        coords = list(self.coords(index))
        coords[axis] = (coords[axis] + step) % self.factors[axis]
        return self.index(coords)

    def fetch(self, value, axis, step):
        pairs = [(self.ahead(i, axis, step), i) for i in range(self.size)]
        return lax.ppermute(value, "dp", pairs)

    def push(self, value, axis, step):
        pairs = [(i, self.ahead(i, axis, step)) for i in range(self.size)]
        return lax.ppermute(value, "dp", pairs)

    def spread(self, shard):
        with jax.named_scope("gather_z"):
            return [shard] + [self.fetch(shard, 0, s) for s in range(1, self.factors[0])]

    def middle(self, along):
        halves = []
        for part, (middle, _) in enumerate(self.routes):
            rows = slice(part * self.half, (part + 1) * self.half)
            value = jnp.concatenate([a[..., rows, :] for a in along], axis=-2)
            steps = range(1, self.factors[middle])
            with jax.named_scope("gather_middle"):
                halves.append([value] + [self.fetch(value, middle, s) for s in steps])
        return halves

    def finish(self, halves):
        pieces = []
        for (_, last), parts in zip(self.routes, halves):
            value = jnp.concatenate(parts, axis=-2)
            pieces.append(value)
            with jax.named_scope("gather_last"):
                pieces.extend(self.fetch(value, last, s) for s in range(1, self.factors[last]))
        return pieces

    def gather(self, shard):
        return self.finish(self.middle(self.spread(shard)))

    def spread_middle(self, shard):
        parts = []
        for part, (middle, _) in enumerate(self.routes):
            value = shard[..., part * self.half : (part + 1) * self.half, :]
            with jax.named_scope("gather_middle"):
                steps = range(1, self.factors[middle])
                parts.append([value] + [self.fetch(value, middle, s) for s in steps])
        return parts

    def steps(self, value, axis, steps):
        with jax.named_scope("gather_step"):
            return [self.fetch(value, axis, s) for s in steps if s < self.factors[axis]]

    def halves_of(self, along, counts):
        halves, start = [], 0
        for count in counts:
            rows = slice(start, start + count * self.half)
            start += count * self.half
            value = jnp.stack([a[..., rows, :] for a in along], axis=-3)
            lead, wide = value.shape[:-3], value.shape[-1]
            value = value.reshape(lead + (self.factors[0], count, self.half, wide))
            value = jnp.swapaxes(value, -4, -3)
            halves.append([value.reshape(lead + (-1, wide))])
        return halves

    def reduce_last(self, pieces):
        pieces, halves = list(pieces), []
        for _, last in self.routes:
            mine, pieces = pieces[: self.factors[last]], pieces[self.factors[last] :]
            with jax.named_scope("reduce_last"):
                sent = [self.push(mine[s], last, s) for s in range(1, self.factors[last])]
            halves.append([mine[0]] + sent)
        return halves

    def reduce_middle(self, halves):
        rows, out = self.factors[0] * self.half, []
        for (middle, _), parts in zip(self.routes, halves):
            cut = [
                sum(p[..., s * rows : (s + 1) * rows, :].astype(F32) for p in parts).astype(BF16)
                for s in range(self.factors[middle])
            ]
            with jax.named_scope("reduce_middle"):
                sent = [self.push(cut[s], middle, s) for s in range(1, self.factors[middle])]
            out.append([cut[0]] + sent)
        return out

    def first_pieces(self, halves):
        def along(step):
            rows = slice(step * self.half, (step + 1) * self.half)
            totals = [sum(p[..., rows, :].astype(F32) for p in parts) for parts in halves]
            return jnp.concatenate(totals, axis=-2)

        return [along(0)] + [along(s).astype(BF16) for s in range(1, self.factors[0])]

    def send_first(self, pieces, steps):
        with jax.named_scope("reduce_z"):
            return [self.push(pieces[s], 0, s) for s in steps if s < len(pieces)]

    def reduce_first(self, halves):
        pieces = self.first_pieces(halves)
        return pieces[:1] + self.send_first(pieces, (1, 2, 3))

    def reduce_end(self, parts):
        return sum(p.astype(F32) for p in parts)

    def scatter(self, pieces):
        return self.reduce_end(self.reduce_first(self.reduce_middle(self.reduce_last(pieces))))

    def gather_small(self, value, axes):
        for axis in axes:
            with jax.named_scope("gather_small"):
                parts = [value] + [self.fetch(value, axis, s) for s in range(1, self.factors[axis])]
            value = jnp.concatenate(parts, axis=0)
        return value

    def small_in_order(self, value):
        zeroth, second, third = self.factors
        value = value.reshape((third, second, zeroth, value.shape[1], 2, self.half))
        first_half = value[..., 0, :].transpose(3, 1, 0, 2, 4)
        second_half = value[..., 1, :].transpose(3, 0, 1, 2, 4)
        count = value.shape[3]
        return jnp.concatenate(
            [first_half.reshape(count, -1), second_half.reshape(count, -1)], axis=1
        )

    def blocks_of(self, value):
        count, full = value.shape
        second, third = self.factors[1], self.factors[2]
        first_half = value[:, : full // 2].reshape(count, second, third, self.factors[0], self.half)
        second_half = value[:, full // 2 :].reshape(count, third, second, self.factors[0], self.half)
        return jnp.concatenate(
            [first_half.transpose(2, 1, 3, 0, 4), second_half.transpose(1, 2, 3, 0, 4)], axis=-1
        )

    def reduce_small(self, value, axis):
        value = value.astype(BF16)
        total = value[0].astype(F32)
        with jax.named_scope("reduce_small"):
            for step in range(1, self.factors[axis]):
                total = total + self.push(value[step], axis, step).astype(F32)
        return total

    def piece_rows(self):
        full = self.size * self.half
        rows = []
        for _, last in self.routes:
            rows.extend([full // self.factors[last]] * self.factors[last])
        return rows

    def cut(self, value, axis=0):
        edges = np.cumsum(self.piece_rows())[:-1].tolist()
        return jnp.split(value, edges, axis=axis)

    def places(self):
        return (self.features()[:: self.half] // self.half).astype(jnp.int32)

    def features(self):
        here = self.coords(lax.axis_index("dp"))
        indices = []
        for part, (middle, last) in enumerate(self.routes):
            shape = (self.factors[last], self.factors[middle], self.factors[0], self.half)
            steps = [None, None, None]
            steps[last], steps[middle], steps[0], sub = (
                jnp.asarray(g.reshape(-1), jnp.int32) for g in np.indices(shape)
            )
            coords = [(h + s) % f for h, s, f in zip(here, steps, self.factors)]
            indices.append(self.index(coords) * self.block + part * self.half + sub)
        return jnp.concatenate(indices)


class TensorPair:
    def __init__(self, size, slot_count, local_rows):
        self.size = size
        self.relative = size == 2 and slot_count == 1
        self.local_rows = local_rows

    def swap(self, value):
        return lax.ppermute(value, "tensor", [(0, 1), (1, 0)])

    def parts(self, value):
        if self.relative:
            return [value, self.swap(value)]
        return [lax.all_gather(value, "tensor", axis=0, tiled=True)]

    def whole(self, value):
        return jnp.concatenate(self.parts(value), axis=0)

    def own(self, value):
        if self.relative:
            return value[: self.local_rows]
        start = lax.axis_index("tensor") * self.local_rows
        return lax.dynamic_slice_in_dim(value, start, self.local_rows, axis=0)

    def both(self, value):
        if self.relative:
            return value, self.swap(value)
        return lax.psum(value.astype(F32), "tensor"), jnp.zeros((1, value.shape[1]), F32)

    def own_both(self, halves):
        if self.relative:
            return halves[0], self.swap(halves[1])
        value = jnp.concatenate(halves, axis=0)
        total = lax.psum_scatter(value, "tensor", scatter_dimension=0, tiled=True)
        return total, jnp.zeros((1, value.shape[1]), F32)

    def small_total(self, value):
        if self.size == 2:
            return value + self.swap(value)
        return lax.psum(value, "tensor")


def join(*groups):
    flat, tree = jax.tree.flatten(groups)
    return jax.tree.unflatten(tree, lax.optimization_barrier(tuple(flat)))


def normalize(values):
    row_mean = jnp.mean(values, axis=-1, keepdims=True)
    centered = values - row_mean
    variance = jnp.mean(centered * centered, axis=-1, keepdims=True)
    inverse = lax.rsqrt(variance + 1e-05)
    return centered * inverse, inverse


def norm_input_grad(grad, gain, normed, inverse):
    scaled = grad * gain
    first = jnp.mean(scaled, axis=-1, keepdims=True)
    second = jnp.mean(scaled * normed, axis=-1, keepdims=True)
    return inverse * (scaled - first - normed * second)


def dot_nn(left, right):
    return lax.dot_general(left, right, (((1,), (0,)), ((), ())), preferred_element_type=F32)


def dot_nt(left, right):
    return lax.dot_general(left, right, (((1,), (1,)), ((), ())), preferred_element_type=F32)


def dot_tn(left, right):
    return lax.dot_general(left, right, (((0,), (0,)), ((), ())), preferred_element_type=F32)


def gelu_and_slope(values):
    cdf = 0.5 + 0.5 * lax.erf(values * (0.5**0.5))
    density = jnp.exp(-0.5 * values * values) * 0.3989422804014327
    return values * cdf, cdf + values * density


def params(limit):
    return pltpu.CompilerParams(vmem_limit_bytes=limit * MIB)


def cost(micros):
    return pl.CostEstimate(
        flops=int(micros * 1e9), transcendentals=0, bytes_accessed=int(micros * 1e6)
    )


def whole_spec(array):
    return pl.BlockSpec(array.shape, lambda *grid: (0,) * len(array.shape))


def stack_rows(refs):
    return jnp.concatenate([r[...] for r in refs], axis=0)


def head_lanes(seq, head):
    lane = lax.broadcasted_iota(jnp.int32, (seq, 2 * HEAD_DIM), 1)
    mine = (lane >= HEAD_DIM) if head else (lane < HEAD_DIM)
    return mine, lane == (0 if head else HEAD_DIM)


def head_operands(query_ref, key_ref, invalid, head):
    seq = query_ref.shape[0]
    mine, extra = head_lanes(seq, head)
    one, zero = jnp.asarray(1, BF16), jnp.asarray(0, BF16)
    scaled = query_ref[...] * jnp.asarray(HEAD_DIM**-0.5, BF16)
    query = jnp.where(mine, scaled, jnp.where(extra, one, zero))
    keys = jnp.where(mine, key_ref[...], jnp.where(extra, invalid, zero))
    return query, keys


def key_column(invalid_ref):
    seq = invalid_ref.shape[-1]
    return jnp.broadcast_to(invalid_ref[0], (2 * HEAD_DIM, seq)).T.astype(BF16)


def attend_kernel(query_ref, key_ref, value_ref, invalid_ref, mixed_ref, total_ref, turned_ref):
    seq = query_ref.shape[0]
    invalid = key_column(invalid_ref)
    values = value_ref[...].T
    for head in range(2):
        rows = slice(head * HEAD_DIM, (head + 1) * HEAD_DIM)
        query, keys = head_operands(query_ref, key_ref, invalid, head)
        with_ones = jnp.concatenate([values[rows], jnp.ones((16, seq), BF16)], axis=0)
        scores = dot_nt(keys, query)
        largest = jnp.max(scores, axis=0, keepdims=True)
        weights = jnp.exp(scores - largest)
        mixed = dot_nn(with_ones, weights.astype(BF16))
        weight_sum = mixed[HEAD_DIM : HEAD_DIM + 1]
        turned_ref[rows] = mixed[:HEAD_DIM] * (1.0 / weight_sum)
        total_ref[0, 0, head : head + 1] = largest + jnp.log(weight_sum)
    mixed_ref[...] = turned_ref[...].T.astype(BF16)


def attend_back_kernel(
    query_ref,
    key_ref,
    value_ref,
    invalid_ref,
    mixed_ref,
    total_ref,
    grad_ref,
    grad_query_ref,
    grad_key_ref,
    grad_value_ref,
    turned_ref,
):
    seq = query_ref.shape[0]
    invalid = key_column(invalid_ref)
    keys_turned = key_ref[...].T
    product = mixed_ref[...].astype(F32).T * grad_ref[...].astype(F32).T
    for head in range(2):
        rows = slice(head * HEAD_DIM, (head + 1) * HEAD_DIM)
        mine, _ = head_lanes(seq, head)
        query, keys = head_operands(query_ref, key_ref, invalid, head)
        grad = jnp.where(mine, grad_ref[...], jnp.asarray(0, BF16))
        row_dot = jnp.sum(product[rows], axis=0, keepdims=True)
        prob = jnp.exp(dot_nt(keys, query) - total_ref[0, 0, head : head + 1])
        grad_prob = dot_nt(value_ref[...], grad) - row_dot
        grad_score = (prob * grad_prob).astype(BF16)
        turned_ref[rows] = dot_nn(keys_turned[rows], grad_score) * HEAD_DIM**-0.5
        grad_value = dot_nn(prob.astype(BF16), grad)
        grad_key = dot_nn(grad_score, jnp.where(mine, query, jnp.asarray(0, BF16)))
        if head == 0:
            first_value, first_key = grad_value, grad_key
    grad_value_ref[...] = (first_value + grad_value).astype(BF16)
    grad_key_ref[...] = (first_key + grad_key).astype(BF16)
    grad_query_ref[...] = turned_ref[...].T.astype(BF16)


def attend_specs():
    def columns(offset):
        return pl.BlockSpec((SEQ_LEN, 2 * HEAD_DIM), lambda s, p: (s, p + offset))

    invalid = pl.BlockSpec((1, 1, SEQ_LEN), lambda s, p: (s, 0, 0))
    total = pl.BlockSpec((1, 1, 2, SEQ_LEN), lambda s, p: (s, p, 0, 0))
    return columns, invalid, total


def attend(packed, invalid, first, count):
    slots, pairs = invalid.shape[0], packed.shape[1] // (6 * HEAD_DIM)
    columns, invalid_spec, total_spec = attend_specs()
    return pl.pallas_call(
        attend_kernel,
        grid=(slots, count),
        in_specs=[columns(first), columns(pairs + first), columns(2 * pairs + first), invalid_spec],
        out_specs=[columns(0), total_spec],
        out_shape=[
            jax.ShapeDtypeStruct((packed.shape[0], count * 2 * HEAD_DIM), BF16),
            jax.ShapeDtypeStruct((slots, count, 2, SEQ_LEN), F32),
        ],
        scratch_shapes=[pltpu.VMEM((2 * HEAD_DIM, SEQ_LEN), F32)],
        compiler_params=params(14),
        cost_estimate=cost(4 * slots * count),
        name="attend",
    )(packed, packed, packed, invalid)


def attend_back(packed, invalid, mixed, total, grad_mixed, first, count):
    slots, pairs = invalid.shape[0], packed.shape[1] // (6 * HEAD_DIM)
    columns, invalid_spec, _ = attend_specs()
    return pl.pallas_call(
        attend_back_kernel,
        grid=(slots, count),
        in_specs=[
            columns(first),
            columns(pairs + first),
            columns(2 * pairs + first),
            invalid_spec,
            columns(first),
            pl.BlockSpec((1, 1, 2, SEQ_LEN), lambda s, p: (s, p + first, 0, 0)),
            columns(first),
        ],
        out_specs=[columns(0)] * 3,
        out_shape=[jax.ShapeDtypeStruct((mixed.shape[0], count * 2 * HEAD_DIM), BF16)] * 3,
        scratch_shapes=[
            pltpu.VMEM((2 * HEAD_DIM, SEQ_LEN), F32),
        ],
        compiler_params=params(36),
        cost_estimate=cost(9 * slots * count),
        name="attend_back",
    )(packed, packed, packed, invalid, mixed, total, grad_mixed)


def joined(pieces, first, count):
    return jnp.concatenate(
        [jnp.concatenate([p[g] for p in pieces], axis=0) for g in range(first, first + count)],
        axis=1,
    )


def times_pieces(rows, pieces, first, count, fits):
    if not fits:
        return dot_nn(rows, joined(pieces, first, count)).astype(BF16)
    wide = pieces[0].shape[2]

    def kernel(rows_ref, *refs):
        weight = jnp.concatenate([r[0] for r in refs[:-1]], axis=0)
        refs[-1][...] = dot_nn(rows_ref[...], weight).astype(BF16)

    return pl.pallas_call(
        kernel,
        grid=(count,),
        in_specs=[whole_spec(rows)]
        + [pl.BlockSpec((1, p.shape[1], wide), lambda j: (first + j, 0, 0)) for p in pieces],
        out_specs=pl.BlockSpec((rows.shape[0], wide), lambda j: (0, j)),
        out_shape=jax.ShapeDtypeStruct((rows.shape[0], count * wide), BF16),
        compiler_params=params(12),
        cost_estimate=cost(2 * count),
        name="times_pieces",
    )(rows, *pieces)


def times_pieces_turned(columns, pieces, places, fits, cuts=1):
    count = len(columns)
    rows, wide = columns[0].shape
    if not fits:
        weight = [joined(pieces, g, 1)[:, c * wide : (c + 1) * wide] for g, c in places]
        total = dot_nt(jnp.concatenate(columns, axis=1), jnp.concatenate(weight, axis=1))
        return jnp.split(total.astype(BF16), cuts) if cuts > 1 else total.astype(BF16)
    starts = np.cumsum([0] + [p.shape[1] for p in pieces]).tolist()

    def kernel(*refs):
        lefts, weights, out_refs = refs[:count], refs[count:-cuts], refs[-cuts:]
        left = jnp.concatenate([r[...] for r in lefts], axis=1)
        weight = jnp.concatenate(
            [
                jnp.concatenate([r[0] for r in weights[i * count : (i + 1) * count]], axis=1)
                for i in range(len(pieces))
            ],
            axis=0,
        )
        for k, out_ref in enumerate(out_refs):
            cut = slice(k * rows // cuts, (k + 1) * rows // cuts)
            out_ref[...] = dot_nt(left[cut], weight).astype(BF16)

    def place_spec(piece, group, column):
        return pl.BlockSpec((1, piece.shape[1], wide), lambda i: (group, 0, column))

    outs = pl.pallas_call(
        kernel,
        grid=(1,),
        in_specs=[whole_spec(c) for c in columns] + [place_spec(p, *q) for p in pieces for q in places],
        out_specs=[pl.BlockSpec((rows // cuts, starts[-1]), lambda i: (0, 0))] * cuts,
        out_shape=[jax.ShapeDtypeStruct((rows // cuts, starts[-1]), BF16)] * cuts,
        compiler_params=params(16),
        cost_estimate=cost(1 + count),
        name="times_pieces_turned",
    )(*columns, *[p for p in pieces for _ in places])
    return outs if cuts > 1 else outs[0]


def weight_grads(lefts, rights, piece_rows, fits):
    wide = rights[0].shape[1]
    rights = [r if isinstance(r, tuple) else (r, 0) for r in rights]
    starts = np.cumsum([0] + piece_rows).tolist()
    if not fits:
        blocks = [a[:, c * wide : (c + 1) * wide] for a, c in rights]
        full = jnp.stack([dot_tn(a, b).astype(BF16) for a, b in zip(lefts, blocks)])
        return [full[:, s:e] for s, e in zip(starts, starts[1:])]
    count = len(rights)
    names = []
    for left in lefts:
        if not any(left is other for other in names):
            names.append(left)
    which = [next(i for i, o in enumerate(names) if o is left) for left in lefts]

    def kernel(*refs):
        left_refs, right_refs = refs[: len(names)], refs[len(names) : len(names) + count]
        out_refs = refs[len(names) + count :]
        turned = [r[...].T for r in left_refs]
        for k in range(count):
            product = dot_nn(turned[which[k]], right_refs[k][...]).astype(BF16)
            for i, (start, end) in enumerate(zip(starts, starts[1:])):
                out_refs[i][k] = product[start:end]

    return pl.pallas_call(
        kernel,
        grid=(1,),
        in_specs=[whole_spec(a) for a in names]
        + [pl.BlockSpec((a.shape[0], wide), lambda i, c=c: (0, c)) for a, c in rights],
        out_specs=[pl.BlockSpec((count, r, wide), lambda i: (0, 0, 0)) for r in piece_rows],
        out_shape=[jax.ShapeDtypeStruct((count, r, wide), BF16) for r in piece_rows],
        compiler_params=params(20),
        cost_estimate=cost(1 + 1.5 * count),
        name="weight_grads",
    )(*names, *[a for a, _ in rights])


def joined_rows(parts):
    return parts[0] if len(parts) == 1 else jnp.concatenate(parts, axis=0)


def first_norm(rows_in, gain, bias, fits):
    width = rows_in[0].shape[1]
    rows = sum(p.shape[0] for p in rows_in)

    def work(values, gain, bias):
        normed, _ = normalize(values.astype(F32))
        return (normed * gain + bias).astype(BF16)

    if not fits:
        return work(joined_rows(rows_in), gain, bias)

    def kernel(*refs):
        gain, bias, out_ref = refs[-3][...], refs[-2][...], refs[-1]
        start = 0
        for ref in refs[:-3]:
            out_ref[start : start + ref.shape[0]] = work(ref[...], gain, bias)
            start += ref.shape[0]

    return pl.pallas_call(
        kernel,
        out_shape=jax.ShapeDtypeStruct((rows, width), BF16),
        compiler_params=params(12),
        cost_estimate=cost(3),
        name="first_norm",
    )(*rows_in, gain, bias)


def second_norm(rows_in, live, mine, other, shift, gain, bias, fits):
    rows, width = mine.shape

    def work(rows_in, live, mine, other, shift, gain, bias):
        branch = mine.astype(F32) + other.astype(F32) + shift
        middle = rows_in.astype(F32) + live * branch
        normed, _ = normalize(middle)
        return middle, (normed * gain + bias).astype(BF16)

    if not fits:
        return work(joined_rows(rows_in), live, mine, other, shift, gain, bias)
    half = rows // 2

    def kernel(own_ref, next_ref, *refs):
        rows_in = jnp.where(pl.program_id(0) == 0, own_ref[...], next_ref[...])
        refs[-2][...], refs[-1][...] = work(rows_in, *[r[...] for r in refs[:-2]])

    def block(columns, place=lambda i: i):
        return pl.BlockSpec((half, columns), lambda i: (place(i), 0))

    return pl.pallas_call(
        kernel,
        grid=(2,),
        in_specs=[
            block(width, lambda i: 0),
            block(width, lambda i: 0),
            block(1),
            block(width),
            block(width, lambda i: 1 - i),
        ]
        + [whole_spec(shift)] * 3,
        out_specs=[block(width), block(width)],
        out_shape=[
            pltpu.HBM((rows, width), F32),
            jax.ShapeDtypeStruct((rows, width), BF16),
        ],
        compiler_params=params(40),
        cost_estimate=cost(4),
        name="second_norm",
    )(*rows_in, live, mine, other, shift, gain, bias)


def norm_back(grad_out, live, mine, other, middle, gain, fits):
    rows, width = middle.shape

    def work(grad_out, live, mine, other, middle, gain):
        grad_out = grad_out.astype(F32)
        grad = mine.astype(F32) + other.astype(F32)
        normed, inverse = normalize(middle)
        grad_middle = grad_out + norm_input_grad(grad, gain, normed, inverse)
        grad_branch = (live * grad_middle).astype(BF16)
        sums = [grad * normed, grad, grad_branch.astype(F32), grad_out]
        sums = jnp.concatenate([jnp.sum(s, axis=0, keepdims=True) for s in sums], axis=0)
        return grad_middle, grad_branch, sums

    if not fits:
        return work(joined_rows(grad_out), live, mine, other, middle, gain)
    half = rows // 2

    def kernel(own_ref, next_ref, live_ref, mine_ref, other_ref, middle_ref, gain_ref, *refs):
        step = pl.program_id(0)
        grad = jnp.where(step == 0, own_ref[...], next_ref[...])
        rest = [r[...] for r in (live_ref, mine_ref, other_ref, middle_ref, gain_ref)]
        grad_middle, refs[1][...], sums = work(grad, *rest)

        @pl.when(step == 0)
        def _():
            refs[0][...] = grad_middle
            refs[2][...] = sums

        @pl.when(step == 1)
        def _():
            refs[2][...] += sums

    def block(columns, place=lambda i: i):
        return pl.BlockSpec((half, columns), lambda i: (place(i), 0))

    return pl.pallas_call(
        kernel,
        grid=(2,),
        in_specs=[
            block(width, lambda i: 0),
            block(width, lambda i: 0),
            block(1),
            block(width),
            block(width, lambda i: 1 - i),
            block(width),
            whole_spec(gain),
        ],
        out_specs=[
            block(width, lambda i: 0),
            block(width),
            pl.BlockSpec((4, width), lambda i: (0, 0)),
        ],
        out_shape=[
            jax.ShapeDtypeStruct((half, width), F32),
            jax.ShapeDtypeStruct((rows, width), BF16),
            jax.ShapeDtypeStruct((4, width), F32),
        ],
        compiler_params=params(44),
        cost_estimate=cost(7),
        name="norm_back",
    )(*grad_out, live, mine, other, middle, gain)


def first_norm_back(grad_middle, rest, mine, other, rows_in, gain, fits):
    rows, width = rows_in.shape

    def work(grad_middle, rest, mine, other, rows_in, gain):
        grad = mine.astype(F32) + other.astype(F32)
        normed, inverse = normalize(rows_in.astype(F32))
        grad_rows = grad_middle + rest.astype(F32) + norm_input_grad(grad, gain, normed, inverse)
        sums = [jnp.sum(s, axis=0, keepdims=True) for s in (grad * normed, grad)]
        return grad_rows.astype(BF16), jnp.concatenate(sums, axis=0)

    if not fits:
        return work(grad_middle, rest, mine, other, rows_in, gain)

    def kernel(*refs):
        refs[-2][...], refs[-1][...] = work(*[r[...] for r in refs[:-2]])

    own = pl.BlockSpec((rows, width), lambda i: (0, 0))
    return pl.pallas_call(
        kernel,
        grid=(1,),
        in_specs=[own] * 5 + [pl.BlockSpec((1, width), lambda i: (0, 0))],
        out_specs=[own, pl.BlockSpec((2, width), lambda i: (0, 0))],
        out_shape=[
            jax.ShapeDtypeStruct((rows, width), BF16),
            jax.ShapeDtypeStruct((2, width), F32),
        ],
        compiler_params=params(14),
        cost_estimate=cost(4),
        name="first_norm_back",
    )(grad_middle, rest, mine, other, rows_in, gain)


def feed_kernel(counts, carried, plain, scattered, places_ref, *refs):
    halves, pieces, grad_pieces = counts
    normed_ref, shift_ref, grad_refs = refs[0], refs[1], refs[2 : 2 + halves]
    refs = refs[2 + halves :]
    first_refs, second_refs, refs = refs[:pieces], refs[pieces : 2 * pieces], refs[2 * pieces :]
    before, refs = (refs[:2], refs[2:]) if carried else ((), refs)
    out_ref, grad_two_ref, shift_grad_ref = refs[:3]
    weight_grad_refs = refs[3 : 3 + grad_pieces]
    grad_ref, normed_turned, grad_turned, out_sum, grad_sum = refs[3 + grad_pieces :]
    step = pl.program_id(0)
    blocks = places_ref.shape[0]
    size = normed_ref.shape[1] // blocks

    def place(i):
        return pl.ds(pl.multiple_of(places_ref[i] * size, size), size)

    @pl.when(step == 0)
    def _():
        start = 0
        for ref in grad_refs:
            grad_ref[start : start + ref.shape[0]] = ref[...]
            start += ref.shape[0]
        if scattered:
            for i in range(blocks):
                rows = slice(i * size, (i + 1) * size)
                normed_turned[place(i)] = normed_ref[:, rows].T
                grad_turned[place(i)] = grad_ref[:, rows].T
        else:
            normed_turned[...] = normed_ref[...].T
            grad_turned[...] = grad_ref[...].T

    if plain:
        first = jnp.concatenate([first_refs[0][place(i)] for i in range(blocks)], axis=0)
        second = jnp.concatenate([second_refs[0][place(i)] for i in range(blocks)], axis=0)
    else:
        first = jnp.concatenate([w[0] for w in first_refs], axis=0)
        second = jnp.concatenate([w[0] for w in second_refs], axis=0)
    hidden = dot_nn(normed_ref[...], first) + shift_ref[...]
    hidden_act, slope = gelu_and_slope(hidden)
    hidden_act = hidden_act.astype(BF16)
    grad_pre = (dot_nn(grad_ref[...], second) * slope).astype(BF16)
    shift_grad_ref[...] = jnp.sum(grad_pre.astype(F32), axis=0, keepdims=True)
    last = pl.num_programs(0) - 1
    products = (
        (out_sum, out_ref, hidden_act, second, before[:1]),
        (grad_sum, grad_two_ref, grad_pre, first, before[1:]),
    )

    @pl.when(step == 0)
    def _():
        for sum_ref, _, left, right, start in products:
            product = dot_nt(left, right)
            sum_ref[...] = product + start[0][...].astype(F32) if carried else product

    @pl.when(step == last)
    def _():
        for sum_ref, end_ref, left, right, _ in products:
            end_ref[...] = (sum_ref[...] + dot_nt(left, right)).astype(BF16)

    if scattered:
        weight_grad_refs[0][...] = dot_nn(normed_turned[...], grad_pre).astype(BF16)
        weight_grad_refs[1][...] = dot_nn(grad_turned[...], hidden_act).astype(BF16)
    else:
        for k, (left, right) in enumerate(
            ((normed_turned, grad_pre), (grad_turned, hidden_act))
        ):
            product, start = dot_nn(left[...], right).astype(BF16), 0
            for ref in weight_grad_refs:
                ref[k, 0] = product[start : start + ref.shape[2]]
                start += ref.shape[2]


def feed_forward(normed, grads, shift, weight, places, piece_rows, before, fits):
    rows, width = normed.shape
    plain, scattered = not isinstance(weight, list), piece_rows is None
    units = shift.shape[1]
    wide = units if plain else weight[0].shape[2]
    groups = units // wide
    if not fits:
        size = width // places.shape[0]
        order = (places[:, None] * size + jnp.arange(size)[None, :]).reshape(-1)
        if plain:
            both = jnp.take(weight, order, axis=0)
            first_w, second_w = both[:, :units], both[:, units:]
        else:
            first_w, second_w = joined(weight, 0, groups), joined(weight, groups, groups)
        grad = jnp.concatenate(grads, axis=0)
        hidden_act, slope = gelu_and_slope(dot_nn(normed, first_w) + shift)
        hidden_act = hidden_act.astype(BF16)
        grad_pre = (dot_nn(grad, second_w) * slope).astype(BF16)
        out, grad_two = dot_nt(hidden_act, second_w), dot_nt(grad_pre, first_w)
        if before:
            out, grad_two = out + before[0].astype(F32), grad_two + before[1].astype(F32)
        outs = [dot_tn(normed, grad_pre).astype(BF16), dot_tn(grad, hidden_act).astype(BF16)]
        if scattered:
            outs = [jnp.zeros_like(g).at[order].set(g) for g in outs]
        else:
            size = units // 2
            outs = jnp.stack([g[:, k * size : (k + 1) * size] for g in outs for k in range(2)])
            outs = jnp.split(outs, np.cumsum(piece_rows)[:-1].tolist(), 1)
        shift_grad = jnp.sum(grad_pre, axis=0, dtype=F32, keepdims=True)
        return [out.astype(BF16), grad_two.astype(BF16), shift_grad] + outs

    tile = units // 2
    per = wide // tile
    pieces = [weight] if plain else weight

    def once(array):
        return pl.BlockSpec(
            array.shape, lambda j, p: (0,) * len(array.shape), pipeline_mode=pl.Buffered(1)
        )

    def weight_spec(piece, second):
        if plain:
            return pl.BlockSpec((width, tile), lambda j, p: (0, second * per + j))
        return pl.BlockSpec(
            (1, piece.shape[1], tile), lambda j, p: (second * groups + j // per, 0, j % per)
        )

    if scattered:
        grad_specs = [pl.BlockSpec((width, tile), lambda j, p: (0, j))] * 2
        grad_shapes = [jax.ShapeDtypeStruct((width, units), BF16)] * 2
    else:
        half = units // 2
        split = half // tile
        grad_specs = [
            pl.BlockSpec((2, 1, r, tile), lambda j, p: (0, j // split, 0, j % split))
            for r in piece_rows
        ]
        grad_shapes = [pltpu.HBM((2, 2, r, half), BF16) for r in piece_rows]
    before = tuple(before)
    outs = pl.pallas_call(
        functools.partial(
            feed_kernel,
            (len(grads), len(pieces), len(grad_shapes)),
            bool(before),
            plain,
            scattered,
        ),
        grid_spec=pltpu.PrefetchScalarGridSpec(
            num_scalar_prefetch=1,
            grid=(units // tile,),
            in_specs=[once(normed), pl.BlockSpec((1, tile), lambda j, p: (0, j))]
            + [once(g) for g in grads]
            + [weight_spec(p, 0) for p in pieces]
            + [weight_spec(p, 1) for p in pieces]
            + [once(b) for b in before],
            out_specs=[
                pl.BlockSpec((rows, width), lambda j, p: (0, 0)),
                pl.BlockSpec((rows, width), lambda j, p: (0, 0)),
                pl.BlockSpec((1, tile), lambda j, p: (0, j)),
            ]
            + grad_specs,
            scratch_shapes=[
                pltpu.VMEM((rows, width), BF16),
                pltpu.VMEM((width, rows), BF16),
                pltpu.VMEM((width, rows), BF16),
                pltpu.VMEM((rows, width), F32),
                pltpu.VMEM((rows, width), F32),
            ],
        ),
        out_shape=[
            pltpu.HBM((rows, width), BF16),
            pltpu.HBM((rows, width), BF16),
            jax.ShapeDtypeStruct((1, units), F32),
        ]
        + grad_shapes,
        compiler_params=params(44),
        cost_estimate=cost(25),
        name="feed_forward",
    )(places, normed, shift, *grads, *pieces, *pieces, *before)
    outs = list(outs)
    if not scattered:
        outs[3:] = [g.reshape((4,) + g.shape[2:]) for g in outs[3:]]
    return outs


def on_device(
    inputs,
    cotangent,
    slot_live,
    token_type,
    attn_norm_gain,
    attn_norm_bias,
    qkv_weight,
    proj_weight,
    proj_bias,
    mlp_norm_gain,
    mlp_norm_bias,
    fc1_weight,
    fc1_bias,
    fc2_weight,
    fc2_bias,
):
    dp_size = lax.axis_size("dp")
    tensor_size = lax.axis_size("tensor")
    local_rows, width = inputs.shape
    slot_count = slot_live.shape[0]
    whole_rows = local_rows * tensor_size
    block = fc1_weight.shape[0]
    width_here = qkv_weight.shape[2]
    hidden_here = fc1_weight.shape[1]
    hidden_block = fc1_bias.shape[0]
    hidden_cut = hidden_here // 2
    fits = whole_rows <= 2048
    grid = DpGrid(dp_size, block)
    pair = TensorPair(tensor_size, slot_count, local_rows)
    half_cut = hidden_cut // 2

    bias_columns = -(-hidden_block // block)
    bias_pad = bias_columns * block - hidden_block
    smalls = jnp.stack(
        (attn_norm_gain, attn_norm_bias, proj_bias, mlp_norm_gain, mlp_norm_bias, fc2_bias)
    )
    bias_block = jnp.pad(fc1_bias, (0, bias_pad)).reshape(bias_columns, block)
    smalls = jnp.concatenate([smalls, bias_block], axis=0)
    fc2_turned = fc2_weight.T
    cuts = slice(0, hidden_cut), slice(hidden_cut, hidden_here)
    groups = [
        w[:, start : start + half_cut]
        for w in (fc1_weight, fc2_turned)
        for start in (0, half_cut)
    ]
    first_shard = jnp.stack(groups)
    second_shard = jnp.stack(
        [
            w[:, start : start + half_cut]
            for w in (fc1_weight, fc2_turned)
            for start in (hidden_cut, hidden_cut + half_cut)
        ]
    )
    attn_shard = jnp.concatenate([qkv_weight, proj_weight.T[None]], axis=0)
    count = smalls.shape[0]
    spare = ((0, 3), (0, 0), (0, width_here - block))
    attn_shard = jnp.concatenate([attn_shard, jnp.pad(smalls[None], spare)], axis=1)

    attn_along = grid.spread(attn_shard)
    smalls = jnp.stack([a[0, block:, :block] for a in attn_along])
    second_parts = grid.spread_middle(second_shard)
    attn_along, smalls, second_parts, first_shard, inputs, cotangent = join(
        attn_along, smalls, second_parts, first_shard, inputs, cotangent
    )

    attn_halves = grid.middle(attn_along)
    smalls = grid.gather_small(smalls, (1, 2))
    second_own = jnp.concatenate(second_parts[0] + second_parts[1], axis=-2)
    second_counts = [len(p) for p in second_parts]
    features, places = grid.features(), grid.places()
    select = (jnp.arange(width, dtype=jnp.int32)[:, None] == features[None, :]).astype(BF16)
    own_in = dot_nn(inputs, select).astype(BF16)
    own_in, first_shard = join(own_in, first_shard)
    first_along = [first_shard] + grid.steps(first_shard, 0, (1,))
    rows_in = pair.parts(own_in)
    own_grad = dot_nn(cotangent, select)
    live_col = jnp.repeat(slot_live.astype(F32), SEQ_LEN)[:, None]
    own_live = pair.own(live_col)
    grad_mlp = pair.parts((own_live * own_grad).astype(BF16))
    rest_grad = ((1.0 - own_live) * own_grad).astype(BF16)
    valid_whole = pair.whole((token_type != 3).astype(F32))
    invalid = jnp.where(valid_whole > 0, 0.0, -1e30).reshape(slot_count, 1, SEQ_LEN)
    attn_halves, first_along, second_own, smalls = join(
        attn_halves, first_along, second_own, smalls
    )

    attn_pieces = grid.finish(attn_halves)
    first_along += grid.steps(first_along[0], 0, (2, 3))
    smalls = grid.small_in_order(smalls)
    gain_one, shift_one, proj_shift, gain_two, shift_two, fc2_shift = (
        smalls[i : i + 1].astype(F32) for i in range(6)
    )
    fc1_shift = dot_nt(smalls[6:], select).reshape(bias_columns, dp_size, block)
    fc1_shift = fc1_shift.transpose(1, 0, 2).reshape(dp_size, bias_columns * block)
    fc1_shift = fc1_shift[:, :hidden_block].reshape(1, hidden_here)
    norm_one = first_norm(rows_in, gain_one, shift_one, fits)
    attn_pieces, first_along, norm_one, second_own, grad_mlp, invalid = join(
        attn_pieces, first_along, norm_one, second_own, grad_mlp, invalid
    )

    first_halves = grid.middle(first_along)
    second_along = [second_own] + grid.steps(second_own, 0, (1,))
    packed = times_pieces(norm_one, attn_pieces, 0, 3, fits)
    pairs = width_here // (2 * HEAD_DIM)
    parts = 2 if pairs % 2 == 0 else 1
    share = pairs // parts
    first_halves, second_along, packed, attn_pieces, norm_one = join(
        first_halves, second_along, packed, attn_pieces, norm_one
    )

    first_pieces = grid.finish(first_halves)
    second_along += grid.steps(second_along[0], 0, (2,))
    mixed, total = attend(packed, invalid, 0, pairs)
    attn_out = times_pieces_turned([mixed], attn_pieces, [(3, 0)], fits)
    first_pieces, second_along, attn_out = join(first_pieces, second_along, attn_out)

    second_along += grid.steps(second_along[0], 0, (3,))
    middle, norm_two = second_norm(
        rows_in, live_col, *pair.both(attn_out), proj_shift, gain_two, shift_two, fits
    )
    first_pieces, second_along, middle, norm_two = join(
        first_pieces, second_along, middle, norm_two
    )

    second_pieces = grid.finish(grid.halves_of(second_along, second_counts))
    piece_rows = grid.piece_rows()
    shifts = [fc1_shift[:, :hidden_cut], fc1_shift[:, hidden_cut:]]
    feed_a = feed_forward(
        norm_two, grad_mlp, shifts[0], first_pieces, places, piece_rows, (), fits
    )
    second_pieces, feed_a, norm_two = join(second_pieces, feed_a, norm_two)

    last_a = grid.reduce_last(feed_a[3:])
    feed_b = feed_forward(
        norm_two, grad_mlp, shifts[1], second_pieces, places, piece_rows, feed_a[:2], fits
    )
    grad_fc1_bias = jnp.concatenate([feed_a[2], feed_b[2]], axis=1)
    last_a, feed_b = join(last_a, feed_b)
    mlp_out, grad_two = feed_b[:2]

    middle_a = grid.reduce_middle(last_a)
    grad_middle, grad_branch, sums = norm_back(
        grad_mlp, live_col, *pair.both(grad_two), middle, gain_two, fits
    )
    grad_branch, pieces_b = join(grad_branch, feed_b[3:])
    last_b = grid.reduce_last(pieces_b)
    grad_mixed = times_pieces(grad_branch, attn_pieces, 3, 1, fits)
    middle_a, grad_mixed, mlp_out = join(middle_a, grad_mixed, mlp_out)

    def back(part):
        packed_late, mixed_late, total_late, late = join(packed, mixed, total, grad_mixed)
        return attend_back(
            packed_late, invalid, mixed_late, total_late, late, part * share, share
        )

    def grads(part, columns):
        lefts, rights = (norm_one,) * 3, tuple(columns)
        if part == 0:
            lefts = lefts + (grad_branch,) * parts
            rights = rights + tuple((mixed, p) for p in range(parts))
        return weight_grads(lefts, rights, piece_rows, fits)

    pieces_a = grid.first_pieces(middle_a)
    first_a = grid.send_first(pieces_a, (1, 3))
    columns = back(0)
    mlp_out = pair.own_both(jnp.split(mlp_out, 2) if pair.relative else [mlp_out])
    last_b, first_a, pieces_a, columns, grad_mixed, mlp_out = join(
        last_b, first_a, pieces_a, columns, grad_mixed, mlp_out
    )

    middle_b = grid.reduce_middle(last_b)
    first_a = pieces_a[:1] + first_a + grid.send_first(pieces_a, (2,))
    pieces_c = grads(0, columns)
    middle_b, pieces_c, grad_mixed, first_a = join(middle_b, pieces_c, grad_mixed, first_a)

    last_c = grid.reduce_last(pieces_c)
    pieces_b = grid.first_pieces(middle_b)
    first_b = grid.send_first(pieces_b, (1, 3))
    pieces_d, places_c = (), [(j, p) for p in range(parts) for j in range(3)]
    if parts == 2:
        more = back(1)
        last_c, first_b, pieces_b, more = join(last_c, first_b, pieces_b, more)
        columns = columns + more
        pieces_d = grads(1, more)

    middle_c = grid.reduce_middle(last_c)
    first_b = pieces_b[:1] + first_b + grid.send_first(pieces_b, (2,))
    grad_one = times_pieces_turned(columns, attn_pieces, places_c, fits, 2)
    middle_c, first_b, pieces_d, grad_one = join(middle_c, first_b, pieces_d, grad_one)

    last_d = grid.reduce_last(pieces_d) if parts == 2 else ()
    first_c = grid.reduce_first(middle_c)
    grad_rows, sums_one = first_norm_back(
        grad_middle if fits else pair.own(grad_middle),
        rest_grad,
        *pair.own_both(grad_one),
        own_in,
        gain_one,
        fits,
    )
    sums_one = pair.small_total(sums_one)
    last_d, sums_one, grad_rows = join(last_d, sums_one, grad_rows)

    middle_d = grid.reduce_middle(last_d) if parts == 2 else ()
    bias_grads = grad_fc1_bias.astype(BF16).reshape(dp_size, hidden_block)
    bias_grads = jnp.pad(bias_grads, ((0, 0), (0, bias_pad))).reshape(dp_size, bias_columns, block)
    bias_grads = dot_nn(bias_grads.transpose(1, 0, 2).reshape(bias_columns, width), select)
    small_grads = jnp.concatenate([sums_one, sums, bias_grads], axis=0)
    small_grads = grid.blocks_of(small_grads)
    small_grads, grad_rows, _ = join(small_grads, grad_rows, [m[0] for m in middle_d])
    grad_inputs = dot_nt(grad_rows, select).astype(BF16)
    small_grads = grid.reduce_small(small_grads, 2)
    small_grads = grid.reduce_small(small_grads, 1)
    middle_d, small_grads, first_c, grad_inputs, mlp_out = join(
        middle_d, small_grads, first_c, grad_inputs, mlp_out
    )

    if parts == 2:
        count, lanes = small_grads.shape[1], middle_d[0][0].shape[2]
        spare = ((0, 2), (0, 0), (0, lanes - block))
        pieces_d = [
            jnp.concatenate([p, jnp.pad(g.astype(p.dtype)[None], spare)], axis=1)
            for p, g in zip(grid.first_pieces(middle_d), small_grads)
        ]
        sum_d = grid.reduce_end(pieces_d[:1] + grid.send_first(pieces_d, (1, 2, 3)))
        sum_d, small_grads = sum_d[:, :block], sum_d[0, block:, :block]
    else:
        small_grads = grid.reduce_small(small_grads, 0)
    mlp_out = sum(m.astype(F32) for m in mlp_out)
    result = pair.own(middle) + own_live * (mlp_out + fc2_shift)
    outputs = dot_nt(result.astype(BF16), select).astype(BF16)
    first_a, first_b = grid.reduce_end(first_a), grid.reduce_end(first_b)
    out_fc1 = jnp.concatenate([first_a[0], first_a[1], first_b[0], first_b[1]], axis=1)
    out_fc2 = jnp.concatenate([first_a[2], first_a[3], first_b[2], first_b[3]], axis=1)
    out_c = grid.reduce_end(first_c)
    out_qkv = out_c[:3]
    if parts == 2:
        out_qkv = jnp.concatenate([out_qkv, sum_d], axis=2)
    out_proj = jnp.concatenate([out_c[3 + p] for p in range(parts)], axis=1)
    return (
        outputs,
        grad_inputs,
        small_grads[0],
        small_grads[1],
        out_qkv,
        out_proj.T,
        small_grads[4],
        small_grads[2],
        small_grads[3],
        out_fc1,
        small_grads[6:].reshape(-1)[:hidden_block],
        out_fc2.T,
        small_grads[5],
    )


def solution(mesh):
    in_specs = (
        P(("dp", "tensor"), None),
        P(("dp", "tensor"), None),
        P("dp"),
        P(("dp", "tensor")),
        P("dp"),
        P("dp"),
        P(None, "dp", "tensor"),
        P("tensor", "dp"),
        P("dp"),
        P("dp"),
        P("dp"),
        P("dp", "tensor"),
        P(("tensor", "dp")),
        P("tensor", "dp"),
        P("dp"),
    )
    out_specs = (
        P(("dp", "tensor"), None),
        P(("dp", "tensor"), None),
        P("dp"),
        P("dp"),
        P(None, "dp", "tensor"),
        P("tensor", "dp"),
        P("dp"),
        P("dp"),
        P("dp"),
        P("dp", "tensor"),
        P(("tensor", "dp")),
        P("tensor", "dp"),
        P("dp"),
    )
    return jax.shard_map(
        on_device, mesh=mesh, in_specs=in_specs, out_specs=out_specs, check_vma=False
    )
```

```python
import functools

import jax
import jax.numpy as jnp
import numpy as np
from jax import lax
from jax.experimental import pallas as pl
from jax.experimental.pallas import tpu as pltpu
from jax.sharding import PartitionSpec as P

HEAD_DIM = 64
SEQ_LEN = 1104
F32 = jnp.float32
BF16 = jnp.bfloat16
MIB = 2**20


def dp_factors(size):
    if size % 8 == 0:
        return (4, 2, size // 8)
    return (1, 1, size)


class DpGrid:
    def __init__(self, size, block):
        self.size = size
        self.block = block
        self.half = block // 2
        self.factors = dp_factors(size)
        self.routes = ((2, 1), (1, 2))

    def coords(self, index):
        _, second, third = self.factors
        return (index // (second * third), (index // third) % second, index % third)

    def index(self, coords):
        _, second, third = self.factors
        return (coords[0] * second + coords[1]) * third + coords[2]

    def ahead(self, index, axis, step):
        coords = list(self.coords(index))
        coords[axis] = (coords[axis] + step) % self.factors[axis]
        return self.index(coords)

    def fetch(self, value, axis, step):
        pairs = [(self.ahead(i, axis, step), i) for i in range(self.size)]
        return lax.ppermute(value, "dp", pairs)

    def push(self, value, axis, step):
        pairs = [(i, self.ahead(i, axis, step)) for i in range(self.size)]
        return lax.ppermute(value, "dp", pairs)

    def spread(self, shard):
        with jax.named_scope("gather_z"):
            return [shard] + [self.fetch(shard, 0, s) for s in range(1, self.factors[0])]

    def middle(self, along):
        halves = []
        for part, (middle, _) in enumerate(self.routes):
            rows = slice(part * self.half, (part + 1) * self.half)
            value = jnp.concatenate([a[..., rows, :] for a in along], axis=-2)
            steps = range(1, self.factors[middle])
            with jax.named_scope("gather_middle"):
                halves.append([value] + [self.fetch(value, middle, s) for s in steps])
        return halves

    def finish(self, halves):
        pieces = []
        for (_, last), parts in zip(self.routes, halves):
            value = jnp.concatenate(parts, axis=-2)
            pieces.append(value)
            with jax.named_scope("gather_last"):
                pieces.extend(self.fetch(value, last, s) for s in range(1, self.factors[last]))
        return pieces

    def gather(self, shard):
        return self.finish(self.middle(self.spread(shard)))

    def spread_middle(self, shard):
        parts = []
        for part, (middle, _) in enumerate(self.routes):
            value = shard[..., part * self.half : (part + 1) * self.half, :]
            with jax.named_scope("gather_middle"):
                steps = range(1, self.factors[middle])
                parts.append([value] + [self.fetch(value, middle, s) for s in steps])
        return parts

    def steps(self, value, axis, steps):
        with jax.named_scope("gather_step"):
            return [self.fetch(value, axis, s) for s in steps if s < self.factors[axis]]

    def halves_of(self, along, counts):
        halves, start = [], 0
        for count in counts:
            rows = slice(start, start + count * self.half)
            start += count * self.half
            value = jnp.stack([a[..., rows, :] for a in along], axis=-3)
            lead, wide = value.shape[:-3], value.shape[-1]
            value = value.reshape(lead + (self.factors[0], count, self.half, wide))
            value = jnp.swapaxes(value, -4, -3)
            halves.append([value.reshape(lead + (-1, wide))])
        return halves

    def reduce_last(self, pieces):
        pieces, halves = list(pieces), []
        for _, last in self.routes:
            mine, pieces = pieces[: self.factors[last]], pieces[self.factors[last] :]
            with jax.named_scope("reduce_last"):
                sent = [self.push(mine[s], last, s) for s in range(1, self.factors[last])]
            halves.append([mine[0]] + sent)
        return halves

    def reduce_middle(self, halves):
        rows, out = self.factors[0] * self.half, []
        for (middle, _), parts in zip(self.routes, halves):
            cut = [
                sum(p[..., s * rows : (s + 1) * rows, :].astype(F32) for p in parts).astype(BF16)
                for s in range(self.factors[middle])
            ]
            with jax.named_scope("reduce_middle"):
                sent = [self.push(cut[s], middle, s) for s in range(1, self.factors[middle])]
            out.append([cut[0]] + sent)
        return out

    def first_pieces(self, halves):
        def along(step):
            rows = slice(step * self.half, (step + 1) * self.half)
            totals = [sum(p[..., rows, :].astype(F32) for p in parts) for parts in halves]
            return jnp.concatenate(totals, axis=-2)

        return [along(0)] + [along(s).astype(BF16) for s in range(1, self.factors[0])]

    def send_first(self, pieces, steps):
        with jax.named_scope("reduce_z"):
            return [self.push(pieces[s], 0, s) for s in steps if s < len(pieces)]

    def reduce_first(self, halves):
        pieces = self.first_pieces(halves)
        return pieces[:1] + self.send_first(pieces, (1, 2, 3))

    def reduce_end(self, parts):
        return sum(p.astype(F32) for p in parts)

    def scatter(self, pieces):
        return self.reduce_end(self.reduce_first(self.reduce_middle(self.reduce_last(pieces))))

    def gather_small(self, value, axes):
        for axis in axes:
            with jax.named_scope("gather_small"):
                parts = [value] + [self.fetch(value, axis, s) for s in range(1, self.factors[axis])]
            value = jnp.concatenate(parts, axis=0)
        return value

    def small_in_order(self, value):
        zeroth, second, third = self.factors
        value = value.reshape((third, second, zeroth, value.shape[1], 2, self.half))
        first_half = value[..., 0, :].transpose(3, 1, 0, 2, 4)
        second_half = value[..., 1, :].transpose(3, 0, 1, 2, 4)
        count = value.shape[3]
        return jnp.concatenate(
            [first_half.reshape(count, -1), second_half.reshape(count, -1)], axis=1
        )

    def blocks_of(self, value):
        count, full = value.shape
        second, third = self.factors[1], self.factors[2]
        first_half = value[:, : full // 2].reshape(count, second, third, self.factors[0], self.half)
        second_half = value[:, full // 2 :].reshape(count, third, second, self.factors[0], self.half)
        return jnp.concatenate(
            [first_half.transpose(2, 1, 3, 0, 4), second_half.transpose(1, 2, 3, 0, 4)], axis=-1
        )

    def reduce_small(self, value, axis):
        value = value.astype(BF16)
        total = value[0].astype(F32)
        with jax.named_scope("reduce_small"):
            for step in range(1, self.factors[axis]):
                total = total + self.push(value[step], axis, step).astype(F32)
        return total

    def piece_rows(self):
        full = self.size * self.half
        rows = []
        for _, last in self.routes:
            rows.extend([full // self.factors[last]] * self.factors[last])
        return rows

    def cut(self, value, axis=0):
        edges = np.cumsum(self.piece_rows())[:-1].tolist()
        return jnp.split(value, edges, axis=axis)

    def places(self):
        return (self.features()[:: self.half] // self.half).astype(jnp.int32)

    def features(self):
        here = self.coords(lax.axis_index("dp"))
        indices = []
        for part, (middle, last) in enumerate(self.routes):
            shape = (self.factors[last], self.factors[middle], self.factors[0], self.half)
            steps = [None, None, None]
            steps[last], steps[middle], steps[0], sub = (
                jnp.asarray(g.reshape(-1), jnp.int32) for g in np.indices(shape)
            )
            coords = [(h + s) % f for h, s, f in zip(here, steps, self.factors)]
            indices.append(self.index(coords) * self.block + part * self.half + sub)
        return jnp.concatenate(indices)


class TensorPair:
    def __init__(self, size, slot_count, local_rows):
        self.size = size
        self.relative = size == 2 and slot_count == 1
        self.local_rows = local_rows

    def swap(self, value):
        return lax.ppermute(value, "tensor", [(0, 1), (1, 0)])

    def parts(self, value):
        if self.relative:
            return [value, self.swap(value)]
        return [lax.all_gather(value, "tensor", axis=0, tiled=True)]

    def whole(self, value):
        return jnp.concatenate(self.parts(value), axis=0)

    def own(self, value):
        if self.relative:
            return value[: self.local_rows]
        start = lax.axis_index("tensor") * self.local_rows
        return lax.dynamic_slice_in_dim(value, start, self.local_rows, axis=0)

    def both(self, value):
        if self.relative:
            return value, self.swap(value)
        return lax.psum(value.astype(F32), "tensor"), jnp.zeros((1, value.shape[1]), F32)

    def own_both(self, halves):
        if self.relative:
            return halves[0], self.swap(halves[1])
        value = jnp.concatenate(halves, axis=0)
        total = lax.psum_scatter(value, "tensor", scatter_dimension=0, tiled=True)
        return total, jnp.zeros((1, value.shape[1]), F32)

    def small_total(self, value):
        if self.size == 2:
            return value + self.swap(value)
        return lax.psum(value, "tensor")


def join(*groups):
    flat, tree = jax.tree.flatten(groups)
    return jax.tree.unflatten(tree, lax.optimization_barrier(tuple(flat)))


def normalize(values):
    row_mean = jnp.mean(values, axis=-1, keepdims=True)
    centered = values - row_mean
    variance = jnp.mean(centered * centered, axis=-1, keepdims=True)
    inverse = lax.rsqrt(variance + 1e-05)
    return centered * inverse, inverse


def norm_input_grad(grad, gain, normed, inverse):
    scaled = grad * gain
    first = jnp.mean(scaled, axis=-1, keepdims=True)
    second = jnp.mean(scaled * normed, axis=-1, keepdims=True)
    return inverse * (scaled - first - normed * second)


def dot_nn(left, right):
    return lax.dot_general(left, right, (((1,), (0,)), ((), ())), preferred_element_type=F32)


def dot_nt(left, right):
    return lax.dot_general(left, right, (((1,), (1,)), ((), ())), preferred_element_type=F32)


def dot_tn(left, right):
    return lax.dot_general(left, right, (((0,), (0,)), ((), ())), preferred_element_type=F32)


def gelu_and_slope(values):
    cdf = 0.5 + 0.5 * lax.erf(values * (0.5**0.5))
    density = jnp.exp(-0.5 * values * values) * 0.3989422804014327
    return values * cdf, cdf + values * density


def params(limit):
    return pltpu.CompilerParams(vmem_limit_bytes=limit * MIB)


def cost(micros):
    return pl.CostEstimate(
        flops=int(micros * 1e9), transcendentals=0, bytes_accessed=int(micros * 1e6)
    )


def whole_spec(array):
    return pl.BlockSpec(array.shape, lambda *grid: (0,) * len(array.shape))


def stack_rows(refs):
    return jnp.concatenate([r[...] for r in refs], axis=0)


def head_lanes(seq, head):
    lane = lax.broadcasted_iota(jnp.int32, (seq, 2 * HEAD_DIM), 1)
    mine = (lane >= HEAD_DIM) if head else (lane < HEAD_DIM)
    return mine, lane == (0 if head else HEAD_DIM)


def head_operands(query_ref, key_ref, invalid, head):
    seq = query_ref.shape[0]
    mine, extra = head_lanes(seq, head)
    one, zero = jnp.asarray(1, BF16), jnp.asarray(0, BF16)
    scaled = query_ref[...] * jnp.asarray(HEAD_DIM**-0.5, BF16)
    query = jnp.where(mine, scaled, jnp.where(extra, one, zero))
    keys = jnp.where(mine, key_ref[...], jnp.where(extra, invalid, zero))
    return query, keys


def key_column(invalid_ref):
    seq = invalid_ref.shape[-1]
    return jnp.broadcast_to(invalid_ref[0], (2 * HEAD_DIM, seq)).T.astype(BF16)


def attend_kernel(query_ref, key_ref, value_ref, invalid_ref, mixed_ref, total_ref, turned_ref):
    seq = query_ref.shape[0]
    invalid = key_column(invalid_ref)
    values = value_ref[...].T
    for head in range(2):
        rows = slice(head * HEAD_DIM, (head + 1) * HEAD_DIM)
        query, keys = head_operands(query_ref, key_ref, invalid, head)
        with_ones = jnp.concatenate([values[rows], jnp.ones((16, seq), BF16)], axis=0)
        scores = dot_nt(keys, query)
        largest = jnp.max(scores, axis=0, keepdims=True)
        weights = jnp.exp(scores - largest)
        mixed = dot_nn(with_ones, weights.astype(BF16))
        weight_sum = mixed[HEAD_DIM : HEAD_DIM + 1]
        turned_ref[rows] = mixed[:HEAD_DIM] * (1.0 / weight_sum)
        total_ref[0, 0, head : head + 1] = largest + jnp.log(weight_sum)
    mixed_ref[...] = turned_ref[...].T.astype(BF16)


def attend_back_kernel(
    query_ref,
    key_ref,
    value_ref,
    invalid_ref,
    mixed_ref,
    total_ref,
    grad_ref,
    grad_query_ref,
    grad_key_ref,
    grad_value_ref,
    turned_ref,
):
    seq = query_ref.shape[0]
    invalid = key_column(invalid_ref)
    keys_turned = key_ref[...].T
    product = mixed_ref[...].astype(F32).T * grad_ref[...].astype(F32).T
    for head in range(2):
        rows = slice(head * HEAD_DIM, (head + 1) * HEAD_DIM)
        mine, _ = head_lanes(seq, head)
        query, keys = head_operands(query_ref, key_ref, invalid, head)
        grad = jnp.where(mine, grad_ref[...], jnp.asarray(0, BF16))
        row_dot = jnp.sum(product[rows], axis=0, keepdims=True)
        prob = jnp.exp(dot_nt(keys, query) - total_ref[0, 0, head : head + 1])
        grad_prob = dot_nt(value_ref[...], grad) - row_dot
        grad_score = (prob * grad_prob).astype(BF16)
        turned_ref[rows] = dot_nn(keys_turned[rows], grad_score) * HEAD_DIM**-0.5
        grad_value = dot_nn(prob.astype(BF16), grad)
        grad_key = dot_nn(grad_score, jnp.where(mine, query, jnp.asarray(0, BF16)))
        if head == 0:
            first_value, first_key = grad_value, grad_key
    grad_value_ref[...] = (first_value + grad_value).astype(BF16)
    grad_key_ref[...] = (first_key + grad_key).astype(BF16)
    grad_query_ref[...] = turned_ref[...].T.astype(BF16)


def attend_specs():
    def columns(offset):
        return pl.BlockSpec((SEQ_LEN, 2 * HEAD_DIM), lambda s, p: (s, p + offset))

    invalid = pl.BlockSpec((1, 1, SEQ_LEN), lambda s, p: (s, 0, 0))
    total = pl.BlockSpec((1, 1, 2, SEQ_LEN), lambda s, p: (s, p, 0, 0))
    return columns, invalid, total


def attend(packed, invalid, first, count):
    slots, pairs = invalid.shape[0], packed.shape[1] // (6 * HEAD_DIM)
    columns, invalid_spec, total_spec = attend_specs()
    return pl.pallas_call(
        attend_kernel,
        grid=(slots, count),
        in_specs=[columns(first), columns(pairs + first), columns(2 * pairs + first), invalid_spec],
        out_specs=[columns(0), total_spec],
        out_shape=[
            jax.ShapeDtypeStruct((packed.shape[0], count * 2 * HEAD_DIM), BF16),
            jax.ShapeDtypeStruct((slots, count, 2, SEQ_LEN), F32),
        ],
        scratch_shapes=[pltpu.VMEM((2 * HEAD_DIM, SEQ_LEN), F32)],
        compiler_params=params(14),
        cost_estimate=cost(4 * slots * count),
        name="attend",
    )(packed, packed, packed, invalid)


def attend_back(packed, invalid, mixed, total, grad_mixed, first, count):
    slots, pairs = invalid.shape[0], packed.shape[1] // (6 * HEAD_DIM)
    columns, invalid_spec, _ = attend_specs()
    return pl.pallas_call(
        attend_back_kernel,
        grid=(slots, count),
        in_specs=[
            columns(first),
            columns(pairs + first),
            columns(2 * pairs + first),
            invalid_spec,
            columns(first),
            pl.BlockSpec((1, 1, 2, SEQ_LEN), lambda s, p: (s, p + first, 0, 0)),
            columns(first),
        ],
        out_specs=[columns(0)] * 3,
        out_shape=[jax.ShapeDtypeStruct((mixed.shape[0], count * 2 * HEAD_DIM), BF16)] * 3,
        scratch_shapes=[
            pltpu.VMEM((2 * HEAD_DIM, SEQ_LEN), F32),
        ],
        compiler_params=params(36),
        cost_estimate=cost(9 * slots * count),
        name="attend_back",
    )(packed, packed, packed, invalid, mixed, total, grad_mixed)


def joined(pieces, first, count):
    return jnp.concatenate(
        [jnp.concatenate([p[g] for p in pieces], axis=0) for g in range(first, first + count)],
        axis=1,
    )


def times_pieces(rows, pieces, first, count, fits):
    if not fits:
        return dot_nn(rows, joined(pieces, first, count)).astype(BF16)
    wide = pieces[0].shape[2]

    def kernel(rows_ref, *refs):
        weight = jnp.concatenate([r[0] for r in refs[:-1]], axis=0)
        refs[-1][...] = dot_nn(rows_ref[...], weight).astype(BF16)

    return pl.pallas_call(
        kernel,
        grid=(count,),
        in_specs=[whole_spec(rows)]
        + [pl.BlockSpec((1, p.shape[1], wide), lambda j: (first + j, 0, 0)) for p in pieces],
        out_specs=pl.BlockSpec((rows.shape[0], wide), lambda j: (0, j)),
        out_shape=jax.ShapeDtypeStruct((rows.shape[0], count * wide), BF16),
        compiler_params=params(12),
        cost_estimate=cost(2 * count),
        name="times_pieces",
    )(rows, *pieces)


def times_pieces_turned(columns, pieces, places, fits, cuts=1):
    count = len(columns)
    rows, wide = columns[0].shape
    if not fits:
        weight = [joined(pieces, g, 1)[:, c * wide : (c + 1) * wide] for g, c in places]
        total = dot_nt(jnp.concatenate(columns, axis=1), jnp.concatenate(weight, axis=1))
        return jnp.split(total.astype(BF16), cuts) if cuts > 1 else total.astype(BF16)
    starts = np.cumsum([0] + [p.shape[1] for p in pieces]).tolist()

    def kernel(*refs):
        lefts, weights, out_refs = refs[:count], refs[count:-cuts], refs[-cuts:]
        left = jnp.concatenate([r[...] for r in lefts], axis=1)
        weight = jnp.concatenate(
            [
                jnp.concatenate([r[0] for r in weights[i * count : (i + 1) * count]], axis=1)
                for i in range(len(pieces))
            ],
            axis=0,
        )
        for k, out_ref in enumerate(out_refs):
            cut = slice(k * rows // cuts, (k + 1) * rows // cuts)
            out_ref[...] = dot_nt(left[cut], weight).astype(BF16)

    def place_spec(piece, group, column):
        return pl.BlockSpec((1, piece.shape[1], wide), lambda i: (group, 0, column))

    outs = pl.pallas_call(
        kernel,
        grid=(1,),
        in_specs=[whole_spec(c) for c in columns] + [place_spec(p, *q) for p in pieces for q in places],
        out_specs=[pl.BlockSpec((rows // cuts, starts[-1]), lambda i: (0, 0))] * cuts,
        out_shape=[jax.ShapeDtypeStruct((rows // cuts, starts[-1]), BF16)] * cuts,
        compiler_params=params(16),
        cost_estimate=cost(1 + count),
        name="times_pieces_turned",
    )(*columns, *[p for p in pieces for _ in places])
    return outs if cuts > 1 else outs[0]


def weight_grads(lefts, rights, piece_rows, fits):
    wide = rights[0].shape[1]
    rights = [r if isinstance(r, tuple) else (r, 0) for r in rights]
    starts = np.cumsum([0] + piece_rows).tolist()
    if not fits:
        blocks = [a[:, c * wide : (c + 1) * wide] for a, c in rights]
        full = jnp.stack([dot_tn(a, b).astype(BF16) for a, b in zip(lefts, blocks)])
        return [full[:, s:e] for s, e in zip(starts, starts[1:])]
    count = len(rights)
    names = []
    for left in lefts:
        if not any(left is other for other in names):
            names.append(left)
    which = [next(i for i, o in enumerate(names) if o is left) for left in lefts]

    def kernel(*refs):
        left_refs, right_refs = refs[: len(names)], refs[len(names) : len(names) + count]
        out_refs = refs[len(names) + count :]
        turned = [r[...].T for r in left_refs]
        for k in range(count):
            product = dot_nn(turned[which[k]], right_refs[k][...]).astype(BF16)
            for i, (start, end) in enumerate(zip(starts, starts[1:])):
                out_refs[i][k] = product[start:end]

    return pl.pallas_call(
        kernel,
        grid=(1,),
        in_specs=[whole_spec(a) for a in names]
        + [pl.BlockSpec((a.shape[0], wide), lambda i, c=c: (0, c)) for a, c in rights],
        out_specs=[pl.BlockSpec((count, r, wide), lambda i: (0, 0, 0)) for r in piece_rows],
        out_shape=[jax.ShapeDtypeStruct((count, r, wide), BF16) for r in piece_rows],
        compiler_params=params(20),
        cost_estimate=cost(1 + 1.5 * count),
        name="weight_grads",
    )(*names, *[a for a, _ in rights])


def joined_rows(parts):
    return parts[0] if len(parts) == 1 else jnp.concatenate(parts, axis=0)


def first_norm(rows_in, gain, bias, fits):
    width = rows_in[0].shape[1]
    rows = sum(p.shape[0] for p in rows_in)

    def work(values, gain, bias):
        normed, _ = normalize(values.astype(F32))
        return (normed * gain + bias).astype(BF16)

    if not fits:
        return work(joined_rows(rows_in), gain, bias)

    def kernel(*refs):
        gain, bias, out_ref = refs[-3][...], refs[-2][...], refs[-1]
        start = 0
        for ref in refs[:-3]:
            out_ref[start : start + ref.shape[0]] = work(ref[...], gain, bias)
            start += ref.shape[0]

    return pl.pallas_call(
        kernel,
        out_shape=jax.ShapeDtypeStruct((rows, width), BF16),
        compiler_params=params(12),
        cost_estimate=cost(3),
        name="first_norm",
    )(*rows_in, gain, bias)


def second_norm(rows_in, live, mine, other, shift, gain, bias, fits):
    rows, width = mine.shape

    def work(rows_in, live, mine, other, shift, gain, bias):
        branch = mine.astype(F32) + other.astype(F32) + shift
        middle = rows_in.astype(F32) + live * branch
        normed, _ = normalize(middle)
        return middle, (normed * gain + bias).astype(BF16)

    if not fits:
        return work(joined_rows(rows_in), live, mine, other, shift, gain, bias)
    half = rows // 2

    def kernel(own_ref, next_ref, *refs):
        rows_in = jnp.where(pl.program_id(0) == 0, own_ref[...], next_ref[...])
        refs[-2][...], refs[-1][...] = work(rows_in, *[r[...] for r in refs[:-2]])

    def block(columns, place=lambda i: i):
        return pl.BlockSpec((half, columns), lambda i: (place(i), 0))

    return pl.pallas_call(
        kernel,
        grid=(2,),
        in_specs=[
            block(width, lambda i: 0),
            block(width, lambda i: 0),
            block(1),
            block(width),
            block(width, lambda i: 1 - i),
        ]
        + [whole_spec(shift)] * 3,
        out_specs=[block(width), block(width)],
        out_shape=[
            pltpu.HBM((rows, width), F32),
            jax.ShapeDtypeStruct((rows, width), BF16),
        ],
        compiler_params=params(40),
        cost_estimate=cost(4),
        name="second_norm",
    )(*rows_in, live, mine, other, shift, gain, bias)


def norm_back(grad_out, live, mine, other, middle, gain, fits):
    rows, width = middle.shape

    def work(grad_out, live, mine, other, middle, gain):
        grad_out = grad_out.astype(F32)
        grad = mine.astype(F32) + other.astype(F32)
        normed, inverse = normalize(middle)
        grad_middle = grad_out + norm_input_grad(grad, gain, normed, inverse)
        grad_branch = (live * grad_middle).astype(BF16)
        sums = [grad * normed, grad, grad_branch.astype(F32), grad_out]
        sums = jnp.concatenate([jnp.sum(s, axis=0, keepdims=True) for s in sums], axis=0)
        return grad_middle, grad_branch, sums

    if not fits:
        return work(joined_rows(grad_out), live, mine, other, middle, gain)
    half = rows // 2

    def kernel(own_ref, next_ref, live_ref, mine_ref, other_ref, middle_ref, gain_ref, *refs):
        step = pl.program_id(0)
        grad = jnp.where(step == 0, own_ref[...], next_ref[...])
        rest = [r[...] for r in (live_ref, mine_ref, other_ref, middle_ref, gain_ref)]
        grad_middle, refs[1][...], sums = work(grad, *rest)

        @pl.when(step == 0)
        def _():
            refs[0][...] = grad_middle
            refs[2][...] = sums

        @pl.when(step == 1)
        def _():
            refs[2][...] += sums

    def block(columns, place=lambda i: i):
        return pl.BlockSpec((half, columns), lambda i: (place(i), 0))

    return pl.pallas_call(
        kernel,
        grid=(2,),
        in_specs=[
            block(width, lambda i: 0),
            block(width, lambda i: 0),
            block(1),
            block(width),
            block(width, lambda i: 1 - i),
            block(width),
            whole_spec(gain),
        ],
        out_specs=[
            block(width, lambda i: 0),
            block(width),
            pl.BlockSpec((4, width), lambda i: (0, 0)),
        ],
        out_shape=[
            jax.ShapeDtypeStruct((half, width), F32),
            jax.ShapeDtypeStruct((rows, width), BF16),
            jax.ShapeDtypeStruct((4, width), F32),
        ],
        compiler_params=params(44),
        cost_estimate=cost(7),
        name="norm_back",
    )(*grad_out, live, mine, other, middle, gain)


def first_norm_back(grad_middle, rest, mine, other, rows_in, gain, fits):
    rows, width = rows_in.shape

    def work(grad_middle, rest, mine, other, rows_in, gain):
        grad = mine.astype(F32) + other.astype(F32)
        normed, inverse = normalize(rows_in.astype(F32))
        grad_rows = grad_middle + rest.astype(F32) + norm_input_grad(grad, gain, normed, inverse)
        sums = [jnp.sum(s, axis=0, keepdims=True) for s in (grad * normed, grad)]
        return grad_rows.astype(BF16), jnp.concatenate(sums, axis=0)

    if not fits:
        return work(grad_middle, rest, mine, other, rows_in, gain)

    def kernel(*refs):
        refs[-2][...], refs[-1][...] = work(*[r[...] for r in refs[:-2]])

    own = pl.BlockSpec((rows, width), lambda i: (0, 0))
    return pl.pallas_call(
        kernel,
        grid=(1,),
        in_specs=[own] * 5 + [pl.BlockSpec((1, width), lambda i: (0, 0))],
        out_specs=[own, pl.BlockSpec((2, width), lambda i: (0, 0))],
        out_shape=[
            jax.ShapeDtypeStruct((rows, width), BF16),
            jax.ShapeDtypeStruct((2, width), F32),
        ],
        compiler_params=params(14),
        cost_estimate=cost(4),
        name="first_norm_back",
    )(grad_middle, rest, mine, other, rows_in, gain)


def feed_kernel(counts, carried, *refs):
    halves, pieces, grad_pieces = counts
    normed_ref, shift_ref, grad_refs = refs[0], refs[1], refs[2 : 2 + halves]
    refs = refs[2 + halves :]
    first_refs, second_refs, refs = refs[:pieces], refs[pieces : 2 * pieces], refs[2 * pieces :]
    before, refs = (refs[:2], refs[2:]) if carried else ((), refs)
    out_ref, grad_two_ref, shift_grad_ref = refs[:3]
    weight_grad_refs = refs[3 : 3 + grad_pieces]
    grad_ref, normed_turned, grad_turned, out_sum, grad_sum = refs[3 + grad_pieces :]
    step = pl.program_id(0)
    @pl.when(step == 0)
    def _():
        start = 0
        for ref in grad_refs:
            grad_ref[start : start + ref.shape[0]] = ref[...]
            start += ref.shape[0]
        normed_turned[...] = normed_ref[...].T
        grad_turned[...] = grad_ref[...].T

    first = jnp.concatenate([w[0] for w in first_refs], axis=0)
    second = jnp.concatenate([w[0] for w in second_refs], axis=0)
    hidden = dot_nn(normed_ref[...], first) + shift_ref[...]
    hidden_act, slope = gelu_and_slope(hidden)
    hidden_act = hidden_act.astype(BF16)
    grad_pre = (dot_nn(grad_ref[...], second) * slope).astype(BF16)
    shift_grad_ref[...] = jnp.sum(grad_pre.astype(F32), axis=0, keepdims=True)
    last = pl.num_programs(0) - 1
    products = (
        (out_sum, out_ref, hidden_act, second, before[:1]),
        (grad_sum, grad_two_ref, grad_pre, first, before[1:]),
    )

    @pl.when(step == 0)
    def _():
        for sum_ref, _, left, right, start in products:
            product = dot_nt(left, right)
            sum_ref[...] = product + start[0][...].astype(F32) if carried else product

    @pl.when(step == last)
    def _():
        for sum_ref, end_ref, left, right, _ in products:
            end_ref[...] = (sum_ref[...] + dot_nt(left, right)).astype(BF16)

    if True:
        for k, (left, right) in enumerate(
            ((normed_turned, grad_pre), (grad_turned, hidden_act))
        ):
            product, start = dot_nn(left[...], right).astype(BF16), 0
            for ref in weight_grad_refs:
                ref[k, 0] = product[start : start + ref.shape[2]]
                start += ref.shape[2]


def feed_forward(normed, grads, shift, weight, places, piece_rows, before, fits):
    rows, width = normed.shape
    plain, scattered = not isinstance(weight, list), piece_rows is None
    units = shift.shape[1]
    wide = units if plain else weight[0].shape[2]
    groups = units // wide
    if not fits:
        size = width // places.shape[0]
        order = (places[:, None] * size + jnp.arange(size)[None, :]).reshape(-1)
        if plain:
            both = jnp.take(weight, order, axis=0)
            first_w, second_w = both[:, :units], both[:, units:]
        else:
            first_w, second_w = joined(weight, 0, groups), joined(weight, groups, groups)
        grad = jnp.concatenate(grads, axis=0)
        hidden_act, slope = gelu_and_slope(dot_nn(normed, first_w) + shift)
        hidden_act = hidden_act.astype(BF16)
        grad_pre = (dot_nn(grad, second_w) * slope).astype(BF16)
        out, grad_two = dot_nt(hidden_act, second_w), dot_nt(grad_pre, first_w)
        if before:
            out, grad_two = out + before[0].astype(F32), grad_two + before[1].astype(F32)
        outs = [dot_tn(normed, grad_pre).astype(BF16), dot_tn(grad, hidden_act).astype(BF16)]
        if scattered:
            outs = [jnp.zeros_like(g).at[order].set(g) for g in outs]
        else:
            size = units // 2
            outs = jnp.stack([g[:, k * size : (k + 1) * size] for g in outs for k in range(2)])
            outs = jnp.split(outs, np.cumsum(piece_rows)[:-1].tolist(), 1)
        shift_grad = jnp.sum(grad_pre, axis=0, dtype=F32, keepdims=True)
        return [out.astype(BF16), grad_two.astype(BF16), shift_grad] + outs

    tile = units // 2
    per = wide // tile
    pieces = [weight] if plain else weight

    def once(array):
        return pl.BlockSpec(
            array.shape, lambda j: (0,) * len(array.shape), pipeline_mode=pl.Buffered(1)
        )

    def weight_spec(piece, second):
        if plain:
            return pl.BlockSpec((width, tile), lambda j: (0, second * per + j))
        return pl.BlockSpec(
            (1, piece.shape[1], tile), lambda j: (second * groups + j // per, 0, j % per)
        )

    if scattered:
        grad_specs = [pl.BlockSpec((width, tile), lambda j: (0, j))] * 2
        grad_shapes = [jax.ShapeDtypeStruct((width, units), BF16)] * 2
    else:
        half = units // 2
        split = half // tile
        grad_specs = [
            pl.BlockSpec((2, 1, r, tile), lambda j: (0, j // split, 0, j % split))
            for r in piece_rows
        ]
        grad_shapes = [pltpu.HBM((2, 2, r, half), BF16) for r in piece_rows]
    before = tuple(before)
    outs = pl.pallas_call(
        functools.partial(
            feed_kernel,
            (len(grads), len(pieces), len(grad_shapes)),
            bool(before),
        ),
        grid_spec=pltpu.PrefetchScalarGridSpec(
            num_scalar_prefetch=0,
            grid=(units // tile,),
            in_specs=[once(normed), pl.BlockSpec((1, tile), lambda j: (0, j))]
            + [once(g) for g in grads]
            + [weight_spec(p, 0) for p in pieces]
            + [weight_spec(p, 1) for p in pieces]
            + [once(b) for b in before],
            out_specs=[
                pl.BlockSpec((rows, width), lambda j: (0, 0)),
                pl.BlockSpec((rows, width), lambda j: (0, 0)),
                pl.BlockSpec((1, tile), lambda j: (0, j)),
            ]
            + grad_specs,
            scratch_shapes=[
                pltpu.VMEM((rows, width), BF16),
                pltpu.VMEM((width, rows), BF16),
                pltpu.VMEM((width, rows), BF16),
                pltpu.VMEM((rows, width), F32),
                pltpu.VMEM((rows, width), F32),
            ],
        ),
        out_shape=[
            pltpu.HBM((rows, width), BF16),
            pltpu.HBM((rows, width), BF16),
            jax.ShapeDtypeStruct((1, units), F32),
        ]
        + grad_shapes,
        compiler_params=params(44),
        cost_estimate=cost(25),
        name="feed_forward",
    )(normed, shift, *grads, *pieces, *pieces, *before)
    outs = list(outs)
    if not scattered:
        outs[3:] = [g.reshape((4,) + g.shape[2:]) for g in outs[3:]]
    return outs


def on_device(
    inputs,
    cotangent,
    slot_live,
    token_type,
    attn_norm_gain,
    attn_norm_bias,
    qkv_weight,
    proj_weight,
    proj_bias,
    mlp_norm_gain,
    mlp_norm_bias,
    fc1_weight,
    fc1_bias,
    fc2_weight,
    fc2_bias,
):
    dp_size = lax.axis_size("dp")
    tensor_size = lax.axis_size("tensor")
    local_rows, width = inputs.shape
    slot_count = slot_live.shape[0]
    whole_rows = local_rows * tensor_size
    block = fc1_weight.shape[0]
    width_here = qkv_weight.shape[2]
    hidden_here = fc1_weight.shape[1]
    hidden_block = fc1_bias.shape[0]
    hidden_cut = hidden_here // 2
    fits = whole_rows <= 2048
    grid = DpGrid(dp_size, block)
    pair = TensorPair(tensor_size, slot_count, local_rows)
    half_cut = hidden_cut // 2

    bias_columns = -(-hidden_block // block)
    bias_pad = bias_columns * block - hidden_block
    smalls = jnp.stack(
        (attn_norm_gain, attn_norm_bias, proj_bias, mlp_norm_gain, mlp_norm_bias, fc2_bias)
    )
    bias_block = jnp.pad(fc1_bias, (0, bias_pad)).reshape(bias_columns, block)
    smalls = jnp.concatenate([smalls, bias_block], axis=0)
    fc2_turned = fc2_weight.T
    cuts = slice(0, hidden_cut), slice(hidden_cut, hidden_here)
    groups = [
        w[:, start : start + half_cut]
        for w in (fc1_weight, fc2_turned)
        for start in (0, half_cut)
    ]
    first_shard = jnp.stack(groups)
    second_shard = jnp.stack(
        [
            w[:, start : start + half_cut]
            for w in (fc1_weight, fc2_turned)
            for start in (hidden_cut, hidden_cut + half_cut)
        ]
    )
    attn_shard = jnp.concatenate([qkv_weight, proj_weight.T[None]], axis=0)
    count = smalls.shape[0]
    spare = ((0, 3), (0, 0), (0, width_here - block))
    attn_shard = jnp.concatenate([attn_shard, jnp.pad(smalls[None], spare)], axis=1)

    attn_along = grid.spread(attn_shard)
    smalls = jnp.stack([a[0, block:, :block] for a in attn_along])
    second_parts = grid.spread_middle(second_shard)
    attn_along, smalls, second_parts, first_shard, inputs, cotangent = join(
        attn_along, smalls, second_parts, first_shard, inputs, cotangent
    )

    attn_halves = grid.middle(attn_along)
    smalls = grid.gather_small(smalls, (1, 2))
    second_own = jnp.concatenate(second_parts[0] + second_parts[1], axis=-2)
    second_counts = [len(p) for p in second_parts]
    features, places = grid.features(), grid.places()
    select = (jnp.arange(width, dtype=jnp.int32)[:, None] == features[None, :]).astype(BF16)
    own_in = dot_nn(inputs, select).astype(BF16)
    own_in, first_shard = join(own_in, first_shard)
    first_along = [first_shard] + grid.steps(first_shard, 0, (1,))
    rows_in = pair.parts(own_in)
    own_grad = dot_nn(cotangent, select)
    live_col = jnp.repeat(slot_live.astype(F32), SEQ_LEN)[:, None]
    own_live = pair.own(live_col)
    grad_mlp = pair.parts((own_live * own_grad).astype(BF16))
    rest_grad = ((1.0 - own_live) * own_grad).astype(BF16)
    valid_whole = pair.whole((token_type != 3).astype(F32))
    invalid = jnp.where(valid_whole > 0, 0.0, -1e30).reshape(slot_count, 1, SEQ_LEN)
    attn_halves, first_along, second_own, smalls = join(
        attn_halves, first_along, second_own, smalls
    )

    attn_pieces = grid.finish(attn_halves)
    first_along += grid.steps(first_along[0], 0, (2, 3))
    smalls = grid.small_in_order(smalls)
    gain_one, shift_one, proj_shift, gain_two, shift_two, fc2_shift = (
        smalls[i : i + 1].astype(F32) for i in range(6)
    )
    fc1_shift = dot_nt(smalls[6:], select).reshape(bias_columns, dp_size, block)
    fc1_shift = fc1_shift.transpose(1, 0, 2).reshape(dp_size, bias_columns * block)
    fc1_shift = fc1_shift[:, :hidden_block].reshape(1, hidden_here)
    norm_one = first_norm(rows_in, gain_one, shift_one, fits)
    attn_pieces, first_along, norm_one, second_own, grad_mlp, invalid = join(
        attn_pieces, first_along, norm_one, second_own, grad_mlp, invalid
    )

    first_halves = grid.middle(first_along)
    second_along = [second_own] + grid.steps(second_own, 0, (1,))
    packed = times_pieces(norm_one, attn_pieces, 0, 3, fits)
    pairs = width_here // (2 * HEAD_DIM)
    parts = 2 if pairs % 2 == 0 else 1
    share = pairs // parts
    first_halves, second_along, packed, attn_pieces, norm_one = join(
        first_halves, second_along, packed, attn_pieces, norm_one
    )

    first_pieces = grid.finish(first_halves)
    second_along += grid.steps(second_along[0], 0, (2,))
    mixed, total = attend(packed, invalid, 0, pairs)
    attn_out = times_pieces_turned([mixed], attn_pieces, [(3, 0)], fits)
    first_pieces, second_along, attn_out = join(first_pieces, second_along, attn_out)

    second_along += grid.steps(second_along[0], 0, (3,))
    middle, norm_two = second_norm(
        rows_in, live_col, *pair.both(attn_out), proj_shift, gain_two, shift_two, fits
    )
    first_pieces, second_along, middle, norm_two = join(
        first_pieces, second_along, middle, norm_two
    )

    second_pieces = grid.finish(grid.halves_of(second_along, second_counts))
    piece_rows = grid.piece_rows()
    shifts = [fc1_shift[:, :hidden_cut], fc1_shift[:, hidden_cut:]]
    feed_a = feed_forward(
        norm_two, grad_mlp, shifts[0], first_pieces, places, piece_rows, (), fits
    )
    second_pieces, feed_a, norm_two = join(second_pieces, feed_a, norm_two)

    last_a = grid.reduce_last(feed_a[3:])
    feed_b = feed_forward(
        norm_two, grad_mlp, shifts[1], second_pieces, places, piece_rows, feed_a[:2], fits
    )
    grad_fc1_bias = jnp.concatenate([feed_a[2], feed_b[2]], axis=1)
    last_a, feed_b = join(last_a, feed_b)
    mlp_out, grad_two = feed_b[:2]

    middle_a = grid.reduce_middle(last_a)
    grad_middle, grad_branch, sums = norm_back(
        grad_mlp, live_col, *pair.both(grad_two), middle, gain_two, fits
    )
    grad_branch, pieces_b = join(grad_branch, feed_b[3:])
    last_b = grid.reduce_last(pieces_b)
    grad_mixed = times_pieces(grad_branch, attn_pieces, 3, 1, fits)
    middle_a, grad_mixed, mlp_out = join(middle_a, grad_mixed, mlp_out)

    def back(part):
        packed_late, mixed_late, total_late, late = join(packed, mixed, total, grad_mixed)
        return attend_back(
            packed_late, invalid, mixed_late, total_late, late, part * share, share
        )

    def grads(part, columns):
        lefts, rights = (norm_one,) * 3, tuple(columns)
        if part == 0:
            lefts = lefts + (grad_branch,) * parts
            rights = rights + tuple((mixed, p) for p in range(parts))
        return weight_grads(lefts, rights, piece_rows, fits)

    pieces_a = grid.first_pieces(middle_a)
    first_a = grid.send_first(pieces_a, (1, 3))
    columns = back(0)
    mlp_out = pair.own_both(jnp.split(mlp_out, 2) if pair.relative else [mlp_out])
    last_b, first_a, pieces_a, columns, grad_mixed, mlp_out = join(
        last_b, first_a, pieces_a, columns, grad_mixed, mlp_out
    )

    middle_b = grid.reduce_middle(last_b)
    first_a = pieces_a[:1] + first_a + grid.send_first(pieces_a, (2,))
    pieces_c = grads(0, columns)
    middle_b, pieces_c, grad_mixed, first_a = join(middle_b, pieces_c, grad_mixed, first_a)

    last_c = grid.reduce_last(pieces_c)
    pieces_b = grid.first_pieces(middle_b)
    first_b = grid.send_first(pieces_b, (1, 3))
    pieces_d, places_c = (), [(j, p) for p in range(parts) for j in range(3)]
    if parts == 2:
        more = back(1)
        last_c, first_b, pieces_b, more = join(last_c, first_b, pieces_b, more)
        columns = columns + more
        pieces_d = grads(1, more)

    middle_c = grid.reduce_middle(last_c)
    first_b = pieces_b[:1] + first_b + grid.send_first(pieces_b, (2,))
    grad_one = times_pieces_turned(columns, attn_pieces, places_c, fits, 2)
    middle_c, first_b, pieces_d, grad_one = join(middle_c, first_b, pieces_d, grad_one)

    last_d = grid.reduce_last(pieces_d) if parts == 2 else ()
    first_c = grid.reduce_first(middle_c)
    grad_rows, sums_one = first_norm_back(
        grad_middle if fits else pair.own(grad_middle),
        rest_grad,
        *pair.own_both(grad_one),
        own_in,
        gain_one,
        fits,
    )
    sums_one = pair.small_total(sums_one)
    last_d, sums_one, grad_rows = join(last_d, sums_one, grad_rows)

    middle_d = grid.reduce_middle(last_d) if parts == 2 else ()
    bias_grads = grad_fc1_bias.astype(BF16).reshape(dp_size, hidden_block)
    bias_grads = jnp.pad(bias_grads, ((0, 0), (0, bias_pad))).reshape(dp_size, bias_columns, block)
    bias_grads = dot_nn(bias_grads.transpose(1, 0, 2).reshape(bias_columns, width), select)
    small_grads = jnp.concatenate([sums_one, sums, bias_grads], axis=0)
    small_grads = grid.blocks_of(small_grads)
    small_grads, grad_rows, _ = join(small_grads, grad_rows, [m[0] for m in middle_d])
    grad_inputs = dot_nt(grad_rows, select).astype(BF16)
    small_grads = grid.reduce_small(small_grads, 2)
    small_grads = grid.reduce_small(small_grads, 1)
    middle_d, small_grads, first_c, grad_inputs, mlp_out = join(
        middle_d, small_grads, first_c, grad_inputs, mlp_out
    )

    if parts == 2:
        count, lanes = small_grads.shape[1], middle_d[0][0].shape[2]
        spare = ((0, 2), (0, 0), (0, lanes - block))
        pieces_d = [
            jnp.concatenate([p, jnp.pad(g.astype(p.dtype)[None], spare)], axis=1)
            for p, g in zip(grid.first_pieces(middle_d), small_grads)
        ]
        sum_d = grid.reduce_end(pieces_d[:1] + grid.send_first(pieces_d, (1, 2, 3)))
        sum_d, small_grads = sum_d[:, :block], sum_d[0, block:, :block]
    else:
        small_grads = grid.reduce_small(small_grads, 0)
    mlp_out = sum(m.astype(F32) for m in mlp_out)
    result = pair.own(middle) + own_live * (mlp_out + fc2_shift)
    outputs = dot_nt(result.astype(BF16), select).astype(BF16)
    first_a, first_b = grid.reduce_end(first_a), grid.reduce_end(first_b)
    out_fc1 = jnp.concatenate([first_a[0], first_a[1], first_b[0], first_b[1]], axis=1)
    out_fc2 = jnp.concatenate([first_a[2], first_a[3], first_b[2], first_b[3]], axis=1)
    out_c = grid.reduce_end(first_c)
    out_qkv = out_c[:3]
    if parts == 2:
        out_qkv = jnp.concatenate([out_qkv, sum_d], axis=2)
    out_proj = jnp.concatenate([out_c[3 + p] for p in range(parts)], axis=1)
    return (
        outputs,
        grad_inputs,
        small_grads[0],
        small_grads[1],
        out_qkv,
        out_proj.T,
        small_grads[4],
        small_grads[2],
        small_grads[3],
        out_fc1,
        small_grads[6:].reshape(-1)[:hidden_block],
        out_fc2.T,
        small_grads[5],
    )


def solution(mesh):
    in_specs = (
        P(("dp", "tensor"), None),
        P(("dp", "tensor"), None),
        P("dp"),
        P(("dp", "tensor")),
        P("dp"),
        P("dp"),
        P(None, "dp", "tensor"),
        P("tensor", "dp"),
        P("dp"),
        P("dp"),
        P("dp"),
        P("dp", "tensor"),
        P(("tensor", "dp")),
        P("tensor", "dp"),
        P("dp"),
    )
    out_specs = (
        P(("dp", "tensor"), None),
        P(("dp", "tensor"), None),
        P("dp"),
        P("dp"),
        P(None, "dp", "tensor"),
        P("tensor", "dp"),
        P("dp"),
        P("dp"),
        P("dp"),
        P("dp", "tensor"),
        P(("tensor", "dp")),
        P("tensor", "dp"),
        P("dp"),
    )
    return jax.shard_map(
        on_device, mesh=mesh, in_specs=in_specs, out_specs=out_specs, check_vma=False
    )
```
